128 devices in a mesh: req: 16 (over z, x_hi, core), mdl: 8 (over x_lo, y).
Axes of the slice: x: 4 (x_hi: 2, x_lo: 2; x = x_hi * 2 + x_lo), y: 4, z: 4, core: 2. Of those that a mesh axis runs over, the one named last changes fastest.
Arguments:
- tokens: bfloat16 [16384, 2048], P('req'), may hold values from -6 to 6
- doc_ids: int32 [16384], P('req'), may hold values from 0 to 16383, as said below
- positions: int32 [16384], P('req'), may hold values from 0 to 1023, as said below
- attn_gain: float32 [2048], replicated, may hold values from 0.5 to 1.5
- mlp_gain: float32 [2048], replicated, may hold values from 0.5 to 1.5
- q_gain: float32 [128], replicated, may hold values from 0.5 to 48
- key_norm_gain: float32 [128], replicated, may hold values from 0.5 to 1.5
- q_weight: float32 [2048, 2048], P('req', 'mdl'), may hold values from -0.125 to 0.125
- key_matrix: float32 [2048, 1024], P('req', 'mdl'), may hold values from -0.125 to 0.125
- value_matrix: float32 [2048, 1024], P('req', 'mdl'), may hold values from -0.125 to 0.125
- o_weight: float32 [2048, 2048], P('mdl', 'req'), may hold values from -0.125 to 0.125
- gate_weight: float32 [2048, 6144], P('mdl', 'req'), may hold values from -0.125 to 0.125
- up_weight: float32 [2048, 6144], P('mdl', 'req'), may hold values from -0.125 to 0.125
- down_weight: float32 [6144, 2048], P('req', 'mdl'), may hold values from -0.078125 to 0.078125
Outputs:
- layer_out: bfloat16 [16384, 2048], P(('req', 'mdl'))
- key_value_cache: bfloat16 [2, 16384, 1024], P(None, 'req', 'mdl')
The draws below stay inside these ranges and needn't reach their ends.
Inputs may be any that keep to these rules, and one draw needn't show every extreme that they name: `doc_ids`: A row's prompt number is the index of its prompt's first row among all packed rows, so it never falls along the rows; a prompt holds at most 1024 rows, every aligned block of 1024 rows has a prompt start in its second half, every block but the first begins inside the prompt that the block before it ends with, and the last row starts a prompt. `positions`: positions count from 0 at each prompt's first row.
All inputs are finite; a program needn't handle non-finite values.
Results may differ from the reference program's by a relative error of at most 0.02.
The reference program's roundings to bfloat16 on the way count: a program that leaves them out, or rounds other values in their place, can miss the bound.
Values may be sent and summed in bfloat16 or wider, within the bound.
No kernel may reach another device: no remote copies, remote signals or barrier semaphores. Data moves between devices by JAX's collectives and lax.ppermute only.
A program may use at most 128 MiB of HBM per device.

```python
import math
import jax
import jax.numpy as jnp
from jax import lax

MODEL_WIDTH = 2048
QUERY_HEADS = 16
KEY_VALUE_HEADS = 8
HEAD_SIZE = 128
FF = 6144
REQUEST_ROWS = 1024
PACKED_ROWS = 16384
N_REQ = 16
N_MDL = 8


def prompt_layout(key):
    rows = REQUEST_ROWS
    blocks = PACKED_ROWS // REQUEST_ROWS
    half = rows // 2
    sub_keys = jax.random.split(jax.random.fold_in(key, 11), 5)
    shrink = jax.random.randint(sub_keys[0], (blocks, 1), 2, 10)
    tosses = jax.random.randint(sub_keys[1], (blocks, rows), 0, 65536)
    extra = tosses < jnp.right_shift(jnp.int32(65536), shrink)
    first = jax.random.randint(sub_keys[2], (blocks, 1), 1, half + 1)
    second = jax.random.randint(sub_keys[3], (blocks, 1), half, rows)
    chosen = jax.random.randint(sub_keys[4], (), 0, blocks - 1)
    block_ids = jnp.arange(blocks, dtype=jnp.int32)[:, None]
    column = jnp.arange(rows, dtype=jnp.int32)[None, :]
    first = jnp.where(block_ids == chosen + 1, half, first)
    second = jnp.where(block_ids == chosen, half, second)
    extra = extra & ~((block_ids == chosen) & (column > half)) & ~((block_ids == chosen + 1) & (column < half))
    starts = extra | (column == first) | (column == second) | (block_ids == blocks - 1) & (column == rows - 1)
    starts = starts & (column > 0) | (block_ids == 0) & (column == 0)
    flat = starts.reshape(-1).astype(jnp.int32)
    index = jnp.arange(flat.shape[0], dtype=jnp.int32)
    begun = lax.cummax(jnp.where(flat == 1, index, 0), axis=0)
    return (begun.astype(jnp.int32), (index - begun).astype(jnp.int32))


def draw_doc_ids(key, part):
    return prompt_layout(key)[0]


def draw_positions(key, part):
    return prompt_layout(key)[1]


def draw_q_gain(key, part):
    return jax.random.uniform(key, (HEAD_SIZE,), jnp.float32, 0.5, 1.5)


def levels(own_key, shape, shards, least, top_value):
    def one(axis_at, blocks):
        draws = jax.random.uniform(jax.random.fold_in(jax.random.fold_in(own_key, 6), axis_at), (blocks,), jnp.float32, least / len(shards), top_value / len(shards))
        return jnp.repeat(jnp.exp(draws), shape[axis_at] // blocks).reshape((-1,) + (1,) * (len(shape) - axis_at - 1))

    loudness = one(*shards[0])
    for cut in shards[1:]:
        loudness = loudness * one(*cut)
    return loudness


def centred(key, extent, width, most, cuts=(), held_as=jnp.bfloat16):
    level = levels(key, extent, cuts, -0.22, 0.18) if cuts else 1.0
    values = jax.random.normal(key, extent, jnp.float32) * width * level
    return jnp.minimum(jnp.maximum(values, -most), most).astype(held_as)


def setup_inputs(seed: int = 0) -> dict:
    key_of = jax.random.split(jax.random.key(seed), 15)
    return {
        "tokens": centred(key_of[0], (PACKED_ROWS, MODEL_WIDTH), 1.0, 6.0, ((0, 16),)),
        "doc_ids": draw_doc_ids(jax.random.fold_in(key_of[14], 71), 0),
        "positions": draw_positions(jax.random.fold_in(key_of[14], 71), 0),
        "attn_gain": jnp.clip(1.0 + 0.1 * jax.random.normal(key_of[3], (MODEL_WIDTH,), jnp.float32), 0.5, 1.5),
        "mlp_gain": jnp.clip(1.0 + 0.1 * jax.random.normal(key_of[4], (MODEL_WIDTH,), jnp.float32), 0.5, 1.5),
        "q_gain": draw_q_gain(jax.random.fold_in(key_of[14], 71), 0),
        "key_norm_gain": jnp.clip(1.0 + 0.1 * jax.random.normal(key_of[6], (HEAD_SIZE,), jnp.float32), 0.5, 1.5),
        "q_weight": centred(key_of[7], (MODEL_WIDTH, QUERY_HEADS * HEAD_SIZE), MODEL_WIDTH ** -0.5, 0.125, ((0, 16), (1, 8)), jnp.float32),
        "key_matrix": centred(key_of[8], (MODEL_WIDTH, KEY_VALUE_HEADS * HEAD_SIZE), MODEL_WIDTH ** -0.5, 0.125, ((0, 16), (1, 8)), jnp.float32),
        "value_matrix": centred(key_of[9], (MODEL_WIDTH, KEY_VALUE_HEADS * HEAD_SIZE), MODEL_WIDTH ** -0.5, 0.125, ((0, 16), (1, 8)), jnp.float32),
        "o_weight": centred(key_of[10], (QUERY_HEADS * HEAD_SIZE, MODEL_WIDTH), (QUERY_HEADS * HEAD_SIZE) ** -0.5, 0.125, ((0, 8), (1, 16)), jnp.float32),
        "gate_weight": centred(key_of[11], (MODEL_WIDTH, FF), MODEL_WIDTH ** -0.5, 0.125, ((0, 8), (1, 16)), jnp.float32),
        "up_weight": centred(key_of[12], (MODEL_WIDTH, FF), MODEL_WIDTH ** -0.5, 0.125, ((0, 8), (1, 16)), jnp.float32),
        "down_weight": centred(key_of[13], (FF, MODEL_WIDTH), FF ** -0.5, 0.078125, ((0, 16), (1, 8)), jnp.float32),
    }


def finish_handover(values):
    return lax.optimization_barrier(values.astype(jnp.bfloat16))

def root_mean_scale(values, gain):
    return values * lax.rsqrt(lax.optimization_barrier(jnp.mean(values * values, axis=-1, keepdims=True)) + 1e-06) * gain

def apply_rotary(tensor, position):
    half = tensor.shape[-1] // 2
    freq = jnp.exp(jnp.arange(half, dtype=jnp.float32) * (-2.0 * math.log(1000000.0) / tensor.shape[-1]))
    angle = position.astype(jnp.float32)[:, None] * freq[None, :]
    cosine = jnp.cos(angle)[:, None, :]
    sine = jnp.sin(angle)[:, None, :]
    front = tensor[..., :half]
    back = tensor[..., half:]
    return jnp.concatenate([front * cosine - back * sine, back * cosine + front * sine], axis=-1)

def reference(tokens, doc_ids, positions, attn_gain, mlp_gain, q_gain, key_norm_gain, q_weight, key_matrix, value_matrix, o_weight, gate_weight, up_weight, down_weight):
    q_b = q_weight.astype(jnp.bfloat16)
    k_b = key_matrix.astype(jnp.bfloat16)
    v_b = value_matrix.astype(jnp.bfloat16)
    o_b = o_weight.astype(jnp.bfloat16)
    gate_b = gate_weight.astype(jnp.bfloat16)
    up_b = up_weight.astype(jnp.bfloat16)
    down_b = down_weight.astype(jnp.bfloat16)
    normed = root_mean_scale(tokens.astype(jnp.float32), attn_gain).astype(jnp.bfloat16)
    query_raw = jnp.dot(normed, q_b, preferred_element_type=jnp.float32)
    unnormed_keys = jnp.dot(normed, k_b, preferred_element_type=jnp.float32)
    unnormed_values = jnp.dot(normed, v_b, preferred_element_type=jnp.float32)
    head_groups = QUERY_HEADS // KEY_VALUE_HEADS
    query_rows = finish_handover(apply_rotary(root_mean_scale(query_raw.reshape(PACKED_ROWS, QUERY_HEADS, HEAD_SIZE), q_gain), positions))
    rotated_keys = finish_handover(apply_rotary(root_mean_scale(unnormed_keys.reshape(PACKED_ROWS, KEY_VALUE_HEADS, HEAD_SIZE), key_norm_gain), positions))
    projected_values = finish_handover(unnormed_values).reshape(PACKED_ROWS, KEY_VALUE_HEADS, HEAD_SIZE)
    key_value_cache = jnp.stack([rotated_keys.reshape(PACKED_ROWS, KEY_VALUE_HEADS * HEAD_SIZE), projected_values.reshape(PACKED_ROWS, KEY_VALUE_HEADS * HEAD_SIZE)])
    grouped_queries = query_rows.reshape(PACKED_ROWS, KEY_VALUE_HEADS, head_groups, HEAD_SIZE)
    padded_keys = jnp.concatenate([jnp.zeros((REQUEST_ROWS, KEY_VALUE_HEADS, HEAD_SIZE), jnp.bfloat16), rotated_keys], axis=0)
    padded_values = jnp.concatenate([jnp.zeros((REQUEST_ROWS, KEY_VALUE_HEADS, HEAD_SIZE), jnp.bfloat16), projected_values], axis=0)
    doc_padded = jnp.concatenate([jnp.full((REQUEST_ROWS,), -1, jnp.int32), doc_ids.astype(jnp.int32)])
    pos_padded = jnp.concatenate([jnp.zeros((REQUEST_ROWS,), jnp.int32), positions.astype(jnp.int32)])
    scale = HEAD_SIZE ** (-0.5)

    def attend(block_index):
        lower = (block_index * REQUEST_ROWS).astype(jnp.int32)
        block_q = lax.dynamic_slice_in_dim(grouped_queries, lower, REQUEST_ROWS, 0).astype(jnp.float32)
        block_doc = lax.dynamic_slice_in_dim(doc_ids.astype(jnp.int32), lower, REQUEST_ROWS, 0)
        block_pos = lax.dynamic_slice_in_dim(positions.astype(jnp.int32), lower, REQUEST_ROWS, 0)
        near_keys = lax.dynamic_slice_in_dim(padded_keys, lower, 2 * REQUEST_ROWS, 0).astype(jnp.float32)
        near_values = lax.dynamic_slice_in_dim(padded_values, lower, 2 * REQUEST_ROWS, 0).astype(jnp.float32)
        near_doc = lax.dynamic_slice_in_dim(doc_padded, lower, 2 * REQUEST_ROWS, 0)
        near_pos = lax.dynamic_slice_in_dim(pos_padded, lower, 2 * REQUEST_ROWS, 0)
        scores = jnp.einsum('qkrd,skd->krqs', block_q, near_keys) * scale
        allowed = (near_doc[None, :] == block_doc[:, None]) & (near_pos[None, :] <= block_pos[:, None])
        scores = jnp.where(allowed[None, None], scores, -jnp.inf)
        top = lax.optimization_barrier(jnp.max(scores, axis=-1, keepdims=True))
        expo = jnp.exp(scores - top)
        probs = finish_handover(expo / lax.optimization_barrier(jnp.sum(expo, axis=-1, keepdims=True))).astype(jnp.float32)
        context = jnp.einsum('krqs,skd->qkrd', probs, near_values)
        return context.astype(jnp.bfloat16).reshape(REQUEST_ROWS, QUERY_HEADS * HEAD_SIZE)
    context = lax.map(attend, jnp.arange(N_REQ, dtype=jnp.int32)).reshape(PACKED_ROWS, QUERY_HEADS * HEAD_SIZE)
    head_cols = QUERY_HEADS * HEAD_SIZE // N_MDL
    attn_out = jnp.zeros((PACKED_ROWS, MODEL_WIDTH), jnp.float32)
    for group in range(N_MDL):
        term = jnp.dot(context[:, group * head_cols:(group + 1) * head_cols], o_b[group * head_cols:(group + 1) * head_cols], preferred_element_type=jnp.float32)
        attn_out = attn_out + finish_handover(term).astype(jnp.float32)
    resid = finish_handover(tokens.astype(jnp.float32) + attn_out).astype(jnp.float32)
    mlp_in = root_mean_scale(resid, mlp_gain).astype(jnp.bfloat16)
    unit_cols = FF // N_MDL
    mlp_out = jnp.zeros((PACKED_ROWS, MODEL_WIDTH), jnp.float32)
    for group in range(N_MDL):
        lower = group * unit_cols
        gate = jnp.dot(mlp_in, gate_b[:, lower:lower + unit_cols], preferred_element_type=jnp.float32)
        upper = jnp.dot(mlp_in, up_b[:, lower:lower + unit_cols], preferred_element_type=jnp.float32)
        hidden = (jax.nn.silu(gate) * upper).astype(jnp.bfloat16)
        term = jnp.dot(hidden, down_b[lower:lower + unit_cols], preferred_element_type=jnp.float32)
        mlp_out = mlp_out + finish_handover(term).astype(jnp.float32)
    layer_out = (resid + mlp_out).astype(jnp.bfloat16)
    return (layer_out, key_value_cache)
```

```python
import math

import jax
import jax.numpy as jnp
from jax import lax
from jax.experimental import pallas as pl
from jax.experimental.pallas import tpu as pltpu
from jax.sharding import Mesh
from jax.sharding import PartitionSpec as P

HEAD = 128
BF = jnp.bfloat16
F32 = jnp.float32
REQ = ("z", "xh", "core")
MDL = ("xl", "y")


def ring(step):
    return [(i, (i + step) % 4) for i in range(4)]


def spread(block, axes):
    count = lax.axis_size(axes)
    wide = jnp.broadcast_to(block[None], (count,) + block.shape)
    return lax.all_to_all(wide, axes, split_axis=0, concat_axis=0, tiled=True)


def swap(block, axis):
    return lax.ppermute(block, axis, [(0, 1), (1, 0)])


def qkv_kernel(core_ref, x_ref, own_ref, oth_ref, gain_ref, qg_ref, kg_ref, cs_ref, q_ref, kv_ref, w_ref):
    core = core_ref[0]

    @pl.when(pl.program_id(0) == 0)
    def _():
        for i in range(8):
            w_ref[pl.ds(pl.multiple_of((2 * i + core) * 128, 128), 128), :] = own_ref[i]
            w_ref[pl.ds(pl.multiple_of((2 * i + 1 - core) * 128, 128), 128), :] = oth_ref[i]

    x = x_ref[...].astype(F32)
    scale = lax.rsqrt(jnp.mean(x * x, axis=-1, keepdims=True) + 1e-06)
    normed = (x * scale * gain_ref[...]).astype(BF)
    raw = jnp.dot(normed, w_ref[...], preferred_element_type=F32)
    cs = cs_ref[...]
    turned = pltpu.roll(cs, 64, 1)
    low = lax.broadcasted_iota(jnp.int32, cs.shape, 1) < 64
    cosine = jnp.where(low, cs, turned)
    sine = jnp.where(low, -turned, cs)

    def head(t, gain):
        t = t * lax.rsqrt(jnp.mean(t * t, axis=-1, keepdims=True) + 1e-06) * gain
        return (t * cosine + pltpu.roll(t, 64, 1) * sine).astype(BF)

    q_ref[:, :128] = head(raw[:, :128], qg_ref[...])
    q_ref[:, 128:] = head(raw[:, 128:256], qg_ref[...])
    kv_ref[0] = head(raw[:, 256:384], kg_ref[...])
    kv_ref[1] = raw[:, 384:].astype(BF)


def project(core, tokens, own, oth, attn_gain, q_gain, key_gain, cs):
    rows = tokens.shape[0]
    tile = 256
    fixed = lambda *shape: pl.BlockSpec(shape, lambda i, c: (0,) * len(shape))
    return pl.pallas_call(
        qkv_kernel,
        grid_spec=pltpu.PrefetchScalarGridSpec(
            num_scalar_prefetch=1,
            grid=(rows // tile,),
            in_specs=[
                pl.BlockSpec((tile, 2048), lambda i, c: (i, 0)),
                fixed(8, 128, 512),
                fixed(8, 128, 512),
                fixed(1, 2048),
                fixed(1, 128),
                fixed(1, 128),
                pl.BlockSpec((tile, 128), lambda i, c: (i, 0)),
            ],
            out_specs=[
                pl.BlockSpec((tile, 256), lambda i, c: (i, 0)),
                pl.BlockSpec((2, tile, 128), lambda i, c: (0, i, 0)),
            ],
            scratch_shapes=[pltpu.VMEM((2048, 512), BF)],
        ),
        out_shape=(
            jax.ShapeDtypeStruct((rows, 256), BF),
            jax.ShapeDtypeStruct((2, rows, 128), BF),
        ),
        compiler_params=pltpu.CompilerParams(vmem_limit_bytes=40 << 20),
        name="qkv",
    )(core, tokens, own, oth, attn_gain[None], q_gain[None], key_gain[None], cs)


def attend_kernel(q_ref, kv_ref, prior_ref, lo_ref, out_ref):
    factor = HEAD ** (-0.5) * math.log2(math.e)
    nt = (((1,), (1,)), ((), ()))
    for i in range(4):
        first = i * 256
        skip = 256 if i == 3 else 0
        count = first + 256
        lo = lo_ref[first : first + 256, :]
        row = lax.broadcasted_iota(jnp.int32, (256, count), 0) + first
        col = lax.broadcasted_iota(jnp.int32, (256, count), 1)
        near = (col >= lo) & (col <= row)
        prior_col = lax.broadcasted_iota(jnp.int32, (256, 512 - skip), 1) + (skip - 512)
        far = prior_col >= lo
        for h in range(2):
            q = q_ref[first : first + 256, h * 128 : h * 128 + 128]
            s1 = lax.dot_general(q, kv_ref[0, :count], nt, preferred_element_type=F32)
            s0 = lax.dot_general(q, prior_ref[0, skip:], nt, preferred_element_type=F32)
            s1 = jnp.where(near, s1, -1e30)
            s0 = jnp.where(far, s0, -1e30)
            top = jnp.maximum(jnp.max(s1, -1, keepdims=True), jnp.max(s0, -1, keepdims=True))
            e1 = jnp.exp2((s1 - top) * factor)
            e0 = jnp.exp2((s0 - top) * factor)
            inv = 1.0 / (jnp.sum(e1, -1, keepdims=True) + jnp.sum(e0, -1, keepdims=True))
            p1 = (e1 * inv).astype(BF)
            p0 = (e0 * inv).astype(BF)
            o = jnp.dot(p1, kv_ref[1, :count], preferred_element_type=F32)
            o = o + jnp.dot(p0, prior_ref[1, skip:], preferred_element_type=F32)
            o = o.astype(BF)
            for part in range(2):
                block = 2 * i + part
                out_ref[block % 4, block // 4, :, h * 128 : h * 128 + 128] = o[part * 128 : part * 128 + 128]


def attend(q, kv, prior, lo):
    return pl.pallas_call(
        attend_kernel,
        out_shape=jax.ShapeDtypeStruct((4, 2, 128, 256), BF),
        compiler_params=pltpu.CompilerParams(vmem_limit_bytes=40 << 20),
        name="attend",
    )(q, kv, prior, lo)


def out_kernel(at_ref, ctx_ref, own_ref, oth_ref, keep_ref, send_ref):
    core = at_ref[0]
    xl = at_ref[1]

    def body(even, odd):
        left = [jnp.concatenate([ctx_ref[s, xl], ctx_ref[s, 1 - xl]], axis=0) for s in range(4)]
        for i in range(8):
            total = None
            for s in range(4):
                w = jnp.concatenate([even[s, i], odd[s, i]], axis=1)
                term = jnp.dot(left[s], w, preferred_element_type=F32)
                total = term if total is None else total + term
            keep_ref[:, i * 256 : i * 256 + 256] = total[:128]
            send_ref[:, i * 256 : i * 256 + 256] = total[128:].astype(BF)

    @pl.when(core == 0)
    def _():
        body(own_ref, oth_ref)

    @pl.when(core == 1)
    def _():
        body(oth_ref, own_ref)


def out_project(at, ctx, own, oth):
    vm = pl.BlockSpec(memory_space=pltpu.VMEM)
    return pl.pallas_call(
        out_kernel,
        in_specs=[pl.BlockSpec(memory_space=pltpu.SMEM), vm, vm, vm],
        out_shape=(
            jax.ShapeDtypeStruct((128, 2048), F32),
            jax.ShapeDtypeStruct((128, 2048), BF),
        ),
        compiler_params=pltpu.CompilerParams(vmem_limit_bytes=40 << 20),
        name="oproj",
    )(at, ctx, own, oth)


def mlp_kernel(x0_ref, x1_ref, x2_ref, x3_ref, x4_ref, own_ref, oth_ref, keep_ref, left_ref, right_ref, far_ref,
               w_ref, x_ref, hid_ref, sems):
    nt = (((1,), (1,)), ((), ()))
    copies = {}
    for g, c in ((0, 0), (1, 0), (0, 1), (1, 1), (2, 0), (2, 1)):
        src = own_ref if c == 0 else oth_ref
        for m in range(8):
            copies[g, c, m] = pltpu.make_async_copy(
                src.at[:, m // 4, m % 4, g * 96 : g * 96 + 96, :],
                w_ref.at[g, c, :, :, m * 256 : m * 256 + 256],
                sems.at[g, c, m],
            )
            copies[g, c, m].start()
    x_ref[0:128] = x0_ref[...]
    x_ref[128:256] = x1_ref[...]
    x_ref[256:384] = x2_ref[...]
    x_ref[384:448] = x3_ref[...]
    x_ref[448:512] = x4_ref[...]
    x = x_ref[...]
    for c in range(2):
        for g in range(2):
            for m in range(8):
                copies[g, c, m].wait()
        gate_w = w_ref[0, c].reshape(768, 2048)
        up_w = w_ref[1, c].reshape(768, 2048)
        for t in range(3):
            gate = lax.dot_general(x, gate_w[t * 256 : t * 256 + 256], nt, preferred_element_type=F32)
            upper = lax.dot_general(x, up_w[t * 256 : t * 256 + 256], nt, preferred_element_type=F32)
            hidden = gate / (1.0 + jnp.exp(-gate)) * upper
            at = c * 768 + t * 256
            hid_ref[:, at : at + 256] = hidden.astype(BF)
    for c in range(2):
        for m in range(8):
            copies[2, c, m].wait()
    hid = hid_ref[...]
    down = w_ref[2].reshape(1536, 2048)
    for n in range(8):
        at = slice(n * 256, n * 256 + 256)
        out = jnp.dot(hid, down[:, at], preferred_element_type=F32)
        keep_ref[:, at] = out[:128]
        left_ref[:, at] = out[128:256].astype(BF)
        right_ref[:, at] = out[256:384].astype(BF)
        far_ref[:, at] = out[384:].astype(BF)


def feed_forward(pieces, own, oth):
    vm = pl.BlockSpec(memory_space=pltpu.VMEM)
    hbm = pl.BlockSpec(memory_space=pl.ANY)
    part = jax.ShapeDtypeStruct((128, 2048), BF)
    return pl.pallas_call(
        mlp_kernel,
        in_specs=[vm] * 5 + [hbm] * 2,
        out_shape=(jax.ShapeDtypeStruct((128, 2048), F32), part, part, part),
        scratch_shapes=[
            pltpu.VMEM((3, 2, 8, 96, 2048), BF),
            pltpu.VMEM((512, 2048), BF),
            pltpu.VMEM((512, 1536), BF),
            pltpu.SemaphoreType.DMA((3, 2, 8)),
        ],
        compiler_params=pltpu.CompilerParams(vmem_limit_bytes=56 << 20),
        name="mlp",
    )(*pieces, own, oth)


def per_device(
    tokens,
    doc_ids,
    positions,
    attn_gain,
    mlp_gain,
    q_gain,
    key_norm_gain,
    q_weight,
    key_matrix,
    value_matrix,
    o_weight,
    gate_weight,
    up_weight,
    down_weight,
):
    rows = tokens.shape[0]
    core = lax.axis_index("core").astype(jnp.int32)
    xl = lax.axis_index("xl").astype(jnp.int32)
    m = lax.axis_index(MDL).astype(jnp.int32)

    qkv_local = jnp.concatenate([q_weight, key_matrix, value_matrix], axis=1).astype(BF)
    qkv_own = spread(qkv_local, ("z", "xh"))
    qkv_oth = swap(qkv_own, "core")

    o_cols = spread(o_weight.astype(BF), ("z", "xh"))
    o_own = spread(o_cols, "y")
    o_oth = swap(o_own, "core")

    mlp_local = jnp.stack([gate_weight.T, up_weight.T, down_weight]).astype(BF)
    mlp_local = mlp_local.reshape(3, 4, 96, 256).transpose(1, 0, 2, 3).reshape(4, 288, 256)
    mlp_group = lax.all_to_all(mlp_local, "y", split_axis=0, concat_axis=0, tiled=True)
    mlp_own = lax.all_gather(mlp_group, ("z", "xh", "xl"), axis=0, tiled=False)
    mlp_own = mlp_own.reshape(8, 2, 4, 288, 256)
    mlp_oth = swap(mlp_own, "core")

    half = HEAD // 2
    freq = jnp.exp(jnp.arange(half, dtype=F32) * (-2.0 * math.log(1000000.0) / HEAD))
    angle = positions.astype(F32)[:, None] * freq[None, :]
    cs = jnp.concatenate([jnp.cos(angle), jnp.sin(angle)], axis=1)
    lo = (jnp.arange(rows, dtype=jnp.int32) - positions)[:, None]

    q, cache = project(core[None], tokens, qkv_own, qkv_oth, attn_gain, q_gain, key_norm_gain, cs)
    prior = lax.ppermute(cache[:, rows // 2 :], REQ, [(i - 1, i) for i in range(1, 16)])
    ctx = attend(q, cache, prior, lo)
    ctx = lax.all_to_all(ctx, "y", split_axis=0, concat_axis=0, tiled=True)
    keep, send = out_project(jnp.stack([core, xl]), ctx, o_own, o_oth)
    got = swap(send, "xl")

    own_rows = lax.dynamic_slice_in_dim(tokens, m * 128, 128, 0).astype(F32)
    resid = (own_rows + (keep + got.astype(F32))).astype(BF)
    resid = lax.optimization_barrier(resid).astype(F32)
    scale = lax.rsqrt(jnp.mean(resid * resid, axis=-1, keepdims=True) + 1e-06)
    mlp_in = (resid * scale * mlp_gain).astype(BF)

    left = lax.ppermute(mlp_in, "y", ring(1))
    right = lax.ppermute(mlp_in, "y", ring(3))
    far_top = lax.ppermute(left[:64], "y", ring(1))
    far_bottom = lax.ppermute(right[64:], "y", ring(3))
    keep, to_left, to_right, to_far = feed_forward((mlp_in, left, right, far_top, far_bottom), mlp_own, mlp_oth)
    via_left = lax.ppermute(to_far[:64], "y", ring(1))
    via_right = lax.ppermute(to_far[64:], "y", ring(3))
    to_right = jnp.concatenate([(to_right[:64].astype(F32) + via_left.astype(F32)).astype(BF), to_right[64:]])
    to_left = jnp.concatenate([to_left[:64], (to_left[64:].astype(F32) + via_right.astype(F32)).astype(BF)])
    from_left = lax.ppermute(to_right, "y", ring(1))
    from_right = lax.ppermute(to_left, "y", ring(3))
    total = keep + from_left.astype(F32) + from_right.astype(F32)
    return ((resid + total).astype(BF), cache)


def solution(mesh):
    fine = Mesh(mesh.devices.reshape(4, 2, 2, 2, 4), REQ + MDL)
    rows = P(REQ)
    in_specs = (
        P(REQ, None),
        rows,
        rows,
        P(),
        P(),
        P(),
        P(),
        P(REQ, MDL),
        P(REQ, MDL),
        P(REQ, MDL),
        P(MDL, REQ),
        P(MDL, REQ),
        P(MDL, REQ),
        P(REQ, MDL),
    )
    out_specs = (P(REQ + MDL, None), P(None, REQ, MDL))
    return jax.shard_map(per_device, mesh=fine, in_specs=in_specs, out_specs=out_specs, check_vma=False)
```

```python
import math

import jax
import jax.numpy as jnp
from jax import lax
from jax.experimental import pallas as pl
from jax.experimental.pallas import tpu as pltpu
from jax.sharding import Mesh
from jax.sharding import PartitionSpec as P

HEAD = 128
BF = jnp.bfloat16
F32 = jnp.float32
REQ = ("z", "xh", "core")
MDL = ("xl", "y")


def ring(step):
    return [(i, (i + step) % 4) for i in range(4)]


def swap(block, axis):
    return lax.ppermute(block, axis, [(0, 1), (1, 0)])


def shard(at_ref, e, side):
    z, xh, core = at_ref[0], at_ref[1], at_ref[2]
    return lax.rem(z + lax.div(jnp.int32(e), 2), 4) * 4 + lax.rem(xh + lax.rem(jnp.int32(e), 2), 2) * 2 + (core if side == 0 else 1 - core)


PLACES = ((0, 0, 2), (1, 2, 2), (2, 4, 1), (3, 5, 1), (4, 6, 2))


def qkv_kernel(at_ref, x_ref, *refs):
    pieces, (gain_ref, qg_ref, kg_ref, cs_ref, q_ref, kv_ref, w_ref) = refs[:10], refs[10:]

    @pl.when(pl.program_id(0) == 0)
    def _():
        for n, first, count in PLACES:
            for side in range(2):
                for i in range(count):
                    at = pl.multiple_of(shard(at_ref, first + i, side) * 128, 128)
                    w_ref[pl.ds(at, 128), :] = pieces[2 * n + side][i, :128]

    x = x_ref[...].astype(F32)
    scale = lax.rsqrt(jnp.mean(x * x, axis=-1, keepdims=True) + 1e-06)
    normed = (x * scale * gain_ref[...]).astype(BF)
    raw = jnp.dot(normed, w_ref[...], preferred_element_type=F32)
    cs = cs_ref[...]
    turned = pltpu.roll(cs, 64, 1)
    low = lax.broadcasted_iota(jnp.int32, cs.shape, 1) < 64
    cosine = jnp.where(low, cs, turned)
    sine = jnp.where(low, -turned, cs)

    def head(t, gain):
        t = t * lax.rsqrt(jnp.mean(t * t, axis=-1, keepdims=True) + 1e-06) * gain
        return (t * cosine + pltpu.roll(t, 64, 1) * sine).astype(BF)

    q_ref[:, :128] = head(raw[:, :128], qg_ref[...])
    q_ref[:, 128:] = head(raw[:, 128:256], qg_ref[...])
    kv_ref[0] = head(raw[:, 256:384], kg_ref[...])
    kv_ref[1] = raw[:, 384:].astype(BF)


def project(at, tokens, pieces, attn_gain, q_gain, key_gain, cs):
    rows = tokens.shape[0]
    tile = 256
    fixed = lambda *shape: pl.BlockSpec(shape, lambda i, c: (0,) * len(shape))
    return pl.pallas_call(
        qkv_kernel,
        grid_spec=pltpu.PrefetchScalarGridSpec(
            num_scalar_prefetch=1,
            grid=(rows // tile,),
            in_specs=[
                pl.BlockSpec((tile, 2048), lambda i, c: (i, 0)),
                *(fixed(count, 192, 512) for _, _, count in PLACES for _ in range(2)),
                fixed(1, 2048),
                fixed(1, 128),
                fixed(1, 128),
                pl.BlockSpec((tile, 128), lambda i, c: (i, 0)),
            ],
            out_specs=[
                pl.BlockSpec((tile, 256), lambda i, c: (i, 0)),
                pl.BlockSpec((2, tile, 128), lambda i, c: (0, i, 0)),
            ],
            scratch_shapes=[pltpu.VMEM((2048, 512), BF)],
        ),
        out_shape=(
            jax.ShapeDtypeStruct((rows, 256), BF),
            jax.ShapeDtypeStruct((2, rows, 128), BF),
        ),
        compiler_params=pltpu.CompilerParams(vmem_limit_bytes=40 << 20),
        name="qkv",
    )(at, tokens, *pieces, attn_gain[None], q_gain[None], key_gain[None], cs)


def attend_kernel(y_ref, q_ref, kv_ref, prior_ref, lo_ref, *refs):
    out_ref = refs[4]
    factor = HEAD ** (-0.5) * math.log2(math.e)
    nt = (((1,), (1,)), ((), ()))
    for i in range(4):
        first = i * 256
        skip = 256 if i == 3 else 0
        count = first + 256
        lo = lo_ref[first : first + 256, :]
        row = lax.broadcasted_iota(jnp.int32, (256, count), 0) + first
        col = lax.broadcasted_iota(jnp.int32, (256, count), 1)
        near = (col >= lo) & (col <= row)
        prior_col = lax.broadcasted_iota(jnp.int32, (256, 512 - skip), 1) + (skip - 512)
        far = prior_col >= lo
        for h in range(2):
            q = q_ref[first : first + 256, h * 128 : h * 128 + 128]
            s1 = lax.dot_general(q, kv_ref[0, :count], nt, preferred_element_type=F32)
            s0 = lax.dot_general(q, prior_ref[0, skip:], nt, preferred_element_type=F32)
            s1 = jnp.where(near, s1, -1e30)
            s0 = jnp.where(far, s0, -1e30)
            top = jnp.maximum(jnp.max(s1, -1, keepdims=True), jnp.max(s0, -1, keepdims=True))
            e1 = jnp.exp2((s1 - top) * factor)
            e0 = jnp.exp2((s0 - top) * factor)
            inv = 1.0 / (jnp.sum(e1, -1, keepdims=True) + jnp.sum(e0, -1, keepdims=True))
            p1 = (e1 * inv).astype(BF)
            p0 = (e0 * inv).astype(BF)
            o = jnp.dot(p1, kv_ref[1, :count], preferred_element_type=F32)
            o = o + jnp.dot(p0, prior_ref[1, skip:], preferred_element_type=F32)
            o = o.astype(BF)
            for part in range(2):
                block = 2 * i + part
                out_ref[block % 4, block // 4, :, h * 128 : h * 128 + 128] = o[part * 128 : part * 128 + 128]
    for k in range(4):
        refs[k][...] = out_ref[lax.rem(y_ref[0] + k, 4)]


def attend(y, q, kv, prior, lo):
    vm = pl.BlockSpec(memory_space=pltpu.VMEM)
    return pl.pallas_call(
        attend_kernel,
        in_specs=[pl.BlockSpec(memory_space=pltpu.SMEM)] + [vm] * 4,
        out_shape=[jax.ShapeDtypeStruct((2, 128, 256), BF)] * 4,
        scratch_shapes=[pltpu.VMEM((4, 2, 128, 256), BF)],
        compiler_params=pltpu.CompilerParams(vmem_limit_bytes=40 << 20),
        name="attend",
    )(y, q, kv, prior, lo)


def out_kernel(at_ref, c0_ref, c1_ref, c2_ref, c3_ref, *refs):
    near, far, (keep_ref, send_ref, w_ref, x_ref, sems) = refs[:10], refs[10:18], refs[18:]
    xl = at_ref[3]

    def each(act):
        sources = [(0, first, count, 128, near[2 * n : 2 * n + 2]) for n, first, count in PLACES]
        for n, (s, first, count) in enumerate(((1, 0, 8), (2, 0, 4), (2, 4, 4), (3, 0, 8))):
            sources.append((s, first, count, 0, far[2 * n : 2 * n + 2]))
        for s, first, count, offset, pair in sources:
            for side in range(2):

                def step(i, carry, s=s, first=first, offset=offset, src=pair[side], side=side):
                    at = pl.ds(pl.multiple_of(shard(at_ref, first + i, side) * 128, 128), 128)
                    for k in range(4):
                        act(pltpu.make_async_copy(
                            src.at[i, offset : offset + 64, k * 128 : k * 128 + 128],
                            w_ref.at[s * 256 + k * 64 : s * 256 + k * 64 + 64, at],
                            sems.at[side, s, first + i, k],
                        ))
                    return carry

                lax.fori_loop(0, count, step, 0)

    each(lambda c: c.start())
    for s, c in enumerate((c0_ref, c1_ref, c2_ref, c3_ref)):
        x_ref[:128, s * 256 : s * 256 + 256] = c[xl]
        x_ref[128:, s * 256 : s * 256 + 256] = c[1 - xl]
    each(lambda c: c.wait())
    x = x_ref[...]

    def column(n, carry):
        at = pl.ds(pl.multiple_of(n * 512, 512), 512)
        total = jnp.dot(x, w_ref[:, at], preferred_element_type=F32)
        keep_ref[:, at] = total[:128]
        send_ref[:, at] = total[128:].astype(BF)
        return carry

    lax.fori_loop(0, 4, column, 0)


def out_project(at, ctx, near, far):
    vm = pl.BlockSpec(memory_space=pltpu.VMEM)
    anywhere = pl.BlockSpec(memory_space=pl.ANY)
    return pl.pallas_call(
        out_kernel,
        in_specs=[pl.BlockSpec(memory_space=pltpu.SMEM)] + [vm] * 4 + [anywhere] * 18,
        out_shape=(
            jax.ShapeDtypeStruct((128, 2048), F32),
            jax.ShapeDtypeStruct((128, 2048), BF),
        ),
        scratch_shapes=[
            pltpu.VMEM((1024, 2048), BF),
            pltpu.VMEM((256, 1024), BF),
            pltpu.SemaphoreType.DMA((2, 4, 8, 4)),
        ],
        compiler_params=pltpu.CompilerParams(vmem_limit_bytes=40 << 20),
        name="oproj",
    )(at, *ctx, *near, *far)


def fetcher(own_ref, oth_ref, w_ref, sems, y):
    def copy(c, g, m):
        src = own_ref if c == 0 else oth_ref
        at = pl.multiple_of(((m // 4) * 4 + lax.rem(y + lax.rem(m, 4), 4)) * 256, 256)
        return pltpu.make_async_copy(
            src.at[:, m // 4, lax.rem(m, 4), g * 96 : g * 96 + 96, :],
            w_ref.at[g, c * 8 : c * 8 + 8, :, pl.ds(at, 256)],
            sems.at[g, c, m],
        )

    def each(c, groups, act):
        def step(m, carry):
            for g in range(groups):
                act(copy(c, g, m))
            return carry

        lax.fori_loop(0, 8, step, 0)

    return each


def gate_kernel(y_ref, x0_ref, x1_ref, x2_ref, x3_ref, x4_ref, own_ref, oth_ref, hid_ref, w_ref, x_ref, sems):
    nt = (((1,), (1,)), ((), ()))
    each = fetcher(own_ref, oth_ref, w_ref, sems, y_ref[0])
    each(0, 2, lambda c: c.start())
    each(1, 2, lambda c: c.start())
    x_ref[0:128] = x0_ref[...]
    x_ref[128:256] = x1_ref[...]
    x_ref[256:384] = x2_ref[...]
    x_ref[384:448] = x3_ref[...]
    x_ref[448:512] = x4_ref[...]
    x = x_ref[...]

    for c in range(2):
        each(c, 2, lambda copy: copy.wait())
        gate_w = w_ref[0, c * 8 : c * 8 + 8].reshape(768, 2048)
        up_w = w_ref[1, c * 8 : c * 8 + 8].reshape(768, 2048)
        for t in range(3):
            gate = lax.dot_general(x, gate_w[t * 256 : t * 256 + 256], nt, preferred_element_type=F32)
            upper = lax.dot_general(x, up_w[t * 256 : t * 256 + 256], nt, preferred_element_type=F32)
            hidden = gate / (1.0 + jnp.exp(-gate)) * upper
            at = c * 768 + t * 256
            hid_ref[:, at : at + 256] = hidden.astype(BF)


def down_kernel(y_ref, hid_ref, own_ref, oth_ref, keep_ref, left_ref, right_ref, far_ref, w_ref, sems):
    each = fetcher(own_ref, oth_ref, w_ref, sems, y_ref[0])
    for c in range(2):
        each(c, 1, lambda copy: copy.start())
    for c in range(2):
        each(c, 1, lambda copy: copy.wait())
    hid = hid_ref[...]

    def column(n, carry):
        at = pl.ds(pl.multiple_of(n * 512, 512), 512)
        out = jnp.dot(hid, w_ref[0, :, :, at].reshape(1536, 512), preferred_element_type=F32)
        keep_ref[:, at] = out[:128]
        left_ref[:, at] = out[128:256].astype(BF)
        right_ref[:, at] = out[256:384].astype(BF)
        far_ref[:, at] = out[384:].astype(BF)
        return carry

    lax.fori_loop(0, 4, column, 0)


def gate_up(y, pieces, own, oth):
    vm = pl.BlockSpec(memory_space=pltpu.VMEM)
    hbm = pl.BlockSpec(memory_space=pltpu.HBM)
    return pl.pallas_call(
        gate_kernel,
        in_specs=[pl.BlockSpec(memory_space=pltpu.SMEM)] + [vm] * 5 + [hbm] * 2,
        out_shape=jax.ShapeDtypeStruct((512, 1536), BF),
        scratch_shapes=[
            pltpu.VMEM((2, 16, 96, 2048), BF),
            pltpu.VMEM((512, 2048), BF),
            pltpu.SemaphoreType.DMA((2, 2, 8)),
        ],
        compiler_params=pltpu.CompilerParams(vmem_limit_bytes=40 << 20),
        name="gate_up",
    )(y, *pieces, own, oth)


def down(y, hidden, own, oth):
    vm = pl.BlockSpec(memory_space=pltpu.VMEM)
    hbm = pl.BlockSpec(memory_space=pltpu.HBM)
    part = jax.ShapeDtypeStruct((128, 2048), BF)
    return pl.pallas_call(
        down_kernel,
        in_specs=[pl.BlockSpec(memory_space=pltpu.SMEM), vm] + [hbm] * 2,
        out_shape=(jax.ShapeDtypeStruct((128, 2048), F32), part, part, part),
        scratch_shapes=[
            pltpu.VMEM((1, 16, 96, 2048), BF),
            pltpu.SemaphoreType.DMA((1, 2, 8)),
        ],
        compiler_params=pltpu.CompilerParams(vmem_limit_bytes=40 << 20),
        name="down",
    )(y, hidden, own, oth)


def pack_kernel(q_ref, k_ref, v_ref, o_ref, out_ref):
    out_ref[:128, :256] = q_ref[...].astype(BF)
    out_ref[:128, 256:384] = k_ref[...].astype(BF)
    out_ref[:128, 384:] = v_ref[...].astype(BF)
    for k in range(4):
        out_ref[128:, k * 128 : k * 128 + 128] = o_ref[k * 64 : k * 64 + 64].astype(BF)


def pack(q, k, v, o):
    return pl.pallas_call(
        pack_kernel,
        out_shape=jax.ShapeDtypeStruct((192, 512), BF),
        name="pack",
    )(q, k, v, o)


def prep_kernel(y_ref, gate_ref, up_ref, down_ref, p0_ref, p1_ref, p2_ref, p3_ref, g_ref, u_ref):
    g_ref[...] = gate_ref[...].T
    u_ref[...] = up_ref[...].T
    for k, out_ref in enumerate((p0_ref, p1_ref, p2_ref, p3_ref)):
        at = pl.ds(pl.multiple_of(lax.rem(y_ref[0] + k, 4) * 96, 96), 96)
        out_ref[:96] = g_ref[at, :].astype(BF)
        out_ref[96:192] = u_ref[at, :].astype(BF)
        out_ref[192:] = down_ref[at, :].astype(BF)


def prepare(y, gate, up, down):
    vm = pl.BlockSpec(memory_space=pltpu.VMEM)
    return pl.pallas_call(
        prep_kernel,
        in_specs=[pl.BlockSpec(memory_space=pltpu.SMEM)] + [vm] * 3,
        out_shape=[jax.ShapeDtypeStruct((288, 256), BF)] * 4,
        scratch_shapes=[pltpu.VMEM((384, 256), F32), pltpu.VMEM((384, 256), F32)],
        name="prep",
    )(y, gate, up, down)


def join_kernel(p0_ref, p1_ref, p2_ref, p3_ref, gu_ref, d_ref):
    for k, ref in enumerate((p0_ref, p1_ref, p2_ref, p3_ref)):
        gu_ref[k] = ref[:192]
        d_ref[k] = ref[192:]


def join(parts):
    return pl.pallas_call(
        join_kernel,
        out_shape=(jax.ShapeDtypeStruct((4, 192, 256), BF), jax.ShapeDtypeStruct((4, 96, 256), BF)),
        name="join",
    )(*parts)


def trade(parts):
    return [parts[0]] + [lax.ppermute(parts[4 - k], "y", ring(4 - k)) for k in (1, 2, 3)]


def per_device(
    tokens,
    doc_ids,
    positions,
    attn_gain,
    mlp_gain,
    q_gain,
    key_norm_gain,
    q_weight,
    key_matrix,
    value_matrix,
    o_weight,
    gate_weight,
    up_weight,
    down_weight,
):
    rows = tokens.shape[0]
    at = jnp.stack([lax.axis_index(name).astype(jnp.int32) for name in ("z", "xh", "core", "xl")])
    xl = lax.axis_index("xl").astype(jnp.int32)
    y = lax.axis_index("y").astype(jnp.int32)
    hold = lax.optimization_barrier

    packed = pack(q_weight, key_matrix, value_matrix, o_weight)
    packed_xh = swap(packed, "xh")

    parts = trade(prepare(y[None], gate_weight, up_weight, down_weight))
    half = HEAD // 2
    freq = jnp.exp(jnp.arange(half, dtype=F32) * (-2.0 * math.log(1000000.0) / HEAD))
    angle = positions.astype(F32)[:, None] * freq[None, :]
    cs = jnp.concatenate([jnp.cos(angle), jnp.sin(angle)], axis=1)
    cs, packed_xh, *parts = hold((cs, packed_xh, *parts))
    gu_group, d_group = join(parts)
    gu_own = lax.all_gather(gu_group, ("z", "xh", "xl"), axis=0, tiled=False).reshape(8, 2, 4, 192, 256)
    d_own = lax.all_gather(d_group, ("z", "xh", "xl"), axis=0, tiled=False).reshape(8, 2, 4, 96, 256)

    lo = (jnp.arange(rows, dtype=jnp.int32) - positions)[:, None]

    here = jnp.stack([packed, packed_xh])
    up = lax.ppermute(here, "z", ring(3))
    under = lax.ppermute(here, "z", ring(1))
    across = [lax.ppermute(up[:1], "z", ring(3)), lax.ppermute(under[1:], "z", ring(1))]
    near = []
    for piece in (here, up, *across, under):
        near += [piece, swap(piece, "core")]

    o_here = jnp.concatenate([piece[:, 128:] for piece in near[::2]])
    o_up = lax.ppermute(o_here, "y", ring(3))
    o_down = lax.ppermute(o_here, "y", ring(1))
    o_far = [lax.ppermute(o_up[:4], "y", ring(3)), lax.ppermute(o_down[4:], "y", ring(1))]
    far = []
    for piece in (o_up, *o_far, o_down):
        far += [piece, swap(piece, "core")]

    q, cache = project(at, tokens, near, attn_gain, q_gain, key_norm_gain, cs)
    prior = lax.ppermute(cache[:, rows // 2 :], REQ, [(i - 1, i) for i in range(1, 16)])
    ctx = trade(attend(y[None], q, cache, prior, lo))
    keep, send = out_project(at, ctx, near, far)
    got = swap(send, "xl")

    own_rows = lax.dynamic_slice_in_dim(tokens, (xl * 4 + y) * 128, 128, 0).astype(F32)
    resid = (own_rows + (keep + got.astype(F32))).astype(BF)
    resid = hold(resid).astype(F32)
    scale = lax.rsqrt(jnp.mean(resid * resid, axis=-1, keepdims=True) + 1e-06)
    mlp_in = (resid * scale * mlp_gain).astype(BF)

    gu_own, mlp_in = hold((gu_own, mlp_in))
    gu_oth = swap(gu_own, "core")
    left = lax.ppermute(mlp_in, "y", ring(1))
    right = lax.ppermute(mlp_in, "y", ring(3))
    far_top = lax.ppermute(left[:64], "y", ring(1))
    far_bottom = lax.ppermute(right[64:], "y", ring(3))
    d_own, left, right, far_top, far_bottom = hold((d_own, left, right, far_top, far_bottom))
    d_oth = swap(d_own, "core")
    hidden = gate_up(y[None], (mlp_in, left, right, far_top, far_bottom), gu_own, gu_oth)
    keep, to_left, to_right, to_far = down(y[None], hidden, d_own, d_oth)
    via_left = lax.ppermute(to_far[:64], "y", ring(1))
    via_right = lax.ppermute(to_far[64:], "y", ring(3))
    to_right = jnp.concatenate([(to_right[:64].astype(F32) + via_left.astype(F32)).astype(BF), to_right[64:]])
    to_left = jnp.concatenate([to_left[:64], (to_left[64:].astype(F32) + via_right.astype(F32)).astype(BF)])
    from_left = lax.ppermute(to_right, "y", ring(1))
    from_right = lax.ppermute(to_left, "y", ring(3))
    total = keep + from_left.astype(F32) + from_right.astype(F32)
    return ((resid + total).astype(BF), cache)


def solution(mesh):
    fine = Mesh(mesh.devices.reshape(4, 2, 2, 2, 4), REQ + MDL)
    rows = P(REQ)
    in_specs = (
        P(REQ, None),
        rows,
        rows,
        P(),
        P(),
        P(),
        P(),
        P(REQ, MDL),
        P(REQ, MDL),
        P(REQ, MDL),
        P(MDL, REQ),
        P(MDL, REQ),
        P(MDL, REQ),
        P(REQ, MDL),
    )
    out_specs = (P(REQ + MDL, None), P(None, REQ, MDL))
    return jax.shard_map(per_device, mesh=fine, in_specs=in_specs, out_specs=out_specs, check_vma=False)
```

```python
import math

import jax
import jax.numpy as jnp
from jax import lax
from jax.experimental import pallas as pl
from jax.experimental.pallas import tpu as pltpu
from jax.sharding import Mesh
from jax.sharding import PartitionSpec as P

HEAD = 128
BF = jnp.bfloat16
F32 = jnp.float32
REQ = ("z", "xh", "core")
MDL = ("xl", "y")


def ring(step):
    return [(i, (i + step) % 4) for i in range(4)]


def swap(block, axis):
    return lax.ppermute(block, axis, [(0, 1), (1, 0)])


def qkv_kernel(core_ref, x_ref, own_ref, oth_ref, gain_ref, qg_ref, kg_ref, cs_ref, q_ref, kv_ref, tail_ref, w_ref):
    core = core_ref[0]

    @pl.when(pl.program_id(0) == 0)
    def _():
        def place(i, carry):
            for src, side in ((own_ref, core), (oth_ref, 1 - core)):
                at = pl.ds(pl.multiple_of((2 * i + side) * 128, 128), 128)
                for k in range(4):
                    w_ref[at, k * 128 : k * 128 + 128] = src[i, k * 128 : k * 128 + 128]
            return carry

        lax.fori_loop(0, 8, place, 0)

    x = x_ref[...].astype(F32)
    scale = lax.rsqrt(jnp.mean(x * x, axis=-1, keepdims=True) + 1e-06)
    normed = (x * scale * gain_ref[...]).astype(BF)
    raw = jnp.dot(normed, w_ref[...], preferred_element_type=F32)
    cs = cs_ref[...]
    turned = pltpu.roll(cs, 64, 1)
    low = lax.broadcasted_iota(jnp.int32, cs.shape, 1) < 64
    cosine = jnp.where(low, cs, turned)
    sine = jnp.where(low, -turned, cs)

    def head(t, gain):
        t = t * lax.rsqrt(jnp.mean(t * t, axis=-1, keepdims=True) + 1e-06) * gain
        return (t * cosine + pltpu.roll(t, 64, 1) * sine).astype(BF)

    q_ref[:, :128] = head(raw[:, :128], qg_ref[...])
    q_ref[:, 128:] = head(raw[:, 128:256], qg_ref[...])
    keys = head(raw[:, 256:384], kg_ref[...])
    values = raw[:, 384:].astype(BF)
    kv_ref[0] = keys
    kv_ref[1] = values

    @pl.when(pl.program_id(0) >= 2)
    def _():
        tail_ref[0] = keys
        tail_ref[1] = values


def project(core, tokens, own, oth, attn_gain, q_gain, key_gain, cs):
    rows = tokens.shape[0]
    tile = 256
    fixed = lambda *shape: pl.BlockSpec(shape, lambda i, c: (0,) * len(shape))
    return pl.pallas_call(
        qkv_kernel,
        grid_spec=pltpu.PrefetchScalarGridSpec(
            num_scalar_prefetch=1,
            grid=(rows // tile,),
            in_specs=[
                pl.BlockSpec((tile, 2048), lambda i, c: (i, 0)),
                fixed(8, 512, 128),
                fixed(8, 512, 128),
                fixed(1, 2048),
                fixed(1, 128),
                fixed(1, 128),
                pl.BlockSpec((tile, 128), lambda i, c: (i, 0)),
            ],
            out_specs=[
                pl.BlockSpec((tile, 256), lambda i, c: (i, 0)),
                pl.BlockSpec((2, tile, 128), lambda i, c: (0, i, 0)),
                pl.BlockSpec((2, tile, 128), lambda i, c: (0, jnp.maximum(i - 2, 0), 0)),
            ],
            scratch_shapes=[pltpu.VMEM((2048, 512), BF)],
        ),
        out_shape=(
            jax.ShapeDtypeStruct((rows, 256), BF),
            jax.ShapeDtypeStruct((2, rows, 128), BF),
            jax.ShapeDtypeStruct((2, rows // 2, 128), BF),
        ),
        compiler_params=pltpu.CompilerParams(vmem_limit_bytes=40 << 20),
        name="qkv",
    )(core, tokens, own, oth, attn_gain[None], q_gain[None], key_gain[None], cs)


def attend_kernel(q_ref, kv_ref, prior_ref, lo_ref, out_ref):
    factor = HEAD ** (-0.5) * math.log2(math.e)
    nt = (((1,), (1,)), ((), ()))
    for i in range(4):
        first = i * 256
        skip = 256 if i == 3 else 0
        count = first + 256
        lo = lo_ref[first : first + 256, :]
        row = lax.broadcasted_iota(jnp.int32, (256, count), 0) + first
        col = lax.broadcasted_iota(jnp.int32, (256, count), 1)
        near = (col >= lo) & (col <= row)
        prior_col = lax.broadcasted_iota(jnp.int32, (256, 512 - skip), 1) + (skip - 512)
        far = prior_col >= lo
        for h in range(2):
            q = q_ref[first : first + 256, h * 128 : h * 128 + 128]
            s1 = lax.dot_general(q, kv_ref[0, :count], nt, preferred_element_type=F32)
            s0 = lax.dot_general(q, prior_ref[0, skip:], nt, preferred_element_type=F32)
            s1 = jnp.where(near, s1, -1e30)
            s0 = jnp.where(far, s0, -1e30)
            top = jnp.maximum(jnp.max(s1, -1, keepdims=True), jnp.max(s0, -1, keepdims=True))
            e1 = jnp.exp2((s1 - top) * factor)
            e0 = jnp.exp2((s0 - top) * factor)
            inv = 1.0 / (jnp.sum(e1, -1, keepdims=True) + jnp.sum(e0, -1, keepdims=True))
            p1 = (e1 * inv).astype(BF)
            p0 = (e0 * inv).astype(BF)
            o = jnp.dot(p1, kv_ref[1, :count], preferred_element_type=F32)
            o = o + jnp.dot(p0, prior_ref[1, skip:], preferred_element_type=F32)
            o = o.astype(BF)
            for part in range(2):
                block = 2 * i + part
                out_ref[block % 4, block // 4, :, h * 128 : h * 128 + 128] = o[part * 128 : part * 128 + 128]


def attend(q, kv, prior, lo):
    return pl.pallas_call(
        attend_kernel,
        out_shape=jax.ShapeDtypeStruct((4, 2, 128, 256), BF),
        compiler_params=pltpu.CompilerParams(vmem_limit_bytes=40 << 20),
        name="attend",
    )(q, kv, prior, lo)


def out_kernel(at_ref, ctx_ref, own_ref, oth_ref, keep_ref, send_ref, w_ref, x_ref, sems):
    core = at_ref[0]
    xl = at_ref[1]

    def each(act):
        def step(n, carry):
            s, i = n // 8, lax.rem(n, 8)
            for which, (src, side) in enumerate(((own_ref, core), (oth_ref, 1 - core))):
                at = pl.ds(pl.multiple_of((2 * i + side) * 128, 128), 128)
                act(pltpu.make_async_copy(
                    src.at[s, i], w_ref.at[pl.ds(pl.multiple_of(s * 256, 256), 256), at], sems.at[which, s, i]
                ))
            return carry

        lax.fori_loop(0, 32, step, 0)

    each(lambda c: c.start())
    for s in range(4):
        x_ref[:128, s * 256 : s * 256 + 256] = ctx_ref[s, xl]
        x_ref[128:, s * 256 : s * 256 + 256] = ctx_ref[s, 1 - xl]
    each(lambda c: c.wait())
    x = x_ref[...]

    def column(n, carry):
        at = pl.ds(pl.multiple_of(n * 512, 512), 512)
        total = jnp.dot(x, w_ref[:, at], preferred_element_type=F32)
        keep_ref[:, at] = total[:128]
        send_ref[:, at] = total[128:].astype(BF)
        return carry

    lax.fori_loop(0, 4, column, 0)


def out_project(at, ctx, own, oth):
    vm = pl.BlockSpec(memory_space=pltpu.VMEM)
    anywhere = pl.BlockSpec(memory_space=pl.ANY)
    return pl.pallas_call(
        out_kernel,
        in_specs=[pl.BlockSpec(memory_space=pltpu.SMEM)] + [vm] + [anywhere] * 2,
        out_shape=(
            jax.ShapeDtypeStruct((128, 2048), F32),
            jax.ShapeDtypeStruct((128, 2048), BF),
        ),
        scratch_shapes=[
            pltpu.VMEM((1024, 2048), BF),
            pltpu.VMEM((256, 1024), BF),
            pltpu.SemaphoreType.DMA((2, 4, 8)),
        ],
        compiler_params=pltpu.CompilerParams(vmem_limit_bytes=40 << 20),
        name="oproj",
    )(at, ctx, own, oth)


def fetcher(own_ref, oth_ref, w_ref, sems, y):
    def copy(c, g, m):
        src = own_ref if c == 0 else oth_ref
        at = pl.multiple_of(((m // 4) * 4 + lax.rem(y + lax.rem(m, 4), 4)) * 256, 256)
        return pltpu.make_async_copy(
            src.at[:, m // 4, lax.rem(m, 4), g * 96 : g * 96 + 96, :],
            w_ref.at[g, c * 8 : c * 8 + 8, :, pl.ds(at, 256)],
            sems.at[g, c, m],
        )

    def each(c, groups, act):
        def step(m, carry):
            for g in range(groups):
                act(copy(c, g, m))
            return carry

        lax.fori_loop(0, 8, step, 0)

    return each


def gate_kernel(y_ref, x0_ref, x1_ref, x2_ref, x3_ref, x4_ref, own_ref, oth_ref, hid_ref, w_ref, x_ref, sems):
    nt = (((1,), (1,)), ((), ()))
    each = fetcher(own_ref, oth_ref, w_ref, sems, y_ref[0])
    each(0, 2, lambda c: c.start())
    each(1, 2, lambda c: c.start())
    x_ref[0:128] = x0_ref[...]
    x_ref[128:256] = x1_ref[...]
    x_ref[256:384] = x2_ref[...]
    x_ref[384:448] = x3_ref[...]
    x_ref[448:512] = x4_ref[...]
    x = x_ref[...]

    for c in range(2):
        each(c, 2, lambda copy: copy.wait())
        gate_w = w_ref[0, c * 8 : c * 8 + 8].reshape(768, 2048)
        up_w = w_ref[1, c * 8 : c * 8 + 8].reshape(768, 2048)
        for t in range(3):
            gate = lax.dot_general(x, gate_w[t * 256 : t * 256 + 256], nt, preferred_element_type=F32)
            upper = lax.dot_general(x, up_w[t * 256 : t * 256 + 256], nt, preferred_element_type=F32)
            hidden = gate / (1.0 + jnp.exp(-gate)) * upper
            at = c * 768 + t * 256
            hid_ref[:, at : at + 256] = hidden.astype(BF)


def down_kernel(y_ref, hid_ref, own_ref, oth_ref, keep_ref, left_ref, right_ref, far_ref, w_ref, sems):
    each = fetcher(own_ref, oth_ref, w_ref, sems, y_ref[0])
    for c in range(2):
        each(c, 1, lambda copy: copy.start())
    for c in range(2):
        each(c, 1, lambda copy: copy.wait())
    hid = hid_ref[...]

    def column(n, carry):
        at = pl.ds(pl.multiple_of(n * 512, 512), 512)
        out = jnp.dot(hid, w_ref[0, :, :, at].reshape(1536, 512), preferred_element_type=F32)
        keep_ref[:, at] = out[:128]
        left_ref[:, at] = out[128:256].astype(BF)
        right_ref[:, at] = out[256:384].astype(BF)
        far_ref[:, at] = out[384:].astype(BF)
        return carry

    lax.fori_loop(0, 4, column, 0)


def gate_up(y, pieces, own, oth):
    vm = pl.BlockSpec(memory_space=pltpu.VMEM)
    hbm = pl.BlockSpec(memory_space=pltpu.HBM)
    return pl.pallas_call(
        gate_kernel,
        in_specs=[pl.BlockSpec(memory_space=pltpu.SMEM)] + [vm] * 5 + [hbm] * 2,
        out_shape=jax.ShapeDtypeStruct((512, 1536), BF),
        scratch_shapes=[
            pltpu.VMEM((2, 16, 96, 2048), BF),
            pltpu.VMEM((512, 2048), BF),
            pltpu.SemaphoreType.DMA((2, 2, 8)),
        ],
        compiler_params=pltpu.CompilerParams(vmem_limit_bytes=40 << 20),
        name="gate_up",
    )(y, *pieces, own, oth)


def down(y, hidden, own, oth):
    vm = pl.BlockSpec(memory_space=pltpu.VMEM)
    hbm = pl.BlockSpec(memory_space=pltpu.HBM)
    part = jax.ShapeDtypeStruct((128, 2048), BF)
    return pl.pallas_call(
        down_kernel,
        in_specs=[pl.BlockSpec(memory_space=pltpu.SMEM), vm] + [hbm] * 2,
        out_shape=(jax.ShapeDtypeStruct((128, 2048), F32), part, part, part),
        scratch_shapes=[
            pltpu.VMEM((1, 16, 96, 2048), BF),
            pltpu.SemaphoreType.DMA((1, 2, 8)),
        ],
        compiler_params=pltpu.CompilerParams(vmem_limit_bytes=40 << 20),
        name="down",
    )(y, hidden, own, oth)


def pack_kernel(q_ref, k_ref, v_ref, o_ref, out_ref):
    parts = [q_ref[:, :128], q_ref[:, 128:], k_ref[...], v_ref[...], o_ref[...]]
    whole = jnp.concatenate(parts, axis=0).astype(BF)
    for i in range(8):
        out_ref[i] = whole


def pack(q, k, v, o):
    return pl.pallas_call(
        pack_kernel,
        out_shape=jax.ShapeDtypeStruct((8, 768, 128), BF),
        name="pack",
    )(q, k, v, o)


def prep_kernel(y_ref, gate_ref, up_ref, down_ref, p0_ref, p1_ref, p2_ref, p3_ref, g_ref, u_ref):
    g_ref[...] = gate_ref[...].T
    u_ref[...] = up_ref[...].T
    for k, out_ref in enumerate((p0_ref, p1_ref, p2_ref, p3_ref)):
        at = pl.ds(pl.multiple_of(lax.rem(y_ref[0] + k, 4) * 96, 96), 96)
        out_ref[:96] = g_ref[at, :].astype(BF)
        out_ref[96:192] = u_ref[at, :].astype(BF)
        out_ref[192:] = down_ref[at, :].astype(BF)


def prepare(y, gate, up, down):
    vm = pl.BlockSpec(memory_space=pltpu.VMEM)
    return pl.pallas_call(
        prep_kernel,
        in_specs=[pl.BlockSpec(memory_space=pltpu.SMEM)] + [vm] * 3,
        out_shape=[jax.ShapeDtypeStruct((288, 256), BF)] * 4,
        scratch_shapes=[pltpu.VMEM((384, 256), F32), pltpu.VMEM((384, 256), F32)],
        name="prep",
    )(y, gate, up, down)


def join_kernel(p0_ref, p1_ref, p2_ref, p3_ref, gu_ref, d_ref):
    for k, ref in enumerate((p0_ref, p1_ref, p2_ref, p3_ref)):
        gu_ref[k] = ref[:192]
        d_ref[k] = ref[192:]


def join(parts):
    return pl.pallas_call(
        join_kernel,
        out_shape=(jax.ShapeDtypeStruct((4, 192, 256), BF), jax.ShapeDtypeStruct((4, 96, 256), BF)),
        name="join",
    )(*parts)


def trade(parts):
    return [parts[0]] + [lax.ppermute(parts[4 - k], "y", ring(4 - k)) for k in (1, 2, 3)]


def per_device(
    tokens,
    doc_ids,
    positions,
    attn_gain,
    mlp_gain,
    q_gain,
    key_norm_gain,
    q_weight,
    key_matrix,
    value_matrix,
    o_weight,
    gate_weight,
    up_weight,
    down_weight,
):
    rows = tokens.shape[0]
    core = lax.axis_index("core").astype(jnp.int32)
    xl = lax.axis_index("xl").astype(jnp.int32)
    y = lax.axis_index("y").astype(jnp.int32)
    hold = lax.optimization_barrier

    packed = pack(q_weight, key_matrix, value_matrix, o_weight)
    at_own = lax.all_to_all(packed, ("z", "xh"), split_axis=0, concat_axis=0, tiled=True)

    parts = trade(prepare(y[None], gate_weight, up_weight, down_weight))
    half = HEAD // 2
    freq = jnp.exp(jnp.arange(half, dtype=F32) * (-2.0 * math.log(1000000.0) / HEAD))
    angle = positions.astype(F32)[:, None] * freq[None, :]
    cs = jnp.concatenate([jnp.cos(angle), jnp.sin(angle)], axis=1)
    cs, at_own, *parts = hold((cs, at_own, *parts))
    gu_group, d_group = join(parts)
    gu_own = lax.all_gather(gu_group, ("z", "xh", "xl"), axis=0, tiled=False).reshape(8, 2, 4, 192, 256)
    d_own = lax.all_gather(d_group, ("z", "xh", "xl"), axis=0, tiled=False).reshape(8, 2, 4, 96, 256)

    lo = (jnp.arange(rows, dtype=jnp.int32) - positions)[:, None]

    at_oth = swap(at_own, "core")

    o_wide = jnp.broadcast_to(at_own[None, :, 512:], (4, 8, 256, 128))
    o_own = lax.all_to_all(o_wide, "y", split_axis=0, concat_axis=0, tiled=True)

    q, cache, tail = project(core[None], tokens, at_own, at_oth, attn_gain, q_gain, key_norm_gain, cs)
    prior = lax.ppermute(tail, REQ, [(i - 1, i) for i in range(1, 16)])
    ctx = attend(q, cache, prior, lo)
    ctx, o_own = hold((ctx, o_own))
    o_oth = swap(o_own, "core")
    ctx = lax.all_to_all(ctx, "y", split_axis=0, concat_axis=0, tiled=True)
    keep, send = out_project(jnp.stack([core, xl]), ctx, o_own, o_oth)
    got = swap(send, "xl")

    own_rows = lax.dynamic_slice_in_dim(tokens, (xl * 4 + y) * 128, 128, 0).astype(F32)
    resid = (own_rows + (keep + got.astype(F32))).astype(BF)
    resid = hold(resid).astype(F32)
    scale = lax.rsqrt(jnp.mean(resid * resid, axis=-1, keepdims=True) + 1e-06)
    mlp_in = (resid * scale * mlp_gain).astype(BF)

    gu_own, mlp_in = hold((gu_own, mlp_in))
    gu_oth = swap(gu_own, "core")
    left = lax.ppermute(mlp_in, "y", ring(1))
    right = lax.ppermute(mlp_in, "y", ring(3))
    far_top = lax.ppermute(left[:64], "y", ring(1))
    far_bottom = lax.ppermute(right[64:], "y", ring(3))
    d_own, left, right, far_top, far_bottom = hold((d_own, left, right, far_top, far_bottom))
    d_oth = swap(d_own, "core")
    hidden = gate_up(y[None], (mlp_in, left, right, far_top, far_bottom), gu_own, gu_oth)
    keep, to_left, to_right, to_far = down(y[None], hidden, d_own, d_oth)
    via_left = lax.ppermute(to_far[:64], "y", ring(1))
    via_right = lax.ppermute(to_far[64:], "y", ring(3))
    to_right = jnp.concatenate([(to_right[:64].astype(F32) + via_left.astype(F32)).astype(BF), to_right[64:]])
    to_left = jnp.concatenate([to_left[:64], (to_left[64:].astype(F32) + via_right.astype(F32)).astype(BF)])
    from_left = lax.ppermute(to_right, "y", ring(1))
    from_right = lax.ppermute(to_left, "y", ring(3))
    total = keep + from_left.astype(F32) + from_right.astype(F32)
    return ((resid + total).astype(BF), cache)


def solution(mesh):
    fine = Mesh(mesh.devices.reshape(4, 2, 2, 2, 4), REQ + MDL)
    rows = P(REQ)
    in_specs = (
        P(REQ, None),
        rows,
        rows,
        P(),
        P(),
        P(),
        P(),
        P(REQ, MDL),
        P(REQ, MDL),
        P(REQ, MDL),
        P(MDL, REQ),
        P(MDL, REQ),
        P(MDL, REQ),
        P(REQ, MDL),
    )
    out_specs = (P(REQ + MDL, None), P(None, REQ, MDL))
    return jax.shard_map(per_device, mesh=fine, in_specs=in_specs, out_specs=out_specs, check_vma=False)
```

```python
import math

import jax
import jax.numpy as jnp
from jax import lax
from jax.experimental import pallas as pl
from jax.experimental.pallas import tpu as pltpu
from jax.sharding import Mesh
from jax.sharding import PartitionSpec as P

HEAD = 128
BF = jnp.bfloat16
F32 = jnp.float32
REQ = ("z", "xh", "core")
MDL = ("xl", "y")


def ring(step):
    return [(i, (i + step) % 4) for i in range(4)]


def swap(block, axis):
    return lax.ppermute(block, axis, [(0, 1), (1, 0)])


def qkv_kernel(core_ref, x_ref, own_ref, oth_ref, gain_ref, qg_ref, kg_ref, cs_ref, q_ref, kv_ref, tail_ref, w_ref):
    core = core_ref[0]

    @pl.when(pl.program_id(0) == 0)
    def _():
        def place(i, carry):
            for src, side in ((own_ref, core), (oth_ref, 1 - core)):
                at = pl.ds(pl.multiple_of((2 * i + side) * 128, 128), 128)
                for k in range(4):
                    w_ref[at, k * 128 : k * 128 + 128] = src[i, k * 128 : k * 128 + 128]
            return carry

        lax.fori_loop(0, 8, place, 0)

    x = x_ref[...].astype(F32)
    scale = lax.rsqrt(jnp.mean(x * x, axis=-1, keepdims=True) + 1e-06)
    normed = (x * scale * gain_ref[...]).astype(BF)
    raw = jnp.dot(normed, w_ref[...], preferred_element_type=F32)
    cs = cs_ref[...]
    turned = pltpu.roll(cs, 64, 1)
    low = lax.broadcasted_iota(jnp.int32, cs.shape, 1) < 64
    cosine = jnp.where(low, cs, turned)
    sine = jnp.where(low, -turned, cs)

    def head(t, gain):
        t = t * lax.rsqrt(jnp.mean(t * t, axis=-1, keepdims=True) + 1e-06) * gain
        return (t * cosine + pltpu.roll(t, 64, 1) * sine).astype(BF)

    q_ref[:, :128] = head(raw[:, :128], qg_ref[...])
    q_ref[:, 128:] = head(raw[:, 128:256], qg_ref[...])
    keys = head(raw[:, 256:384], kg_ref[...])
    values = raw[:, 384:].astype(BF)
    kv_ref[0] = keys
    kv_ref[1] = values

    @pl.when(pl.program_id(0) >= 2)
    def _():
        tail_ref[0] = keys
        tail_ref[1] = values


def project(core, tokens, own, oth, attn_gain, q_gain, key_gain, cs):
    rows = tokens.shape[0]
    tile = 256
    fixed = lambda *shape: pl.BlockSpec(shape, lambda i, c: (0,) * len(shape))
    return pl.pallas_call(
        qkv_kernel,
        grid_spec=pltpu.PrefetchScalarGridSpec(
            num_scalar_prefetch=1,
            grid=(rows // tile,),
            in_specs=[
                pl.BlockSpec((tile, 2048), lambda i, c: (i, 0)),
                fixed(8, 512, 128),
                fixed(8, 512, 128),
                fixed(1, 2048),
                fixed(1, 128),
                fixed(1, 128),
                pl.BlockSpec((tile, 128), lambda i, c: (i, 0)),
            ],
            out_specs=[
                pl.BlockSpec((tile, 256), lambda i, c: (i, 0)),
                pl.BlockSpec((2, tile, 128), lambda i, c: (0, i, 0)),
                pl.BlockSpec((2, tile, 128), lambda i, c: (0, jnp.maximum(i - 2, 0), 0)),
            ],
            scratch_shapes=[pltpu.VMEM((2048, 512), BF)],
        ),
        out_shape=(
            jax.ShapeDtypeStruct((rows, 256), BF),
            jax.ShapeDtypeStruct((2, rows, 128), BF),
            jax.ShapeDtypeStruct((2, rows // 2, 128), BF),
        ),
        compiler_params=pltpu.CompilerParams(vmem_limit_bytes=40 << 20),
        name="qkv",
    )(core, tokens, own, oth, attn_gain[None], q_gain[None], key_gain[None], cs)


def attend_kernel(q_ref, kv_ref, prior_ref, lo_ref, out_ref):
    factor = HEAD ** (-0.5) * math.log2(math.e)
    nt = (((1,), (1,)), ((), ()))
    for i in range(4):
        first = i * 256
        skip = 256 if i == 3 else 0
        count = first + 256
        lo = lo_ref[first : first + 256, :]
        row = lax.broadcasted_iota(jnp.int32, (256, count), 0) + first
        col = lax.broadcasted_iota(jnp.int32, (256, count), 1)
        near = (col >= lo) & (col <= row)
        prior_col = lax.broadcasted_iota(jnp.int32, (256, 512 - skip), 1) + (skip - 512)
        far = prior_col >= lo
        for h in range(2):
            q = q_ref[first : first + 256, h * 128 : h * 128 + 128]
            s1 = lax.dot_general(q, kv_ref[0, :count], nt, preferred_element_type=F32)
            s0 = lax.dot_general(q, prior_ref[0, skip:], nt, preferred_element_type=F32)
            s1 = jnp.where(near, s1, -1e30)
            s0 = jnp.where(far, s0, -1e30)
            top = jnp.maximum(jnp.max(s1, -1, keepdims=True), jnp.max(s0, -1, keepdims=True))
            e1 = jnp.exp2((s1 - top) * factor)
            e0 = jnp.exp2((s0 - top) * factor)
            inv = 1.0 / (jnp.sum(e1, -1, keepdims=True) + jnp.sum(e0, -1, keepdims=True))
            p1 = (e1 * inv).astype(BF)
            p0 = (e0 * inv).astype(BF)
            o = jnp.dot(p1, kv_ref[1, :count], preferred_element_type=F32)
            o = o + jnp.dot(p0, prior_ref[1, skip:], preferred_element_type=F32)
            o = o.astype(BF)
            for part in range(2):
                block = 2 * i + part
                out_ref[block % 4, block // 4, :, h * 128 : h * 128 + 128] = o[part * 128 : part * 128 + 128]


def attend(q, kv, prior, lo):
    return pl.pallas_call(
        attend_kernel,
        out_shape=jax.ShapeDtypeStruct((4, 2, 128, 256), BF),
        compiler_params=pltpu.CompilerParams(vmem_limit_bytes=40 << 20),
        name="attend",
    )(q, kv, prior, lo)


def out_kernel(at_ref, ctx_ref, own_ref, oth_ref, keep_ref, send_ref, w_ref, x_ref, sems):
    core = at_ref[0]
    xl = at_ref[1]

    def each(act):
        def step(n, carry):
            s, i = n // 8, lax.rem(n, 8)
            for which, (src, side) in enumerate(((own_ref, core), (oth_ref, 1 - core))):
                at = pl.ds(pl.multiple_of((2 * i + side) * 128, 128), 128)
                act(pltpu.make_async_copy(
                    src.at[s, i], w_ref.at[pl.ds(pl.multiple_of(s * 256, 256), 256), at], sems.at[which, s, i]
                ))
            return carry

        lax.fori_loop(0, 32, step, 0)

    each(lambda c: c.start())
    for s in range(4):
        x_ref[:128, s * 256 : s * 256 + 256] = ctx_ref[s, xl]
        x_ref[128:, s * 256 : s * 256 + 256] = ctx_ref[s, 1 - xl]
    each(lambda c: c.wait())
    x = x_ref[...]

    def column(n, carry):
        at = pl.ds(pl.multiple_of(n * 512, 512), 512)
        total = jnp.dot(x, w_ref[:, at], preferred_element_type=F32)
        keep_ref[:, at] = total[:128]
        send_ref[:, at] = total[128:].astype(BF)
        return carry

    lax.fori_loop(0, 4, column, 0)


def out_project(at, ctx, own, oth):
    vm = pl.BlockSpec(memory_space=pltpu.VMEM)
    anywhere = pl.BlockSpec(memory_space=pl.ANY)
    return pl.pallas_call(
        out_kernel,
        in_specs=[pl.BlockSpec(memory_space=pltpu.SMEM)] + [vm] + [anywhere] * 2,
        out_shape=(
            jax.ShapeDtypeStruct((128, 2048), F32),
            jax.ShapeDtypeStruct((128, 2048), BF),
        ),
        scratch_shapes=[
            pltpu.VMEM((1024, 2048), BF),
            pltpu.VMEM((256, 1024), BF),
            pltpu.SemaphoreType.DMA((2, 4, 8)),
        ],
        compiler_params=pltpu.CompilerParams(vmem_limit_bytes=40 << 20),
        name="oproj",
    )(at, ctx, own, oth)


def fetcher(own_ref, oth_ref, w_ref, sems, y, first):
    def copy(c, g, m):
        src = own_ref if c == 0 else oth_ref
        at = pl.multiple_of(((m // 4) * 4 + lax.rem(y + lax.rem(m, 4), 4)) * 256, 256)
        return pltpu.make_async_copy(
            src.at[:, m // 4, lax.rem(m, 4), first + g * 96 : first + g * 96 + 96, :],
            w_ref.at[g, c * 8 : c * 8 + 8, :, pl.ds(at, 256)],
            sems.at[g, c, m],
        )

    def each(c, groups, act):
        def step(m, carry):
            for g in range(groups):
                act(copy(c, g, m))
            return carry

        lax.fori_loop(0, 8, step, 0)

    return each


def gate_kernel(y_ref, x0_ref, x1_ref, x2_ref, x3_ref, x4_ref, own_ref, oth_ref, hid_ref, w_ref, x_ref, sems):
    nt = (((1,), (1,)), ((), ()))
    each = fetcher(own_ref, oth_ref, w_ref, sems, y_ref[0], 0)
    each(0, 2, lambda c: c.start())
    each(1, 2, lambda c: c.start())
    x_ref[0:128] = x0_ref[...]
    x_ref[128:256] = x1_ref[...]
    x_ref[256:384] = x2_ref[...]
    x_ref[384:448] = x3_ref[...]
    x_ref[448:512] = x4_ref[...]
    x = x_ref[...]

    for c in range(2):
        each(c, 2, lambda copy: copy.wait())
        gate_w = w_ref[0, c * 8 : c * 8 + 8].reshape(768, 2048)
        up_w = w_ref[1, c * 8 : c * 8 + 8].reshape(768, 2048)
        for t in range(3):
            gate = lax.dot_general(x, gate_w[t * 256 : t * 256 + 256], nt, preferred_element_type=F32)
            upper = lax.dot_general(x, up_w[t * 256 : t * 256 + 256], nt, preferred_element_type=F32)
            hidden = gate / (1.0 + jnp.exp(-gate)) * upper
            at = c * 768 + t * 256
            hid_ref[:, at : at + 256] = hidden.astype(BF)


def far_kernel(y_ref, hid_ref, own_ref, oth_ref, top_ref, bottom_ref, w_ref, sems):
    each = fetcher(own_ref, oth_ref, w_ref, sems, y_ref[0], 192)
    for c in range(2):
        each(c, 1, lambda copy: copy.start())
    for c in range(2):
        each(c, 1, lambda copy: copy.wait())
    hid = hid_ref[384:]

    def column(n, carry):
        at = pl.ds(pl.multiple_of(n * 512, 512), 512)
        out = jnp.dot(hid, w_ref[0, :, :, at].reshape(1536, 512), preferred_element_type=F32)
        top_ref[:, at] = out[:64].astype(BF)
        bottom_ref[:, at] = out[64:].astype(BF)
        return carry

    lax.fori_loop(0, 4, column, 0)


def down_kernel(hid_ref, w_ref, keep_ref, left_ref, right_ref):
    hid = hid_ref[:384]

    def column(n, carry):
        at = pl.ds(pl.multiple_of(n * 512, 512), 512)
        out = jnp.dot(hid, w_ref[0, :, :, at].reshape(1536, 512), preferred_element_type=F32)
        keep_ref[:, at] = out[:128]
        left_ref[:, at] = out[128:256].astype(BF)
        right_ref[:, at] = out[256:].astype(BF)
        return carry

    lax.fori_loop(0, 4, column, 0)


def gate_up(y, pieces, own, oth):
    vm = pl.BlockSpec(memory_space=pltpu.VMEM)
    hbm = pl.BlockSpec(memory_space=pltpu.HBM)
    return pl.pallas_call(
        gate_kernel,
        in_specs=[pl.BlockSpec(memory_space=pltpu.SMEM)] + [vm] * 5 + [hbm] * 2,
        out_shape=jax.ShapeDtypeStruct((512, 1536), BF),
        scratch_shapes=[
            pltpu.VMEM((2, 16, 96, 2048), BF),
            pltpu.VMEM((512, 2048), BF),
            pltpu.SemaphoreType.DMA((2, 2, 8)),
        ],
        compiler_params=pltpu.CompilerParams(vmem_limit_bytes=40 << 20),
        name="gate_up",
    )(y, *pieces, own, oth)


def down_far(y, hidden, own, oth):
    vm = pl.BlockSpec(memory_space=pltpu.VMEM)
    hbm = pl.BlockSpec(memory_space=pltpu.HBM)
    half = jax.ShapeDtypeStruct((64, 2048), BF)
    return pl.pallas_call(
        far_kernel,
        in_specs=[pl.BlockSpec(memory_space=pltpu.SMEM), vm] + [hbm] * 2,
        out_shape=(half, half, jax.ShapeDtypeStruct((1, 16, 96, 2048), BF)),
        scratch_shapes=[pltpu.SemaphoreType.DMA((1, 2, 8))],
        compiler_params=pltpu.CompilerParams(vmem_limit_bytes=40 << 20),
        name="down_far",
    )(y, hidden, own, oth)


def down(hidden, weight):
    part = jax.ShapeDtypeStruct((128, 2048), BF)
    return pl.pallas_call(
        down_kernel,
        out_shape=(jax.ShapeDtypeStruct((128, 2048), F32), part, part),
        compiler_params=pltpu.CompilerParams(vmem_limit_bytes=40 << 20),
        name="down",
    )(hidden, weight)


def pack_kernel(q_ref, k_ref, v_ref, o_ref, out_ref):
    parts = [q_ref[:, :128], q_ref[:, 128:], k_ref[...], v_ref[...], o_ref[...]]
    whole = jnp.concatenate(parts, axis=0).astype(BF)
    for i in range(8):
        out_ref[i] = whole


def pack(q, k, v, o):
    return pl.pallas_call(
        pack_kernel,
        out_shape=jax.ShapeDtypeStruct((8, 768, 128), BF),
        name="pack",
    )(q, k, v, o)


def prep_kernel(y_ref, gate_ref, up_ref, down_ref, p0_ref, p1_ref, p2_ref, p3_ref, g_ref, u_ref):
    g_ref[...] = gate_ref[...].T
    u_ref[...] = up_ref[...].T
    for k, out_ref in enumerate((p0_ref, p1_ref, p2_ref, p3_ref)):
        at = pl.ds(pl.multiple_of(lax.rem(y_ref[0] + k, 4) * 96, 96), 96)
        out_ref[:96] = g_ref[at, :].astype(BF)
        out_ref[96:192] = u_ref[at, :].astype(BF)
        out_ref[192:] = down_ref[at, :].astype(BF)


def prepare(y, gate, up, down):
    vm = pl.BlockSpec(memory_space=pltpu.VMEM)
    return pl.pallas_call(
        prep_kernel,
        in_specs=[pl.BlockSpec(memory_space=pltpu.SMEM)] + [vm] * 3,
        out_shape=[jax.ShapeDtypeStruct((288, 256), BF)] * 4,
        scratch_shapes=[pltpu.VMEM((384, 256), F32), pltpu.VMEM((384, 256), F32)],
        name="prep",
    )(y, gate, up, down)


def join_kernel(p0_ref, p1_ref, p2_ref, p3_ref, out_ref):
    for k, ref in enumerate((p0_ref, p1_ref, p2_ref, p3_ref)):
        out_ref[k] = ref[...]


def join(parts):
    return pl.pallas_call(join_kernel, out_shape=jax.ShapeDtypeStruct((4, 288, 256), BF), name="join")(*parts)


def trade(parts):
    return [parts[0]] + [lax.ppermute(parts[4 - k], "y", ring(4 - k)) for k in (1, 2, 3)]


def per_device(
    tokens,
    doc_ids,
    positions,
    attn_gain,
    mlp_gain,
    q_gain,
    key_norm_gain,
    q_weight,
    key_matrix,
    value_matrix,
    o_weight,
    gate_weight,
    up_weight,
    down_weight,
):
    rows = tokens.shape[0]
    core = lax.axis_index("core").astype(jnp.int32)
    xl = lax.axis_index("xl").astype(jnp.int32)
    y = lax.axis_index("y").astype(jnp.int32)
    hold = lax.optimization_barrier

    packed = pack(q_weight, key_matrix, value_matrix, o_weight)
    at_own = lax.all_to_all(packed, ("z", "xh"), split_axis=0, concat_axis=0, tiled=True)

    parts = trade(prepare(y[None], gate_weight, up_weight, down_weight))
    half = HEAD // 2
    freq = jnp.exp(jnp.arange(half, dtype=F32) * (-2.0 * math.log(1000000.0) / HEAD))
    angle = positions.astype(F32)[:, None] * freq[None, :]
    cs = jnp.concatenate([jnp.cos(angle), jnp.sin(angle)], axis=1)
    cs, at_own, *parts = hold((cs, at_own, *parts))
    mlp_own = lax.all_gather(join(parts), ("z", "xh", "xl"), axis=0, tiled=False).reshape(8, 2, 4, 288, 256)
    lo = (jnp.arange(rows, dtype=jnp.int32) - positions)[:, None]

    at_oth = swap(at_own, "core")

    o_wide = jnp.broadcast_to(at_own[None, :, 512:], (4, 8, 256, 128))
    o_own = lax.all_to_all(o_wide, "y", split_axis=0, concat_axis=0, tiled=True)

    q, cache, tail = project(core[None], tokens, at_own, at_oth, attn_gain, q_gain, key_norm_gain, cs)
    prior = lax.ppermute(tail, REQ, [(i - 1, i) for i in range(1, 16)])
    ctx = attend(q, cache, prior, lo)
    ctx, o_own = hold((ctx, o_own))
    o_oth = swap(o_own, "core")
    ctx = lax.all_to_all(ctx, "y", split_axis=0, concat_axis=0, tiled=True)
    keep, send = out_project(jnp.stack([core, xl]), ctx, o_own, o_oth)
    got = swap(send, "xl")

    own_rows = lax.dynamic_slice_in_dim(tokens, (xl * 4 + y) * 128, 128, 0).astype(F32)
    resid = (own_rows + (keep + got.astype(F32))).astype(BF)
    resid = hold(resid).astype(F32)
    scale = lax.rsqrt(jnp.mean(resid * resid, axis=-1, keepdims=True) + 1e-06)
    mlp_in = (resid * scale * mlp_gain).astype(BF)

    left = lax.ppermute(mlp_in, "y", ring(1))
    right = lax.ppermute(mlp_in, "y", ring(3))
    mlp_own, left, right = hold((mlp_own, left, right))
    mlp_oth = swap(mlp_own, "core")
    far_top = lax.ppermute(left[:64], "y", ring(1))
    far_bottom = lax.ppermute(right[64:], "y", ring(3))
    hidden = gate_up(y[None], (mlp_in, left, right, far_top, far_bottom), mlp_own, mlp_oth)
    top, bottom, weight = down_far(y[None], hidden, mlp_own, mlp_oth)
    via_left = lax.ppermute(top, "y", ring(1))
    via_right = lax.ppermute(bottom, "y", ring(3))
    keep, to_left, to_right = down(hidden, weight)
    to_right = jnp.concatenate([(to_right[:64].astype(F32) + via_left.astype(F32)).astype(BF), to_right[64:]])
    to_left = jnp.concatenate([to_left[:64], (to_left[64:].astype(F32) + via_right.astype(F32)).astype(BF)])
    from_left = lax.ppermute(to_right, "y", ring(1))
    from_right = lax.ppermute(to_left, "y", ring(3))
    total = keep + from_left.astype(F32) + from_right.astype(F32)
    return ((resid + total).astype(BF), cache)


def solution(mesh):
    fine = Mesh(mesh.devices.reshape(4, 2, 2, 2, 4), REQ + MDL)
    rows = P(REQ)
    in_specs = (
        P(REQ, None),
        rows,
        rows,
        P(),
        P(),
        P(),
        P(),
        P(REQ, MDL),
        P(REQ, MDL),
        P(REQ, MDL),
        P(MDL, REQ),
        P(MDL, REQ),
        P(MDL, REQ),
        P(REQ, MDL),
    )
    out_specs = (P(REQ + MDL, None), P(None, REQ, MDL))
    return jax.shard_map(per_device, mesh=fine, in_specs=in_specs, out_specs=out_specs, check_vma=False)
```

```python
import math

import jax
import jax.numpy as jnp
from jax import lax
from jax.experimental import pallas as pl
from jax.experimental.pallas import tpu as pltpu
from jax.sharding import Mesh
from jax.sharding import PartitionSpec as P

HEAD = 128
BF = jnp.bfloat16
F32 = jnp.float32
REQ = ("z", "xh", "core")
MDL = ("xl", "y")


def ring(step):
    return [(i, (i + step) % 4) for i in range(4)]


def swap(block, axis):
    return lax.ppermute(block, axis, [(0, 1), (1, 0)])


def norm_kernel(x_ref, gain_ref, out_ref):
    x = x_ref[...].astype(F32)
    scale = lax.rsqrt(jnp.mean(x * x, axis=-1, keepdims=True) + 1e-06)
    out_ref[...] = (x * scale * gain_ref[...]).astype(BF)


def normalise(x, gain):
    rows, tile = x.shape[0], min(256, x.shape[0])
    block = pl.BlockSpec((tile, 2048), lambda i: (i, 0))
    return pl.pallas_call(
        norm_kernel,
        grid=(rows // tile,),
        in_specs=[block, pl.BlockSpec((1, 2048), lambda i: (0, 0))],
        out_specs=block,
        out_shape=jax.ShapeDtypeStruct(x.shape, BF),
        name="norm",
    )(x, gain[None])


def qkv_kernel(core_ref, x_ref, own_ref, oth_ref, qg_ref, kg_ref, cs_ref, q_ref, kv_ref, tail_ref, w_ref):
    core = core_ref[0]

    @pl.when(pl.program_id(0) == 0)
    def _():
        def place(i, carry):
            for src, side in ((own_ref, core), (oth_ref, 1 - core)):
                at = pl.ds(pl.multiple_of((2 * i + side) * 128, 128), 128)
                for k in range(4):
                    w_ref[at, k * 128 : k * 128 + 128] = src[i, k * 128 : k * 128 + 128]
            return carry

        lax.fori_loop(0, 8, place, 0)

    raw = jnp.dot(x_ref[...], w_ref[...], preferred_element_type=F32)
    cs = cs_ref[...]
    turned = pltpu.roll(cs, 64, 1)
    low = lax.broadcasted_iota(jnp.int32, cs.shape, 1) < 64
    cosine = jnp.where(low, cs, turned)
    sine = jnp.where(low, -turned, cs)

    def head(t, gain):
        t = t * lax.rsqrt(jnp.mean(t * t, axis=-1, keepdims=True) + 1e-06) * gain
        return (t * cosine + pltpu.roll(t, 64, 1) * sine).astype(BF)

    q_ref[:, :128] = head(raw[:, :128], qg_ref[...])
    q_ref[:, 128:] = head(raw[:, 128:256], qg_ref[...])
    keys = head(raw[:, 256:384], kg_ref[...])
    values = raw[:, 384:].astype(BF)
    kv_ref[0] = keys
    kv_ref[1] = values

    @pl.when(pl.program_id(0) >= 2)
    def _():
        tail_ref[0] = keys
        tail_ref[1] = values


def project(core, normed, own, oth, q_gain, key_gain, cs):
    rows = normed.shape[0]
    tile = 256
    fixed = lambda *shape: pl.BlockSpec(shape, lambda i, c: (0,) * len(shape))
    return pl.pallas_call(
        qkv_kernel,
        grid_spec=pltpu.PrefetchScalarGridSpec(
            num_scalar_prefetch=1,
            grid=(rows // tile,),
            in_specs=[
                pl.BlockSpec((tile, 2048), lambda i, c: (i, 0)),
                fixed(8, 512, 128),
                fixed(8, 512, 128),
                fixed(1, 128),
                fixed(1, 128),
                pl.BlockSpec((tile, 128), lambda i, c: (i, 0)),
            ],
            out_specs=[
                pl.BlockSpec((tile, 256), lambda i, c: (i, 0)),
                pl.BlockSpec((2, tile, 128), lambda i, c: (0, i, 0)),
                pl.BlockSpec((2, tile, 128), lambda i, c: (0, jnp.maximum(i - 2, 0), 0)),
            ],
            scratch_shapes=[pltpu.VMEM((2048, 512), BF)],
        ),
        out_shape=(
            jax.ShapeDtypeStruct((rows, 256), BF),
            jax.ShapeDtypeStruct((2, rows, 128), BF),
            jax.ShapeDtypeStruct((2, rows // 2, 128), BF),
        ),
        compiler_params=pltpu.CompilerParams(vmem_limit_bytes=40 << 20),
        name="qkv",
    )(core, normed, own, oth, q_gain[None], key_gain[None], cs)


def attend_kernel(q_ref, kv_ref, prior_ref, lo_ref, out_ref):
    factor = HEAD ** (-0.5) * math.log2(math.e)
    nt = (((1,), (1,)), ((), ()))
    for i in range(4):
        first = i * 256
        skip = 256 if i == 3 else 0
        count = first + 256
        lo = lo_ref[first : first + 256, :]
        row = lax.broadcasted_iota(jnp.int32, (256, count), 0) + first
        col = lax.broadcasted_iota(jnp.int32, (256, count), 1)
        near = (col >= lo) & (col <= row)
        prior_col = lax.broadcasted_iota(jnp.int32, (256, 512 - skip), 1) + (skip - 512)
        far = prior_col >= lo
        for h in range(2):
            q = q_ref[first : first + 256, h * 128 : h * 128 + 128]
            s1 = lax.dot_general(q, kv_ref[0, :count], nt, preferred_element_type=F32)
            s0 = lax.dot_general(q, prior_ref[0, skip:], nt, preferred_element_type=F32)
            s1 = jnp.where(near, s1, -1e30)
            s0 = jnp.where(far, s0, -1e30)
            top = jnp.maximum(jnp.max(s1, -1, keepdims=True), jnp.max(s0, -1, keepdims=True))
            e1 = jnp.exp2((s1 - top) * factor)
            e0 = jnp.exp2((s0 - top) * factor)
            inv = 1.0 / (jnp.sum(e1, -1, keepdims=True) + jnp.sum(e0, -1, keepdims=True))
            p1 = (e1 * inv).astype(BF)
            p0 = (e0 * inv).astype(BF)
            o = jnp.dot(p1, kv_ref[1, :count], preferred_element_type=F32)
            o = o + jnp.dot(p0, prior_ref[1, skip:], preferred_element_type=F32)
            o = o.astype(BF)
            for part in range(2):
                block = 2 * i + part
                out_ref[block % 4, block // 4, :, h * 128 : h * 128 + 128] = o[part * 128 : part * 128 + 128]


def attend(q, kv, prior, lo):
    return pl.pallas_call(
        attend_kernel,
        out_shape=jax.ShapeDtypeStruct((4, 2, 128, 256), BF),
        compiler_params=pltpu.CompilerParams(vmem_limit_bytes=40 << 20),
        name="attend",
    )(q, kv, prior, lo)


def out_kernel(at_ref, ctx_ref, own_ref, oth_ref, keep_ref, send_ref, w_ref, x_ref, sems):
    core = at_ref[0]
    xl = at_ref[1]

    def each(act):
        def step(n, carry):
            s, i = n // 8, lax.rem(n, 8)
            for which, (src, side) in enumerate(((own_ref, core), (oth_ref, 1 - core))):
                at = pl.ds(pl.multiple_of((2 * i + side) * 128, 128), 128)
                act(pltpu.make_async_copy(
                    src.at[s, i], w_ref.at[pl.ds(pl.multiple_of(s * 256, 256), 256), at], sems.at[which, s, i]
                ))
            return carry

        lax.fori_loop(0, 32, step, 0)

    each(lambda c: c.start())
    for s in range(4):
        x_ref[:128, s * 256 : s * 256 + 256] = ctx_ref[s, xl]
        x_ref[128:, s * 256 : s * 256 + 256] = ctx_ref[s, 1 - xl]
    each(lambda c: c.wait())
    x = x_ref[...]

    def column(n, carry):
        at = pl.ds(pl.multiple_of(n * 512, 512), 512)
        total = jnp.dot(x, w_ref[:, at], preferred_element_type=F32)
        keep_ref[:, at] = total[:128]
        send_ref[:, at] = total[128:].astype(BF)
        return carry

    lax.fori_loop(0, 4, column, 0)


def out_project(at, ctx, own, oth):
    vm = pl.BlockSpec(memory_space=pltpu.VMEM)
    anywhere = pl.BlockSpec(memory_space=pl.ANY)
    return pl.pallas_call(
        out_kernel,
        in_specs=[pl.BlockSpec(memory_space=pltpu.SMEM)] + [vm] + [anywhere] * 2,
        out_shape=(
            jax.ShapeDtypeStruct((128, 2048), F32),
            jax.ShapeDtypeStruct((128, 2048), BF),
        ),
        scratch_shapes=[
            pltpu.VMEM((1024, 2048), BF),
            pltpu.VMEM((256, 1024), BF),
            pltpu.SemaphoreType.DMA((2, 4, 8)),
        ],
        compiler_params=pltpu.CompilerParams(vmem_limit_bytes=40 << 20),
        name="oproj",
    )(at, ctx, own, oth)


def fetcher(own_ref, oth_ref, w_ref, sems, y, first):
    def copy(c, g, m):
        src = own_ref if c == 0 else oth_ref
        at = pl.multiple_of(((m // 4) * 4 + lax.rem(y + lax.rem(m, 4), 4)) * 256, 256)
        return pltpu.make_async_copy(
            src.at[:, m // 4, lax.rem(m, 4), first + g * 96 : first + g * 96 + 96, :],
            w_ref.at[g, c * 8 : c * 8 + 8, :, pl.ds(at, 256)],
            sems.at[g, c, m],
        )

    def each(c, groups, act):
        def step(m, carry):
            for g in range(groups):
                act(copy(c, g, m))
            return carry

        lax.fori_loop(0, 8, step, 0)

    return each


def gate_kernel(y_ref, x0_ref, x1_ref, x2_ref, x3_ref, x4_ref, src_ref, hid_ref, w_ref, x_ref, sems):
    nt = (((1,), (1,)), ((), ()))
    each = fetcher(src_ref, src_ref, w_ref, sems, y_ref[0], 0)
    each(0, 2, lambda c: c.start())
    x_ref[0:128] = x0_ref[...]
    x_ref[128:256] = x1_ref[...]
    x_ref[256:384] = x2_ref[...]
    x_ref[384:448] = x3_ref[...]
    x_ref[448:512] = x4_ref[...]
    x = x_ref[...]
    each(0, 2, lambda copy: copy.wait())
    gate_w = w_ref[0].reshape(768, 2048)
    up_w = w_ref[1].reshape(768, 2048)
    for t in range(3):
        gate = lax.dot_general(x, gate_w[t * 256 : t * 256 + 256], nt, preferred_element_type=F32)
        upper = lax.dot_general(x, up_w[t * 256 : t * 256 + 256], nt, preferred_element_type=F32)
        hidden = gate / (1.0 + jnp.exp(-gate)) * upper
        hid_ref[:, t * 256 : t * 256 + 256] = hidden.astype(BF)


def far_kernel(y_ref, hid0_ref, hid1_ref, own_ref, oth_ref, top_ref, bottom_ref, w_ref, sems):
    each = fetcher(own_ref, oth_ref, w_ref, sems, y_ref[0], 192)
    for c in range(2):
        each(c, 1, lambda copy: copy.start())
    for c in range(2):
        each(c, 1, lambda copy: copy.wait())
    hid = jnp.concatenate([hid0_ref[384:], hid1_ref[384:]], axis=1)

    def column(n, carry):
        at = pl.ds(pl.multiple_of(n * 512, 512), 512)
        out = jnp.dot(hid, w_ref[0, :, :, at].reshape(1536, 512), preferred_element_type=F32)
        top_ref[:, at] = out[:64].astype(BF)
        bottom_ref[:, at] = out[64:].astype(BF)
        return carry

    lax.fori_loop(0, 4, column, 0)


def down_kernel(hid0_ref, hid1_ref, w_ref, keep_ref, left_ref, right_ref):
    hid = jnp.concatenate([hid0_ref[:384], hid1_ref[:384]], axis=1)

    def column(n, carry):
        at = pl.ds(pl.multiple_of(n * 512, 512), 512)
        out = jnp.dot(hid, w_ref[0, :, :, at].reshape(1536, 512), preferred_element_type=F32)
        keep_ref[:, at] = out[:128]
        left_ref[:, at] = out[128:256].astype(BF)
        right_ref[:, at] = out[256:].astype(BF)
        return carry

    lax.fori_loop(0, 4, column, 0)


def gate_up(y, pieces, src):
    vm = pl.BlockSpec(memory_space=pltpu.VMEM)
    hbm = pl.BlockSpec(memory_space=pltpu.HBM)
    return pl.pallas_call(
        gate_kernel,
        in_specs=[pl.BlockSpec(memory_space=pltpu.SMEM)] + [vm] * 5 + [hbm],
        out_shape=jax.ShapeDtypeStruct((512, 768), BF),
        scratch_shapes=[
            pltpu.VMEM((2, 8, 96, 2048), BF),
            pltpu.VMEM((512, 2048), BF),
            pltpu.SemaphoreType.DMA((2, 1, 8)),
        ],
        compiler_params=pltpu.CompilerParams(vmem_limit_bytes=40 << 20),
        name="gate_up",
    )(y, *pieces, src)


def down_far(y, hidden, own, oth):
    vm = pl.BlockSpec(memory_space=pltpu.VMEM)
    hbm = pl.BlockSpec(memory_space=pltpu.HBM)
    half = jax.ShapeDtypeStruct((64, 2048), BF)
    return pl.pallas_call(
        far_kernel,
        in_specs=[pl.BlockSpec(memory_space=pltpu.SMEM), vm, vm] + [hbm] * 2,
        out_shape=(half, half, jax.ShapeDtypeStruct((1, 16, 96, 2048), BF)),
        scratch_shapes=[pltpu.SemaphoreType.DMA((1, 2, 8))],
        compiler_params=pltpu.CompilerParams(vmem_limit_bytes=40 << 20),
        name="down_far",
    )(y, *hidden, own, oth)


def down(hidden, weight):
    part = jax.ShapeDtypeStruct((128, 2048), BF)
    return pl.pallas_call(
        down_kernel,
        out_shape=(jax.ShapeDtypeStruct((128, 2048), F32), part, part),
        compiler_params=pltpu.CompilerParams(vmem_limit_bytes=40 << 20),
        name="down",
    )(*hidden, weight)


def pack_kernel(q_ref, k_ref, v_ref, o_ref, out_ref):
    parts = [q_ref[:, :128], q_ref[:, 128:], k_ref[...], v_ref[...], o_ref[...]]
    whole = jnp.concatenate(parts, axis=0).astype(BF)
    for i in range(8):
        out_ref[i] = whole


def pack(q, k, v, o):
    return pl.pallas_call(
        pack_kernel,
        out_shape=jax.ShapeDtypeStruct((8, 768, 128), BF),
        name="pack",
    )(q, k, v, o)


def prep_kernel(y_ref, gate_ref, up_ref, down_ref, p0_ref, p1_ref, p2_ref, p3_ref, g_ref, u_ref):
    g_ref[...] = gate_ref[...].T
    u_ref[...] = up_ref[...].T
    for k, out_ref in enumerate((p0_ref, p1_ref, p2_ref, p3_ref)):
        at = pl.ds(pl.multiple_of(lax.rem(y_ref[0] + k, 4) * 96, 96), 96)
        out_ref[:96] = g_ref[at, :].astype(BF)
        out_ref[96:192] = u_ref[at, :].astype(BF)
        out_ref[192:] = down_ref[at, :].astype(BF)


def prepare(y, gate, up, down):
    vm = pl.BlockSpec(memory_space=pltpu.VMEM)
    return pl.pallas_call(
        prep_kernel,
        in_specs=[pl.BlockSpec(memory_space=pltpu.SMEM)] + [vm] * 3,
        out_shape=[jax.ShapeDtypeStruct((288, 256), BF)] * 4,
        scratch_shapes=[pltpu.VMEM((384, 256), F32), pltpu.VMEM((384, 256), F32)],
        name="prep",
    )(y, gate, up, down)


def join_kernel(p0_ref, p1_ref, p2_ref, p3_ref, out_ref):
    for k, ref in enumerate((p0_ref, p1_ref, p2_ref, p3_ref)):
        out_ref[k] = ref[...]


def join(parts):
    return pl.pallas_call(join_kernel, out_shape=jax.ShapeDtypeStruct((4, 288, 256), BF), name="join")(*parts)


def trade(parts):
    return [parts[0]] + [lax.ppermute(parts[4 - k], "y", ring(4 - k)) for k in (1, 2, 3)]


def per_device(
    tokens,
    doc_ids,
    positions,
    attn_gain,
    mlp_gain,
    q_gain,
    key_norm_gain,
    q_weight,
    key_matrix,
    value_matrix,
    o_weight,
    gate_weight,
    up_weight,
    down_weight,
):
    rows = tokens.shape[0]
    core = lax.axis_index("core").astype(jnp.int32)
    xl = lax.axis_index("xl").astype(jnp.int32)
    y = lax.axis_index("y").astype(jnp.int32)
    hold = lax.optimization_barrier

    packed = pack(q_weight, key_matrix, value_matrix, o_weight)
    at_own = lax.all_to_all(packed, ("z", "xh"), split_axis=0, concat_axis=0, tiled=True)

    parts = trade(prepare(y[None], gate_weight, up_weight, down_weight))
    half = HEAD // 2
    freq = jnp.exp(jnp.arange(half, dtype=F32) * (-2.0 * math.log(1000000.0) / HEAD))
    angle = positions.astype(F32)[:, None] * freq[None, :]
    cs = jnp.concatenate([jnp.cos(angle), jnp.sin(angle)], axis=1)
    normed = normalise(tokens, attn_gain)
    cs, normed, at_own, *parts = hold((cs, normed, at_own, *parts))
    mlp_own = lax.all_gather(join(parts), ("z", "xh", "xl"), axis=0, tiled=False).reshape(8, 2, 4, 288, 256)
    lo = (jnp.arange(rows, dtype=jnp.int32) - positions)[:, None]

    at_oth = swap(at_own, "core")

    o_wide = jnp.broadcast_to(at_own[None, :, 512:], (4, 8, 256, 128))
    o_own = lax.all_to_all(o_wide, "y", split_axis=0, concat_axis=0, tiled=True)

    q, cache, tail = project(core[None], normed, at_own, at_oth, q_gain, key_norm_gain, cs)
    prior = lax.ppermute(tail, REQ, [(i - 1, i) for i in range(1, 16)])
    ctx = attend(q, cache, prior, lo)
    _, o_own = hold((ctx, o_own))
    o_oth = swap(o_own, "core")
    ctx = lax.all_to_all(ctx, "y", split_axis=0, concat_axis=0, tiled=True)
    keep, send = out_project(jnp.stack([core, xl]), ctx, o_own, o_oth)
    got = swap(send, "xl")

    own_rows = lax.dynamic_slice_in_dim(tokens, (xl * 4 + y) * 128, 128, 0).astype(F32)
    resid = (own_rows + (keep + got.astype(F32))).astype(BF)
    resid = hold(resid).astype(F32)
    scale = lax.rsqrt(jnp.mean(resid * resid, axis=-1, keepdims=True) + 1e-06)
    mlp_in = (resid * scale * mlp_gain).astype(BF)

    mlp_own, mlp_in = hold((mlp_own, mlp_in))
    mlp_oth = swap(mlp_own, "core")
    left = lax.ppermute(mlp_in, "y", ring(1))
    right = lax.ppermute(mlp_in, "y", ring(3))
    far_top = lax.ppermute(left[:64], "y", ring(1))
    far_bottom = lax.ppermute(right[64:], "y", ring(3))
    pieces = (mlp_in, left, right, far_top, far_bottom)
    mlp_own = pltpu.with_memory_space_constraint(mlp_own, pltpu.HBM)
    first = gate_up(y[None], pieces, mlp_own)
    first, mlp_oth = hold((first, mlp_oth))
    mlp_oth = pltpu.with_memory_space_constraint(mlp_oth, pltpu.HBM)
    hidden = (first, gate_up(y[None], pieces, mlp_oth))
    top, bottom, weight = down_far(y[None], hidden, mlp_own, mlp_oth)
    via_left = lax.ppermute(top, "y", ring(1))
    via_right = lax.ppermute(bottom, "y", ring(3))
    keep, to_left, to_right = down(hidden, weight)
    to_right = jnp.concatenate([(to_right[:64].astype(F32) + via_left.astype(F32)).astype(BF), to_right[64:]])
    to_left = jnp.concatenate([to_left[:64], (to_left[64:].astype(F32) + via_right.astype(F32)).astype(BF)])
    from_left = lax.ppermute(to_right, "y", ring(1))
    from_right = lax.ppermute(to_left, "y", ring(3))
    total = keep + from_left.astype(F32) + from_right.astype(F32)
    return ((resid + total).astype(BF), cache)


def solution(mesh):
    fine = Mesh(mesh.devices.reshape(4, 2, 2, 2, 4), REQ + MDL)
    rows = P(REQ)
    in_specs = (
        P(REQ, None),
        rows,
        rows,
        P(),
        P(),
        P(),
        P(),
        P(REQ, MDL),
        P(REQ, MDL),
        P(REQ, MDL),
        P(MDL, REQ),
        P(MDL, REQ),
        P(MDL, REQ),
        P(REQ, MDL),
    )
    out_specs = (P(REQ + MDL, None), P(None, REQ, MDL))
    return jax.shard_map(per_device, mesh=fine, in_specs=in_specs, out_specs=out_specs, check_vma=False)
```

```python
import math

import jax
import jax.numpy as jnp
from jax import lax
from jax.experimental import pallas as pl
from jax.experimental.pallas import tpu as pltpu
from jax.sharding import Mesh
from jax.sharding import PartitionSpec as P

HEAD = 128
BF = jnp.bfloat16
F32 = jnp.float32
REQ = ("z", "xh", "core")
MDL = ("xl", "y")


def ring(step):
    return [(i, (i + step) % 4) for i in range(4)]


def swap(block, axis):
    return lax.ppermute(block, axis, [(0, 1), (1, 0)])


def norm_kernel(x_ref, gain_ref, out_ref):
    x = x_ref[...].astype(F32)
    scale = lax.rsqrt(jnp.mean(x * x, axis=-1, keepdims=True) + 1e-06)
    out_ref[...] = (x * scale * gain_ref[...]).astype(BF)


def normalise(x, gain):
    rows, tile = x.shape[0], min(256, x.shape[0])
    block = pl.BlockSpec((tile, 2048), lambda i: (i, 0))
    return pl.pallas_call(
        norm_kernel,
        grid=(rows // tile,),
        in_specs=[block, pl.BlockSpec((1, 2048), lambda i: (0, 0))],
        out_specs=block,
        out_shape=jax.ShapeDtypeStruct(x.shape, BF),
        name="norm",
    )(x, gain[None])


def qkv_kernel(core_ref, x_ref, own_ref, oth_ref, qg_ref, kg_ref, cs_ref, q_ref, kv_ref, tail_ref, w_ref):
    core = core_ref[0]

    @pl.when(pl.program_id(0) == 0)
    def _():
        def place(i, carry):
            for src, side in ((own_ref, core), (oth_ref, 1 - core)):
                at = pl.ds(pl.multiple_of((2 * i + side) * 128, 128), 128)
                for k in range(4):
                    w_ref[at, k * 128 : k * 128 + 128] = src[i, k * 128 : k * 128 + 128]
            return carry

        lax.fori_loop(0, 8, place, 0)

    raw = jnp.dot(x_ref[...], w_ref[...], preferred_element_type=F32)
    cs = cs_ref[...]
    turned = pltpu.roll(cs, 64, 1)
    low = lax.broadcasted_iota(jnp.int32, cs.shape, 1) < 64
    cosine = jnp.where(low, cs, turned)
    sine = jnp.where(low, -turned, cs)

    def head(t, gain):
        t = t * lax.rsqrt(jnp.mean(t * t, axis=-1, keepdims=True) + 1e-06) * gain
        return (t * cosine + pltpu.roll(t, 64, 1) * sine).astype(BF)

    q_ref[:, :128] = head(raw[:, :128], qg_ref[...])
    q_ref[:, 128:] = head(raw[:, 128:256], qg_ref[...])
    keys = head(raw[:, 256:384], kg_ref[...])
    values = raw[:, 384:].astype(BF)
    kv_ref[0] = keys
    kv_ref[1] = values

    @pl.when(pl.program_id(0) >= 2)
    def _():
        tail_ref[0] = keys
        tail_ref[1] = values


def project(core, normed, own, oth, q_gain, key_gain, cs):
    rows = normed.shape[0]
    tile = 256
    fixed = lambda *shape: pl.BlockSpec(shape, lambda i, c: (0,) * len(shape))
    return pl.pallas_call(
        qkv_kernel,
        grid_spec=pltpu.PrefetchScalarGridSpec(
            num_scalar_prefetch=1,
            grid=(rows // tile,),
            in_specs=[
                pl.BlockSpec((tile, 2048), lambda i, c: (i, 0)),
                fixed(8, 512, 128),
                fixed(8, 512, 128),
                fixed(1, 128),
                fixed(1, 128),
                pl.BlockSpec((tile, 128), lambda i, c: (i, 0)),
            ],
            out_specs=[
                pl.BlockSpec((tile, 256), lambda i, c: (i, 0)),
                pl.BlockSpec((2, tile, 128), lambda i, c: (0, i, 0)),
                pl.BlockSpec((2, tile, 128), lambda i, c: (0, jnp.maximum(i - 2, 0), 0)),
            ],
            scratch_shapes=[pltpu.VMEM((2048, 512), BF)],
        ),
        out_shape=(
            jax.ShapeDtypeStruct((rows, 256), BF),
            jax.ShapeDtypeStruct((2, rows, 128), BF),
            jax.ShapeDtypeStruct((2, rows // 2, 128), BF),
        ),
        compiler_params=pltpu.CompilerParams(vmem_limit_bytes=40 << 20),
        name="qkv",
    )(core, normed, own, oth, q_gain[None], key_gain[None], cs)


def attend_kernel(half_ref, q_ref, kv_ref, prior_ref, lo_ref, out_ref):
    factor = HEAD ** (-0.5) * math.log2(math.e)
    nt = (((1,), (1,)), ((), ()))

    def block(i):
        first = i * 256
        skip = 256 if i == 3 else 0
        count = first + 256
        lo = lo_ref[first : first + 256, :]
        row = lax.broadcasted_iota(jnp.int32, (256, count), 0) + first
        col = lax.broadcasted_iota(jnp.int32, (256, count), 1)
        near = (col >= lo) & (col <= row)
        prior_col = lax.broadcasted_iota(jnp.int32, (256, 512 - skip), 1) + (skip - 512)
        far = prior_col >= lo

        def head(h, carry):
            lanes = pl.ds(pl.multiple_of(h * 128, 128), 128)
            q = q_ref[first : first + 256, lanes]
            s1 = lax.dot_general(q, kv_ref[0, :count], nt, preferred_element_type=F32)
            s0 = lax.dot_general(q, prior_ref[0, skip:], nt, preferred_element_type=F32)
            s1 = jnp.where(near, s1, -1e30)
            s0 = jnp.where(far, s0, -1e30)
            top = jnp.maximum(jnp.max(s1, -1, keepdims=True), jnp.max(s0, -1, keepdims=True))
            e1 = jnp.exp2((s1 - top) * factor)
            e0 = jnp.exp2((s0 - top) * factor)
            inv = 1.0 / (jnp.sum(e1, -1, keepdims=True) + jnp.sum(e0, -1, keepdims=True))
            p1 = (e1 * inv).astype(BF)
            p0 = (e0 * inv).astype(BF)
            o = jnp.dot(p1, kv_ref[1, :count], preferred_element_type=F32)
            o = o + jnp.dot(p0, prior_ref[1, skip:], preferred_element_type=F32)
            o = o.astype(BF)
            for part in range(2):
                out_ref[(2 * i + part) % 4, :, lanes] = o[part * 128 : part * 128 + 128]
            return carry

        lax.fori_loop(0, 2, head, 0)

    @pl.when(half_ref[0] == 0)
    def _():
        block(0)
        block(1)

    @pl.when(half_ref[0] == 1)
    def _():
        block(2)
        block(3)


def attend(half, q, kv, prior, lo):
    vm = pl.BlockSpec(memory_space=pltpu.VMEM)
    return pl.pallas_call(
        attend_kernel,
        in_specs=[pl.BlockSpec(memory_space=pltpu.SMEM)] + [vm] * 4,
        out_shape=jax.ShapeDtypeStruct((4, 128, 256), BF),
        compiler_params=pltpu.CompilerParams(vmem_limit_bytes=40 << 20),
        name="attend",
    )(half, q, kv, prior, lo)


def out_columns(y, ctx_ref, w_ref, out_ref):
    x = jnp.concatenate([ctx_ref[lax.rem(y + k, 4)] for k in range(4)], axis=1)

    def column(n, carry):
        at = pl.ds(pl.multiple_of(n * 512, 512), 512)
        out_ref[:, at] = jnp.dot(x, w_ref[:, at], preferred_element_type=F32).astype(out_ref.dtype)
        return carry

    lax.fori_loop(0, 4, column, 0)


def out_first_kernel(at_ref, ctx_ref, *refs):
    pieces, (send_ref, w_ref, sems) = refs[:10], refs[10:]
    core = at_ref[0]

    def each(act):
        for n, (s, first, count, offset) in enumerate(
            ((0, 0, 8, 512), (1, 0, 8, 0), (2, 0, 4, 0), (2, 4, 4, 0), (3, 0, 8, 0))
        ):
            def step(i, carry, n=n, s=s, first=first, offset=offset):
                for side in range(2):
                    column = 2 * (first + i) + (core if side == 0 else 1 - core)
                    act(pltpu.make_async_copy(
                        pieces[2 * n + side].at[i, offset : offset + 256],
                        w_ref.at[s * 256 : s * 256 + 256, pl.ds(pl.multiple_of(column * 128, 128), 128)],
                        sems.at[side, s, first + i],
                    ))
                return carry

            lax.fori_loop(0, count, step, 0)

    each(lambda c: c.start())
    each(lambda c: c.wait())
    out_columns(at_ref[1], ctx_ref, w_ref, send_ref)


def out_second_kernel(at_ref, ctx_ref, w_ref, keep_ref):
    out_columns(at_ref[1], ctx_ref, w_ref, keep_ref)


def out_first(at, ctx, pieces):
    return pl.pallas_call(
        out_first_kernel,
        in_specs=[
            pl.BlockSpec(memory_space=pltpu.SMEM),
            pl.BlockSpec(memory_space=pltpu.VMEM),
            *[pl.BlockSpec(memory_space=pl.ANY)] * 10,
        ],
        out_shape=(jax.ShapeDtypeStruct((128, 2048), BF), jax.ShapeDtypeStruct((1024, 2048), BF)),
        scratch_shapes=[pltpu.SemaphoreType.DMA((2, 4, 8))],
        compiler_params=pltpu.CompilerParams(vmem_limit_bytes=40 << 20),
        name="out_first",
    )(at, ctx, *pieces)


def out_second(at, ctx, weight):
    vm = pl.BlockSpec(memory_space=pltpu.VMEM)
    return pl.pallas_call(
        out_second_kernel,
        in_specs=[pl.BlockSpec(memory_space=pltpu.SMEM), vm, vm],
        out_shape=jax.ShapeDtypeStruct((128, 2048), F32),
        compiler_params=pltpu.CompilerParams(vmem_limit_bytes=40 << 20),
        name="out_second",
    )(at, ctx, weight)


def fetcher(own_ref, oth_ref, w_ref, sems, y, first):
    def copy(c, g, m):
        src = own_ref if c == 0 else oth_ref
        at = pl.multiple_of(((m // 4) * 4 + lax.rem(y + lax.rem(m, 4), 4)) * 256, 256)
        return pltpu.make_async_copy(
            src.at[:, m // 4, lax.rem(m, 4), first + g * 96 : first + g * 96 + 96, :],
            w_ref.at[g, c * 8 : c * 8 + 8, :, pl.ds(at, 256)],
            sems.at[g, c, m],
        )

    def each(c, groups, act):
        def step(m, carry):
            for g in range(groups):
                act(copy(c, g, m))
            return carry

        lax.fori_loop(0, 8, step, 0)

    return each


def gate_kernel(y_ref, x0_ref, x1_ref, x2_ref, x3_ref, x4_ref, own_ref, oth_ref, hid_ref, w_ref, x_ref, sems):
    nt = (((1,), (1,)), ((), ()))
    each = fetcher(own_ref, oth_ref, w_ref, sems, y_ref[0], 0)
    each(0, 2, lambda c: c.start())
    each(1, 2, lambda c: c.start())
    x_ref[0:128] = x0_ref[...]
    x_ref[128:256] = x1_ref[...]
    x_ref[256:384] = x2_ref[...]
    x_ref[384:448] = x3_ref[...]
    x_ref[448:512] = x4_ref[...]
    x = x_ref[...]

    for c in range(2):
        each(c, 2, lambda copy: copy.wait())
        gate_w = w_ref[0, c * 8 : c * 8 + 8].reshape(768, 2048)
        up_w = w_ref[1, c * 8 : c * 8 + 8].reshape(768, 2048)
        for t in range(3):
            gate = lax.dot_general(x, gate_w[t * 256 : t * 256 + 256], nt, preferred_element_type=F32)
            upper = lax.dot_general(x, up_w[t * 256 : t * 256 + 256], nt, preferred_element_type=F32)
            hidden = gate / (1.0 + jnp.exp(-gate)) * upper
            at = c * 768 + t * 256
            hid_ref[:, at : at + 256] = hidden.astype(BF)


def far_kernel(y_ref, hid_ref, own_ref, oth_ref, top_ref, bottom_ref, w_ref, sems):
    each = fetcher(own_ref, oth_ref, w_ref, sems, y_ref[0], 192)
    for c in range(2):
        each(c, 1, lambda copy: copy.start())
    for c in range(2):
        each(c, 1, lambda copy: copy.wait())
    hid = hid_ref[384:]

    def column(n, carry):
        at = pl.ds(pl.multiple_of(n * 512, 512), 512)
        out = jnp.dot(hid, w_ref[0, :, :, at].reshape(1536, 512), preferred_element_type=F32)
        top_ref[:, at] = out[:64].astype(BF)
        bottom_ref[:, at] = out[64:].astype(BF)
        return carry

    lax.fori_loop(0, 4, column, 0)


def down_kernel(hid_ref, w_ref, keep_ref, left_ref, right_ref):
    hid = hid_ref[:384]

    def column(n, carry):
        at = pl.ds(pl.multiple_of(n * 512, 512), 512)
        out = jnp.dot(hid, w_ref[0, :, :, at].reshape(1536, 512), preferred_element_type=F32)
        keep_ref[:, at] = out[:128]
        left_ref[:, at] = out[128:256].astype(BF)
        right_ref[:, at] = out[256:].astype(BF)
        return carry

    lax.fori_loop(0, 4, column, 0)


def gate_up(y, pieces, own, oth):
    vm = pl.BlockSpec(memory_space=pltpu.VMEM)
    hbm = pl.BlockSpec(memory_space=pltpu.HBM)
    return pl.pallas_call(
        gate_kernel,
        in_specs=[pl.BlockSpec(memory_space=pltpu.SMEM)] + [vm] * 5 + [hbm] * 2,
        out_shape=jax.ShapeDtypeStruct((512, 1536), BF),
        scratch_shapes=[
            pltpu.VMEM((2, 16, 96, 2048), BF),
            pltpu.VMEM((512, 2048), BF),
            pltpu.SemaphoreType.DMA((2, 2, 8)),
        ],
        compiler_params=pltpu.CompilerParams(vmem_limit_bytes=40 << 20),
        name="gate_up",
    )(y, *pieces, own, oth)


def down_far(y, hidden, own, oth):
    vm = pl.BlockSpec(memory_space=pltpu.VMEM)
    hbm = pl.BlockSpec(memory_space=pltpu.HBM)
    half = jax.ShapeDtypeStruct((64, 2048), BF)
    return pl.pallas_call(
        far_kernel,
        in_specs=[pl.BlockSpec(memory_space=pltpu.SMEM), vm] + [hbm] * 2,
        out_shape=(half, half, jax.ShapeDtypeStruct((1, 16, 96, 2048), BF)),
        scratch_shapes=[pltpu.SemaphoreType.DMA((1, 2, 8))],
        compiler_params=pltpu.CompilerParams(vmem_limit_bytes=40 << 20),
        name="down_far",
    )(y, hidden, own, oth)


def down(hidden, weight):
    part = jax.ShapeDtypeStruct((128, 2048), BF)
    return pl.pallas_call(
        down_kernel,
        out_shape=(jax.ShapeDtypeStruct((128, 2048), F32), part, part),
        compiler_params=pltpu.CompilerParams(vmem_limit_bytes=40 << 20),
        name="down",
    )(hidden, weight)


def pack_kernel(q_ref, k_ref, v_ref, o_ref, out_ref):
    parts = [q_ref[:, :128], q_ref[:, 128:], k_ref[...], v_ref[...], o_ref[...]]
    whole = jnp.concatenate(parts, axis=0).astype(BF)
    for i in range(8):
        out_ref[i] = whole


def pack(q, k, v, o):
    return pl.pallas_call(
        pack_kernel,
        out_shape=jax.ShapeDtypeStruct((8, 768, 128), BF),
        name="pack",
    )(q, k, v, o)


def prep_kernel(y_ref, gate_ref, up_ref, down_ref, p0_ref, p1_ref, p2_ref, p3_ref, g_ref, u_ref):
    g_ref[...] = gate_ref[...].T
    u_ref[...] = up_ref[...].T
    for k, out_ref in enumerate((p0_ref, p1_ref, p2_ref, p3_ref)):
        at = pl.ds(pl.multiple_of(lax.rem(y_ref[0] + k, 4) * 96, 96), 96)
        out_ref[:96] = g_ref[at, :].astype(BF)
        out_ref[96:192] = u_ref[at, :].astype(BF)
        out_ref[192:] = down_ref[at, :].astype(BF)


def prepare(y, gate, up, down):
    vm = pl.BlockSpec(memory_space=pltpu.VMEM)
    return pl.pallas_call(
        prep_kernel,
        in_specs=[pl.BlockSpec(memory_space=pltpu.SMEM)] + [vm] * 3,
        out_shape=[jax.ShapeDtypeStruct((288, 256), BF)] * 4,
        scratch_shapes=[pltpu.VMEM((384, 256), F32), pltpu.VMEM((384, 256), F32)],
        name="prep",
    )(y, gate, up, down)


def join_kernel(p0_ref, p1_ref, p2_ref, p3_ref, out_ref):
    for k, ref in enumerate((p0_ref, p1_ref, p2_ref, p3_ref)):
        out_ref[k] = ref[...]


def join(parts):
    return pl.pallas_call(join_kernel, out_shape=jax.ShapeDtypeStruct((4, 288, 256), BF), name="join")(*parts)


def trade(parts):
    return [parts[0]] + [lax.ppermute(parts[4 - k], "y", ring(4 - k)) for k in (1, 2, 3)]


def per_device(
    tokens,
    doc_ids,
    positions,
    attn_gain,
    mlp_gain,
    q_gain,
    key_norm_gain,
    q_weight,
    key_matrix,
    value_matrix,
    o_weight,
    gate_weight,
    up_weight,
    down_weight,
):
    rows = tokens.shape[0]
    core = lax.axis_index("core").astype(jnp.int32)
    xl = lax.axis_index("xl").astype(jnp.int32)
    y = lax.axis_index("y").astype(jnp.int32)
    hold = lax.optimization_barrier

    packed = pack(q_weight, key_matrix, value_matrix, o_weight)
    at_own = lax.all_to_all(packed, ("z", "xh"), split_axis=0, concat_axis=0, tiled=True)

    parts = trade(prepare(y[None], gate_weight, up_weight, down_weight))
    half = HEAD // 2
    freq = jnp.exp(jnp.arange(half, dtype=F32) * (-2.0 * math.log(1000000.0) / HEAD))
    angle = positions.astype(F32)[:, None] * freq[None, :]
    cs = jnp.concatenate([jnp.cos(angle), jnp.sin(angle)], axis=1)
    normed = normalise(tokens, attn_gain)
    cs, normed, at_own, *parts = hold((cs, normed, at_own, *parts))
    mlp_own = lax.all_gather(join(parts), ("z", "xh", "xl"), axis=0, tiled=False).reshape(8, 2, 4, 288, 256)
    lo = (jnp.arange(rows, dtype=jnp.int32) - positions)[:, None]

    at_oth = swap(at_own, "core")

    o_here = at_own[:, 512:]
    o_up = lax.ppermute(o_here, "y", ring(3))
    o_down = lax.ppermute(o_here, "y", ring(1))
    q, cache, tail = project(core[None], normed, at_own, at_oth, q_gain, key_norm_gain, cs)
    prior = lax.ppermute(tail, REQ, [(i - 1, i) for i in range(1, 16)])
    _, o_up, o_down = hold((prior, o_up, o_down))
    o_far = [lax.ppermute(o_up[:4], "y", ring(3)), lax.ppermute(o_down[4:], "y", ring(1))]
    turn = lambda part: lax.all_to_all(part, "y", split_axis=0, concat_axis=0, tiled=True)
    at = jnp.stack([core, y])
    theirs = attend(1 - xl[None], q, cache, prior, lo)
    _, q, *rest = hold((theirs, q, o_up, *o_far, o_down))
    pieces = [at_own, at_oth]
    for piece in rest:
        pieces += [piece, swap(piece, "core")]
    mine = attend(xl[None], q, cache, prior, lo)
    send, o_whole = out_first(at, turn(theirs), pieces)
    got = swap(send, "xl")
    keep = out_second(at, turn(mine), o_whole)

    own_rows = lax.dynamic_slice_in_dim(tokens, (xl * 4 + y) * 128, 128, 0).astype(F32)
    resid = (own_rows + (keep + got.astype(F32))).astype(BF)
    resid = hold(resid).astype(F32)
    scale = lax.rsqrt(jnp.mean(resid * resid, axis=-1, keepdims=True) + 1e-06)
    mlp_in = (resid * scale * mlp_gain).astype(BF)

    left = lax.ppermute(mlp_in, "y", ring(1))
    right = lax.ppermute(mlp_in, "y", ring(3))
    mlp_own, left, right = hold((mlp_own, left, right))
    mlp_oth = swap(mlp_own, "core")
    far_top = lax.ppermute(left[:64], "y", ring(1))
    far_bottom = lax.ppermute(right[64:], "y", ring(3))
    mlp_own = pltpu.with_memory_space_constraint(mlp_own, pltpu.HBM)
    hidden = gate_up(y[None], (mlp_in, left, right, far_top, far_bottom), mlp_own, mlp_oth)
    top, bottom, weight = down_far(y[None], hidden, mlp_own, mlp_oth)
    via_left = lax.ppermute(top, "y", ring(1))
    via_right = lax.ppermute(bottom, "y", ring(3))
    keep, to_left, to_right = down(hidden, weight)
    to_right = jnp.concatenate([(to_right[:64].astype(F32) + via_left.astype(F32)).astype(BF), to_right[64:]])
    to_left = jnp.concatenate([to_left[:64], (to_left[64:].astype(F32) + via_right.astype(F32)).astype(BF)])
    from_left = lax.ppermute(to_right, "y", ring(1))
    from_right = lax.ppermute(to_left, "y", ring(3))
    total = keep + from_left.astype(F32) + from_right.astype(F32)
    return ((resid + total).astype(BF), cache)


def solution(mesh):
    fine = Mesh(mesh.devices.reshape(4, 2, 2, 2, 4), REQ + MDL)
    rows = P(REQ)
    in_specs = (
        P(REQ, None),
        rows,
        rows,
        P(),
        P(),
        P(),
        P(),
        P(REQ, MDL),
        P(REQ, MDL),
        P(REQ, MDL),
        P(MDL, REQ),
        P(MDL, REQ),
        P(MDL, REQ),
        P(REQ, MDL),
    )
    out_specs = (P(REQ + MDL, None), P(None, REQ, MDL))
    return jax.shard_map(per_device, mesh=fine, in_specs=in_specs, out_specs=out_specs, check_vma=False)
```

```python
import math

import jax
import jax.numpy as jnp
from jax import lax
from jax.experimental import pallas as pl
from jax.experimental.pallas import tpu as pltpu
from jax.sharding import Mesh
from jax.sharding import PartitionSpec as P

HEAD = 128
BF = jnp.bfloat16
F32 = jnp.float32
REQ = ("z", "xh", "core")
MDL = ("xl", "y")


def ring(step):
    return [(i, (i + step) % 4) for i in range(4)]


def swap(block, axis):
    return lax.ppermute(block, axis, [(0, 1), (1, 0)])


def qkv_kernel(core_ref, x_ref, own_ref, oth_ref, gain_ref, qg_ref, kg_ref, cs_ref, q_ref, kv_ref, tail_ref, w_ref):
    core = core_ref[0]

    @pl.when(pl.program_id(0) == 0)
    def _():
        def place(i, carry):
            for src, side in ((own_ref, core), (oth_ref, 1 - core)):
                at = pl.ds(pl.multiple_of((2 * i + side) * 128, 128), 128)
                for k in range(4):
                    w_ref[at, k * 128 : k * 128 + 128] = src[i, k * 128 : k * 128 + 128]
            return carry

        lax.fori_loop(0, 8, place, 0)

    x = x_ref[...].astype(F32)
    scale = lax.rsqrt(jnp.mean(x * x, axis=-1, keepdims=True) + 1e-06)
    normed = (x * scale * gain_ref[...]).astype(BF)
    raw = jnp.dot(normed, w_ref[...], preferred_element_type=F32)
    cs = cs_ref[...]
    turned = pltpu.roll(cs, 64, 1)
    low = lax.broadcasted_iota(jnp.int32, cs.shape, 1) < 64
    cosine = jnp.where(low, cs, turned)
    sine = jnp.where(low, -turned, cs)

    def head(t, gain):
        t = t * lax.rsqrt(jnp.mean(t * t, axis=-1, keepdims=True) + 1e-06) * gain
        return (t * cosine + pltpu.roll(t, 64, 1) * sine).astype(BF)

    q_ref[:, :128] = head(raw[:, :128], qg_ref[...])
    q_ref[:, 128:] = head(raw[:, 128:256], qg_ref[...])
    keys = head(raw[:, 256:384], kg_ref[...])
    values = raw[:, 384:].astype(BF)
    kv_ref[0] = keys
    kv_ref[1] = values

    @pl.when(pl.program_id(0) >= 2)
    def _():
        tail_ref[0] = keys
        tail_ref[1] = values


def project(core, tokens, own, oth, attn_gain, q_gain, key_gain, cs):
    rows = tokens.shape[0]
    tile = 256
    fixed = lambda *shape: pl.BlockSpec(shape, lambda i, c: (0,) * len(shape))
    return pl.pallas_call(
        qkv_kernel,
        grid_spec=pltpu.PrefetchScalarGridSpec(
            num_scalar_prefetch=1,
            grid=(rows // tile,),
            in_specs=[
                pl.BlockSpec((tile, 2048), lambda i, c: (i, 0)),
                fixed(8, 512, 128),
                fixed(8, 512, 128),
                fixed(1, 2048),
                fixed(1, 128),
                fixed(1, 128),
                pl.BlockSpec((tile, 128), lambda i, c: (i, 0)),
            ],
            out_specs=[
                pl.BlockSpec((tile, 256), lambda i, c: (i, 0)),
                pl.BlockSpec((2, tile, 128), lambda i, c: (0, i, 0)),
                pl.BlockSpec((2, tile, 128), lambda i, c: (0, jnp.maximum(i - 2, 0), 0)),
            ],
            scratch_shapes=[pltpu.VMEM((2048, 512), BF)],
        ),
        out_shape=(
            jax.ShapeDtypeStruct((rows, 256), BF),
            jax.ShapeDtypeStruct((2, rows, 128), BF),
            jax.ShapeDtypeStruct((2, rows // 2, 128), BF),
        ),
        compiler_params=pltpu.CompilerParams(vmem_limit_bytes=40 << 20),
        name="qkv",
    )(core, tokens, own, oth, attn_gain[None], q_gain[None], key_gain[None], cs)


def attend_kernel(q_ref, kv_ref, prior_ref, lo_ref, out_ref):
    factor = HEAD ** (-0.5) * math.log2(math.e)
    nt = (((1,), (1,)), ((), ()))
    for i in range(4):
        first = i * 256
        skip = 256 if i == 3 else 0
        count = first + 256
        lo = lo_ref[first : first + 256, :]
        row = lax.broadcasted_iota(jnp.int32, (256, count), 0) + first
        col = lax.broadcasted_iota(jnp.int32, (256, count), 1)
        near = (col >= lo) & (col <= row)
        prior_col = lax.broadcasted_iota(jnp.int32, (256, 512 - skip), 1) + (skip - 512)
        far = prior_col >= lo
        for h in range(2):
            q = q_ref[first : first + 256, h * 128 : h * 128 + 128]
            s1 = lax.dot_general(q, kv_ref[0, :count], nt, preferred_element_type=F32)
            s0 = lax.dot_general(q, prior_ref[0, skip:], nt, preferred_element_type=F32)
            s1 = jnp.where(near, s1, -1e30)
            s0 = jnp.where(far, s0, -1e30)
            top = jnp.maximum(jnp.max(s1, -1, keepdims=True), jnp.max(s0, -1, keepdims=True))
            e1 = jnp.exp2((s1 - top) * factor)
            e0 = jnp.exp2((s0 - top) * factor)
            inv = 1.0 / (jnp.sum(e1, -1, keepdims=True) + jnp.sum(e0, -1, keepdims=True))
            p1 = (e1 * inv).astype(BF)
            p0 = (e0 * inv).astype(BF)
            o = jnp.dot(p1, kv_ref[1, :count], preferred_element_type=F32)
            o = o + jnp.dot(p0, prior_ref[1, skip:], preferred_element_type=F32)
            o = o.astype(BF)
            for part in range(2):
                block = 2 * i + part
                out_ref[block % 4, block // 4, :, h * 128 : h * 128 + 128] = o[part * 128 : part * 128 + 128]


def attend(q, kv, prior, lo):
    return pl.pallas_call(
        attend_kernel,
        out_shape=jax.ShapeDtypeStruct((4, 2, 128, 256), BF),
        compiler_params=pltpu.CompilerParams(vmem_limit_bytes=40 << 20),
        name="attend",
    )(q, kv, prior, lo)


def out_kernel(at_ref, ctx_ref, own_ref, oth_ref, keep_ref, send_ref, w_ref, x_ref, sems):
    core = at_ref[0]
    xl = at_ref[1]

    def each(act):
        def step(n, carry):
            s, i = n // 8, lax.rem(n, 8)
            for which, (src, side) in enumerate(((own_ref, core), (oth_ref, 1 - core))):
                at = pl.ds(pl.multiple_of((2 * i + side) * 128, 128), 128)
                act(pltpu.make_async_copy(
                    src.at[s, i], w_ref.at[pl.ds(pl.multiple_of(s * 256, 256), 256), at], sems.at[which, s, i]
                ))
            return carry

        lax.fori_loop(0, 32, step, 0)

    each(lambda c: c.start())
    for s in range(4):
        x_ref[:128, s * 256 : s * 256 + 256] = ctx_ref[s, xl]
        x_ref[128:, s * 256 : s * 256 + 256] = ctx_ref[s, 1 - xl]
    each(lambda c: c.wait())
    x = x_ref[...]

    def column(n, carry):
        at = pl.ds(pl.multiple_of(n * 512, 512), 512)
        total = jnp.dot(x, w_ref[:, at], preferred_element_type=F32)
        keep_ref[:, at] = total[:128]
        send_ref[:, at] = total[128:].astype(BF)
        return carry

    lax.fori_loop(0, 4, column, 0)


def out_project(at, ctx, own, oth):
    vm = pl.BlockSpec(memory_space=pltpu.VMEM)
    anywhere = pl.BlockSpec(memory_space=pl.ANY)
    return pl.pallas_call(
        out_kernel,
        in_specs=[pl.BlockSpec(memory_space=pltpu.SMEM)] + [vm] + [anywhere] * 2,
        out_shape=(
            jax.ShapeDtypeStruct((128, 2048), F32),
            jax.ShapeDtypeStruct((128, 2048), BF),
        ),
        scratch_shapes=[
            pltpu.VMEM((1024, 2048), BF),
            pltpu.VMEM((256, 1024), BF),
            pltpu.SemaphoreType.DMA((2, 4, 8)),
        ],
        compiler_params=pltpu.CompilerParams(vmem_limit_bytes=40 << 20),
        name="oproj",
    )(at, ctx, own, oth)


def mid_kernel(m_ref, x_ref, keep_ref, got_ref, gain_ref, resid_ref, top_ref, bottom_ref):
    resid = (x_ref[...].astype(F32) + (keep_ref[...] + got_ref[...].astype(F32))).astype(BF)
    resid_ref[...] = resid
    wide = resid.astype(F32)
    scale = lax.rsqrt(jnp.mean(wide * wide, axis=-1, keepdims=True) + 1e-06)
    normed = (wide * scale * gain_ref[...]).astype(BF)
    top_ref[...] = normed[:64]
    bottom_ref[...] = normed[64:]


def middle(m, tokens, keep, got, gain):
    whole = lambda *shape: pl.BlockSpec(shape, lambda i, m: (0,) * len(shape))
    return pl.pallas_call(
        mid_kernel,
        grid_spec=pltpu.PrefetchScalarGridSpec(
            num_scalar_prefetch=1,
            grid=(1,),
            in_specs=[
                pl.BlockSpec((128, 2048), lambda i, m: (m[0], 0)),
                whole(128, 2048),
                whole(128, 2048),
                whole(1, 2048),
            ],
            out_specs=[whole(128, 2048), whole(64, 2048), whole(64, 2048)],
        ),
        out_shape=(
            jax.ShapeDtypeStruct((128, 2048), BF),
            jax.ShapeDtypeStruct((64, 2048), BF),
            jax.ShapeDtypeStruct((64, 2048), BF),
        ),
        name="mid",
    )(m, tokens, keep, got, gain[None])


def last_kernel(resid_ref, keep_ref, lt_ref, lb_ref, rt_ref, rb_ref, out_ref):
    for at, left, right in ((slice(0, 64), lt_ref, rt_ref), (slice(64, 128), lb_ref, rb_ref)):
        total = keep_ref[at] + left[...].astype(F32) + right[...].astype(F32)
        out_ref[at] = (resid_ref[at].astype(F32) + total).astype(BF)


def fetcher(src_ref, w_ref, sems, y, first):
    def copy(g, m):
        at = pl.multiple_of(((m // 4) * 4 + lax.rem(y + lax.rem(m, 4), 4)) * 256, 256)
        row = (first + g) * 96
        return pltpu.make_async_copy(
            src_ref.at[:, m // 4, lax.rem(m, 4), row : row + 96, :],
            w_ref.at[g, :, :, pl.ds(at, 256)],
            sems.at[g, m],
        )

    def each(groups, act):
        def step(m, carry):
            for g in groups:
                act(copy(g, m))
            return carry

        lax.fori_loop(0, 8, step, 0)

    return each


def load_kernel(y_ref, src_ref, w_ref, sems):
    each = fetcher(src_ref, w_ref, sems, y_ref[0], 0)
    each(range(3), lambda copy: copy.start())
    each(range(3), lambda copy: copy.wait())


def load(y, src):
    return pl.pallas_call(
        load_kernel,
        in_specs=[pl.BlockSpec(memory_space=pltpu.SMEM), pl.BlockSpec(memory_space=pltpu.HBM)],
        out_shape=jax.ShapeDtypeStruct((3, 8, 96, 2048), BF),
        scratch_shapes=[pltpu.SemaphoreType.DMA((3, 8))],
        compiler_params=pltpu.CompilerParams(vmem_limit_bytes=40 << 20),
        name="load",
    )(y, src)


def gate_kernel(y_ref, *refs):
    pieces, (own_ref, src_ref, hid_ref, oth_ref, x_ref, sems) = refs[:8], refs[8:]
    nt = (((1,), (1,)), ((), ()))
    each = fetcher(src_ref, oth_ref, sems, y_ref[0], 0)
    each(range(3), lambda copy: copy.start())
    for k, piece in enumerate(pieces):
        x_ref[k * 64 : k * 64 + 64] = piece[...]
    x = x_ref[...]
    for c, w_ref in enumerate((own_ref, oth_ref)):
        if c == 1:
            each(range(3), lambda copy: copy.wait())
        gate_w = w_ref[0].reshape(768, 2048)
        up_w = w_ref[1].reshape(768, 2048)
        for t in range(3):
            gate = lax.dot_general(x, gate_w[t * 256 : t * 256 + 256], nt, preferred_element_type=F32)
            upper = lax.dot_general(x, up_w[t * 256 : t * 256 + 256], nt, preferred_element_type=F32)
            hidden = gate / (1.0 + jnp.exp(-gate)) * upper
            at = c * 768 + t * 256
            hid_ref[:, at : at + 256] = hidden.astype(BF)


def gate_up(y, pieces, own, src):
    vm = pl.BlockSpec(memory_space=pltpu.VMEM)
    return pl.pallas_call(
        gate_kernel,
        in_specs=[pl.BlockSpec(memory_space=pltpu.SMEM)] + [vm] * 9 + [pl.BlockSpec(memory_space=pltpu.HBM)],
        out_shape=(jax.ShapeDtypeStruct((512, 1536), BF), jax.ShapeDtypeStruct((3, 8, 96, 2048), BF)),
        scratch_shapes=[pltpu.VMEM((512, 2048), BF), pltpu.SemaphoreType.DMA((3, 8))],
        compiler_params=pltpu.CompilerParams(vmem_limit_bytes=40 << 20),
        name="gate_up",
    )(y, *pieces, own, src)


def down_columns(hid, own_ref, oth_ref, store):
    def column(n, carry):
        at = pl.ds(pl.multiple_of(n * 512, 512), 512)
        out = jnp.dot(hid[:, :768], own_ref[2, :, :, at].reshape(768, 512), preferred_element_type=F32)
        out = out + jnp.dot(hid[:, 768:], oth_ref[2, :, :, at].reshape(768, 512), preferred_element_type=F32)
        store(at, out)
        return carry

    lax.fori_loop(0, 4, column, 0)


def far_kernel(hid_ref, own_ref, oth_ref, top_ref, bottom_ref):
    def store(at, out):
        top_ref[:, at] = out[:64].astype(BF)
        bottom_ref[:, at] = out[64:].astype(BF)

    down_columns(hid_ref[384:], own_ref, oth_ref, store)


def near_kernel(hid_ref, own_ref, oth_ref, keep_ref, lt_ref, lb_ref, rt_ref, rb_ref):
    def store(at, out):
        keep_ref[:, at] = out[:128]
        for k, ref in enumerate((lt_ref, lb_ref, rt_ref, rb_ref)):
            ref[:, at] = out[128 + 64 * k : 192 + 64 * k].astype(BF)

    down_columns(hid_ref[:384], own_ref, oth_ref, store)


def down(kernel, name, outs, hidden, own, oth):
    return pl.pallas_call(
        kernel,
        out_shape=outs,
        compiler_params=pltpu.CompilerParams(vmem_limit_bytes=40 << 20),
        name=name,
    )(hidden, own, oth)


def pack_kernel(q_ref, k_ref, v_ref, o_ref, out_ref):
    parts = [q_ref[:, :128], q_ref[:, 128:], k_ref[...], v_ref[...], o_ref[...]]
    whole = jnp.concatenate(parts, axis=0).astype(BF)
    for i in range(8):
        out_ref[i] = whole


def pack(q, k, v, o):
    return pl.pallas_call(
        pack_kernel,
        out_shape=jax.ShapeDtypeStruct((8, 768, 128), BF),
        name="pack",
    )(q, k, v, o)


def prep_kernel(y_ref, gate_ref, up_ref, down_ref, p0_ref, p1_ref, p2_ref, p3_ref, g_ref, u_ref):
    g_ref[...] = gate_ref[...].T
    u_ref[...] = up_ref[...].T
    for k, out_ref in enumerate((p0_ref, p1_ref, p2_ref, p3_ref)):
        at = pl.ds(pl.multiple_of(lax.rem(y_ref[0] + k, 4) * 96, 96), 96)
        out_ref[:96] = g_ref[at, :].astype(BF)
        out_ref[96:192] = u_ref[at, :].astype(BF)
        out_ref[192:] = down_ref[at, :].astype(BF)


def prepare(y, gate, up, down):
    vm = pl.BlockSpec(memory_space=pltpu.VMEM)
    return pl.pallas_call(
        prep_kernel,
        in_specs=[pl.BlockSpec(memory_space=pltpu.SMEM)] + [vm] * 3,
        out_shape=[jax.ShapeDtypeStruct((288, 256), BF)] * 4,
        scratch_shapes=[pltpu.VMEM((384, 256), F32), pltpu.VMEM((384, 256), F32)],
        name="prep",
    )(y, gate, up, down)


def join_kernel(p0_ref, p1_ref, p2_ref, p3_ref, out_ref):
    for k, ref in enumerate((p0_ref, p1_ref, p2_ref, p3_ref)):
        out_ref[k] = ref[...]


def join(parts):
    return pl.pallas_call(join_kernel, out_shape=jax.ShapeDtypeStruct((4, 288, 256), BF), name="join")(*parts)


def trade(parts):
    return [parts[0]] + [lax.ppermute(parts[4 - k], "y", ring(4 - k)) for k in (1, 2, 3)]


def per_device(
    tokens,
    doc_ids,
    positions,
    attn_gain,
    mlp_gain,
    q_gain,
    key_norm_gain,
    q_weight,
    key_matrix,
    value_matrix,
    o_weight,
    gate_weight,
    up_weight,
    down_weight,
):
    rows = tokens.shape[0]
    core = lax.axis_index("core").astype(jnp.int32)
    xl = lax.axis_index("xl").astype(jnp.int32)
    y = lax.axis_index("y").astype(jnp.int32)
    hold = lax.optimization_barrier

    packed = pack(q_weight, key_matrix, value_matrix, o_weight)
    at_own = lax.all_to_all(packed, ("z", "xh"), split_axis=0, concat_axis=0, tiled=True)

    parts = trade(prepare(y[None], gate_weight, up_weight, down_weight))
    half = HEAD // 2
    freq = jnp.exp(jnp.arange(half, dtype=F32) * (-2.0 * math.log(1000000.0) / HEAD))
    angle = positions.astype(F32)[:, None] * freq[None, :]
    cs = jnp.concatenate([jnp.cos(angle), jnp.sin(angle)], axis=1)
    cs, at_own, *parts = hold((cs, at_own, *parts))
    mlp_own = lax.all_gather(join(parts), ("z", "xh", "xl"), axis=0, tiled=False).reshape(8, 2, 4, 288, 256)
    lo = (jnp.arange(rows, dtype=jnp.int32) - positions)[:, None]

    at_oth = swap(at_own, "core")

    o_wide = jnp.broadcast_to(at_own[None, :, 512:], (4, 8, 256, 128))
    o_own = lax.all_to_all(o_wide, "y", split_axis=0, concat_axis=0, tiled=True)

    q, cache, tail = project(core[None], tokens, at_own, at_oth, attn_gain, q_gain, key_norm_gain, cs)
    prior = lax.ppermute(tail, REQ, [(i - 1, i) for i in range(1, 16)])
    ctx = attend(q, cache, prior, lo)
    ctx, o_own = hold((ctx, o_own))
    o_oth = swap(o_own, "core")
    ctx = lax.all_to_all(ctx, "y", split_axis=0, concat_axis=0, tiled=True)
    keep, send = out_project(jnp.stack([core, xl]), ctx, o_own, o_oth)
    got = swap(send, "xl")

    resid, top, bottom = middle((xl * 4 + y)[None], tokens, keep, got, mlp_gain)
    to_right, to_left = ring(1), ring(3)
    left_top = lax.ppermute(top, "y", to_right)
    right_bottom = lax.ppermute(bottom, "y", to_left)
    left_bottom = lax.ppermute(bottom, "y", to_right)
    right_top = lax.ppermute(top, "y", to_left)
    far_top = lax.ppermute(left_top, "y", to_right)
    far_bottom = lax.ppermute(right_bottom, "y", to_left)
    mlp_own, _, _ = hold((mlp_own, left_top, right_bottom))
    mlp_oth = swap(mlp_own, "core")
    own = load(y[None], pltpu.with_memory_space_constraint(mlp_own, pltpu.HBM))
    pieces = (top, bottom, left_top, left_bottom, right_top, right_bottom, far_top, far_bottom)
    hidden, oth = gate_up(y[None], pieces, own, mlp_oth)

    half = jax.ShapeDtypeStruct((64, 2048), BF)
    far_top, far_bottom = down(far_kernel, "down_far", (half, half), hidden, own, oth)
    via_left = lax.ppermute(far_top, "y", to_right)
    via_right = lax.ppermute(far_bottom, "y", to_left)
    whole = jax.ShapeDtypeStruct((128, 2048), F32)
    keep, left_top, left_bottom, right_top, right_bottom = down(
        near_kernel, "down", (whole, half, half, half, half), hidden, own, oth
    )
    got_left_bottom = lax.ppermute(right_bottom, "y", to_right)
    got_right_top = lax.ppermute(left_top, "y", to_left)
    right_top = (right_top.astype(F32) + via_left.astype(F32)).astype(BF)
    left_bottom = (left_bottom.astype(F32) + via_right.astype(F32)).astype(BF)
    got_left_top = lax.ppermute(right_top, "y", to_right)
    got_right_bottom = lax.ppermute(left_bottom, "y", to_left)
    out = pl.pallas_call(last_kernel, out_shape=jax.ShapeDtypeStruct((128, 2048), BF), name="last")(
        resid, keep, got_left_top, got_left_bottom, got_right_top, got_right_bottom
    )
    return (out, cache)


def solution(mesh):
    fine = Mesh(mesh.devices.reshape(4, 2, 2, 2, 4), REQ + MDL)
    rows = P(REQ)
    in_specs = (
        P(REQ, None),
        rows,
        rows,
        P(),
        P(),
        P(),
        P(),
        P(REQ, MDL),
        P(REQ, MDL),
        P(REQ, MDL),
        P(MDL, REQ),
        P(MDL, REQ),
        P(MDL, REQ),
        P(REQ, MDL),
    )
    out_specs = (P(REQ + MDL, None), P(None, REQ, MDL))
    return jax.shard_map(per_device, mesh=fine, in_specs=in_specs, out_specs=out_specs, check_vma=False)
```

```python
import math

import jax
import jax.numpy as jnp
from jax import lax
from jax.experimental import pallas as pl
from jax.experimental.pallas import tpu as pltpu
from jax.sharding import Mesh
from jax.sharding import PartitionSpec as P

HEAD = 128
BF = jnp.bfloat16
F32 = jnp.float32
REQ = ("z", "xh", "core")
MDL = ("xl", "y")


def ring(step):
    return [(i, (i + step) % 4) for i in range(4)]


def swap(block, axis):
    return lax.ppermute(block, axis, [(0, 1), (1, 0)])


def qkv_kernel(core_ref, x_ref, own_ref, oth_ref, gain_ref, qg_ref, kg_ref, cs_ref, q_ref, kv_ref, tail_ref, w_ref):
    core = core_ref[0]

    @pl.when(pl.program_id(0) == 0)
    def _():
        def place(i, carry):
            for src, side in ((own_ref, core), (oth_ref, 1 - core)):
                at = pl.ds(pl.multiple_of((2 * i + side) * 128, 128), 128)
                for k in range(4):
                    w_ref[at, k * 128 : k * 128 + 128] = src[i, k * 128 : k * 128 + 128]
            return carry

        lax.fori_loop(0, 8, place, 0)

    x = x_ref[...].astype(F32)
    scale = lax.rsqrt(jnp.mean(x * x, axis=-1, keepdims=True) + 1e-06)
    normed = (x * scale * gain_ref[...]).astype(BF)
    raw = jnp.dot(normed, w_ref[...], preferred_element_type=F32)
    cs = cs_ref[...]
    turned = pltpu.roll(cs, 64, 1)
    low = lax.broadcasted_iota(jnp.int32, cs.shape, 1) < 64
    cosine = jnp.where(low, cs, turned)
    sine = jnp.where(low, -turned, cs)

    def head(t, gain):
        t = t * lax.rsqrt(jnp.mean(t * t, axis=-1, keepdims=True) + 1e-06) * gain
        return (t * cosine + pltpu.roll(t, 64, 1) * sine).astype(BF)

    q_ref[:, :128] = head(raw[:, :128], qg_ref[...])
    q_ref[:, 128:] = head(raw[:, 128:256], qg_ref[...])
    keys = head(raw[:, 256:384], kg_ref[...])
    values = raw[:, 384:].astype(BF)
    kv_ref[0] = keys
    kv_ref[1] = values

    @pl.when(pl.program_id(0) >= 2)
    def _():
        tail_ref[0] = keys
        tail_ref[1] = values


def project(core, tokens, own, oth, attn_gain, q_gain, key_gain, cs):
    rows = tokens.shape[0]
    tile = 256
    fixed = lambda *shape: pl.BlockSpec(shape, lambda i, c: (0,) * len(shape))
    return pl.pallas_call(
        qkv_kernel,
        grid_spec=pltpu.PrefetchScalarGridSpec(
            num_scalar_prefetch=1,
            grid=(rows // tile,),
            in_specs=[
                pl.BlockSpec((tile, 2048), lambda i, c: (i, 0)),
                fixed(8, 512, 128),
                fixed(8, 512, 128),
                fixed(1, 2048),
                fixed(1, 128),
                fixed(1, 128),
                pl.BlockSpec((tile, 128), lambda i, c: (i, 0)),
            ],
            out_specs=[
                pl.BlockSpec((tile, 256), lambda i, c: (i, 0)),
                pl.BlockSpec((2, tile, 128), lambda i, c: (0, i, 0)),
                pl.BlockSpec((2, tile, 128), lambda i, c: (0, jnp.maximum(i - 2, 0), 0)),
            ],
            scratch_shapes=[pltpu.VMEM((2048, 512), BF)],
        ),
        out_shape=(
            jax.ShapeDtypeStruct((rows, 256), BF),
            jax.ShapeDtypeStruct((2, rows, 128), BF),
            jax.ShapeDtypeStruct((2, rows // 2, 128), BF),
        ),
        compiler_params=pltpu.CompilerParams(vmem_limit_bytes=40 << 20),
        name="qkv",
    )(core, tokens, own, oth, attn_gain[None], q_gain[None], key_gain[None], cs)


def attend_kernel(half_ref, q_ref, kv_ref, prior_ref, lo_ref, out_ref):
    factor = HEAD ** (-0.5) * math.log2(math.e)
    nt = (((1,), (1,)), ((), ()))

    def block(i):
        first = i * 256
        skip = 256 if i == 3 else 0
        count = first + 256
        lo = lo_ref[first : first + 256, :]
        row = lax.broadcasted_iota(jnp.int32, (256, count), 0) + first
        col = lax.broadcasted_iota(jnp.int32, (256, count), 1)
        near = (col >= lo) & (col <= row)
        prior_col = lax.broadcasted_iota(jnp.int32, (256, 512 - skip), 1) + (skip - 512)
        far = prior_col >= lo

        def head(h, carry):
            lanes = pl.ds(pl.multiple_of(h * 128, 128), 128)
            q = q_ref[first : first + 256, lanes]
            s1 = lax.dot_general(q, kv_ref[0, :count], nt, preferred_element_type=F32)
            s0 = lax.dot_general(q, prior_ref[0, skip:], nt, preferred_element_type=F32)
            s1 = jnp.where(near, s1, -1e30)
            s0 = jnp.where(far, s0, -1e30)
            top = jnp.maximum(jnp.max(s1, -1, keepdims=True), jnp.max(s0, -1, keepdims=True))
            e1 = jnp.exp2((s1 - top) * factor)
            e0 = jnp.exp2((s0 - top) * factor)
            inv = 1.0 / (jnp.sum(e1, -1, keepdims=True) + jnp.sum(e0, -1, keepdims=True))
            p1 = (e1 * inv).astype(BF)
            p0 = (e0 * inv).astype(BF)
            o = jnp.dot(p1, kv_ref[1, :count], preferred_element_type=F32)
            o = o + jnp.dot(p0, prior_ref[1, skip:], preferred_element_type=F32)
            o = o.astype(BF)
            for part in range(2):
                out_ref[(2 * i + part) % 4, :, lanes] = o[part * 128 : part * 128 + 128]
            return carry

        lax.fori_loop(0, 2, head, 0)

    @pl.when(half_ref[0] == 0)
    def _():
        block(0)
        block(1)

    @pl.when(half_ref[0] == 1)
    def _():
        block(2)
        block(3)


def attend(half, q, kv, prior, lo):
    vm = pl.BlockSpec(memory_space=pltpu.VMEM)
    return pl.pallas_call(
        attend_kernel,
        in_specs=[pl.BlockSpec(memory_space=pltpu.SMEM)] + [vm] * 4,
        out_shape=jax.ShapeDtypeStruct((4, 128, 256), BF),
        compiler_params=pltpu.CompilerParams(vmem_limit_bytes=40 << 20),
        name="attend",
    )(half, q, kv, prior, lo)


def out_kernel(core_ref, ctx_ref, own_ref, oth_ref, out_ref, w_ref, sems):
    core = core_ref[0]

    def each(act):
        def step(n, carry):
            s, i = n // 8, lax.rem(n, 8)
            for which, (src, side) in enumerate(((own_ref, core), (oth_ref, 1 - core))):
                at = pl.ds(pl.multiple_of((2 * i + side) * 128, 128), 128)
                act(pltpu.make_async_copy(
                    src.at[s, i], w_ref.at[pl.ds(pl.multiple_of(s * 256, 256), 256), at], sems.at[which, s, i]
                ))
            return carry

        lax.fori_loop(0, 32, step, 0)

    each(lambda c: c.start())
    x = jnp.concatenate([ctx_ref[s] for s in range(4)], axis=1)
    each(lambda c: c.wait())

    def column(n, carry):
        at = pl.ds(pl.multiple_of(n * 512, 512), 512)
        out_ref[:, at] = jnp.dot(x, w_ref[:, at], preferred_element_type=F32).astype(out_ref.dtype)
        return carry

    lax.fori_loop(0, 4, column, 0)


def out_project(core, ctx, own, oth, dtype):
    vm = pl.BlockSpec(memory_space=pltpu.VMEM)
    anywhere = pl.BlockSpec(memory_space=pl.ANY)
    return pl.pallas_call(
        out_kernel,
        in_specs=[pl.BlockSpec(memory_space=pltpu.SMEM), vm, anywhere, anywhere],
        out_shape=jax.ShapeDtypeStruct((128, 2048), dtype),
        scratch_shapes=[pltpu.VMEM((1024, 2048), BF), pltpu.SemaphoreType.DMA((2, 4, 8))],
        compiler_params=pltpu.CompilerParams(vmem_limit_bytes=40 << 20),
        name="oproj",
    )(core, ctx, own, oth)


def fetcher(own_ref, oth_ref, w_ref, sems, y, first):
    def copy(c, g, m):
        src = own_ref if c == 0 else oth_ref
        at = pl.multiple_of(((m // 4) * 4 + lax.rem(y + lax.rem(m, 4), 4)) * 256, 256)
        return pltpu.make_async_copy(
            src.at[:, m // 4, lax.rem(m, 4), first + g * 96 : first + g * 96 + 96, :],
            w_ref.at[g, c * 8 : c * 8 + 8, :, pl.ds(at, 256)],
            sems.at[g, c, m],
        )

    def each(c, groups, act):
        def step(m, carry):
            for g in range(groups):
                act(copy(c, g, m))
            return carry

        lax.fori_loop(0, 8, step, 0)

    return each


def gate_kernel(y_ref, x0_ref, x1_ref, x2_ref, x3_ref, x4_ref, own_ref, oth_ref, hid_ref, w_ref, x_ref, sems):
    nt = (((1,), (1,)), ((), ()))
    each = fetcher(own_ref, oth_ref, w_ref, sems, y_ref[0], 0)
    each(0, 2, lambda c: c.start())
    each(1, 2, lambda c: c.start())
    x_ref[0:128] = x0_ref[...]
    x_ref[128:256] = x1_ref[...]
    x_ref[256:384] = x2_ref[...]
    x_ref[384:448] = x3_ref[...]
    x_ref[448:512] = x4_ref[...]
    x = x_ref[...]

    for c in range(2):
        each(c, 2, lambda copy: copy.wait())
        gate_w = w_ref[0, c * 8 : c * 8 + 8].reshape(768, 2048)
        up_w = w_ref[1, c * 8 : c * 8 + 8].reshape(768, 2048)
        for t in range(3):
            gate = lax.dot_general(x, gate_w[t * 256 : t * 256 + 256], nt, preferred_element_type=F32)
            upper = lax.dot_general(x, up_w[t * 256 : t * 256 + 256], nt, preferred_element_type=F32)
            hidden = gate / (1.0 + jnp.exp(-gate)) * upper
            at = c * 768 + t * 256
            hid_ref[:, at : at + 256] = hidden.astype(BF)


def far_kernel(y_ref, hid_ref, own_ref, oth_ref, top_ref, bottom_ref, w_ref, sems):
    each = fetcher(own_ref, oth_ref, w_ref, sems, y_ref[0], 192)
    for c in range(2):
        each(c, 1, lambda copy: copy.start())
    for c in range(2):
        each(c, 1, lambda copy: copy.wait())
    hid = hid_ref[384:]

    def column(n, carry):
        at = pl.ds(pl.multiple_of(n * 512, 512), 512)
        out = jnp.dot(hid, w_ref[0, :, :, at].reshape(1536, 512), preferred_element_type=F32)
        top_ref[:, at] = out[:64].astype(BF)
        bottom_ref[:, at] = out[64:].astype(BF)
        return carry

    lax.fori_loop(0, 4, column, 0)


def down_kernel(hid_ref, w_ref, keep_ref, left_ref, right_ref):
    hid = hid_ref[:384]

    def column(n, carry):
        at = pl.ds(pl.multiple_of(n * 512, 512), 512)
        out = jnp.dot(hid, w_ref[0, :, :, at].reshape(1536, 512), preferred_element_type=F32)
        keep_ref[:, at] = out[:128]
        left_ref[:, at] = out[128:256].astype(BF)
        right_ref[:, at] = out[256:].astype(BF)
        return carry

    lax.fori_loop(0, 4, column, 0)


def gate_up(y, pieces, own, oth):
    vm = pl.BlockSpec(memory_space=pltpu.VMEM)
    hbm = pl.BlockSpec(memory_space=pltpu.HBM)
    return pl.pallas_call(
        gate_kernel,
        in_specs=[pl.BlockSpec(memory_space=pltpu.SMEM)] + [vm] * 5 + [hbm] * 2,
        out_shape=jax.ShapeDtypeStruct((512, 1536), BF),
        scratch_shapes=[
            pltpu.VMEM((2, 16, 96, 2048), BF),
            pltpu.VMEM((512, 2048), BF),
            pltpu.SemaphoreType.DMA((2, 2, 8)),
        ],
        compiler_params=pltpu.CompilerParams(vmem_limit_bytes=40 << 20),
        name="gate_up",
    )(y, *pieces, own, oth)


def down_far(y, hidden, own, oth):
    vm = pl.BlockSpec(memory_space=pltpu.VMEM)
    hbm = pl.BlockSpec(memory_space=pltpu.HBM)
    half = jax.ShapeDtypeStruct((64, 2048), BF)
    return pl.pallas_call(
        far_kernel,
        in_specs=[pl.BlockSpec(memory_space=pltpu.SMEM), vm] + [hbm] * 2,
        out_shape=(half, half, jax.ShapeDtypeStruct((1, 16, 96, 2048), BF)),
        scratch_shapes=[pltpu.SemaphoreType.DMA((1, 2, 8))],
        compiler_params=pltpu.CompilerParams(vmem_limit_bytes=40 << 20),
        name="down_far",
    )(y, hidden, own, oth)


def down(hidden, weight):
    part = jax.ShapeDtypeStruct((128, 2048), BF)
    return pl.pallas_call(
        down_kernel,
        out_shape=(jax.ShapeDtypeStruct((128, 2048), F32), part, part),
        compiler_params=pltpu.CompilerParams(vmem_limit_bytes=40 << 20),
        name="down",
    )(hidden, weight)


def pack_kernel(q_ref, k_ref, v_ref, o_ref, out_ref):
    parts = [q_ref[:, :128], q_ref[:, 128:], k_ref[...], v_ref[...], o_ref[...]]
    whole = jnp.concatenate(parts, axis=0).astype(BF)
    for i in range(8):
        out_ref[i] = whole


def pack(q, k, v, o):
    return pl.pallas_call(
        pack_kernel,
        out_shape=jax.ShapeDtypeStruct((8, 768, 128), BF),
        name="pack",
    )(q, k, v, o)


def prep_kernel(y_ref, gate_ref, up_ref, down_ref, p0_ref, p1_ref, p2_ref, p3_ref, g_ref, u_ref):
    g_ref[...] = gate_ref[...].T
    u_ref[...] = up_ref[...].T
    for k, out_ref in enumerate((p0_ref, p1_ref, p2_ref, p3_ref)):
        at = pl.ds(pl.multiple_of(lax.rem(y_ref[0] + k, 4) * 96, 96), 96)
        out_ref[:96] = g_ref[at, :].astype(BF)
        out_ref[96:192] = u_ref[at, :].astype(BF)
        out_ref[192:] = down_ref[at, :].astype(BF)


def prepare(y, gate, up, down):
    vm = pl.BlockSpec(memory_space=pltpu.VMEM)
    return pl.pallas_call(
        prep_kernel,
        in_specs=[pl.BlockSpec(memory_space=pltpu.SMEM)] + [vm] * 3,
        out_shape=[jax.ShapeDtypeStruct((288, 256), BF)] * 4,
        scratch_shapes=[pltpu.VMEM((384, 256), F32), pltpu.VMEM((384, 256), F32)],
        name="prep",
    )(y, gate, up, down)


def join_kernel(p0_ref, p1_ref, p2_ref, p3_ref, out_ref):
    for k, ref in enumerate((p0_ref, p1_ref, p2_ref, p3_ref)):
        out_ref[k] = ref[...]


def join(parts):
    return pl.pallas_call(join_kernel, out_shape=jax.ShapeDtypeStruct((4, 288, 256), BF), name="join")(*parts)


def trade(parts):
    return [parts[0]] + [lax.ppermute(parts[4 - k], "y", ring(4 - k)) for k in (1, 2, 3)]


def per_device(
    tokens,
    doc_ids,
    positions,
    attn_gain,
    mlp_gain,
    q_gain,
    key_norm_gain,
    q_weight,
    key_matrix,
    value_matrix,
    o_weight,
    gate_weight,
    up_weight,
    down_weight,
):
    rows = tokens.shape[0]
    core = lax.axis_index("core").astype(jnp.int32)
    xl = lax.axis_index("xl").astype(jnp.int32)
    y = lax.axis_index("y").astype(jnp.int32)
    hold = lax.optimization_barrier

    packed = pack(q_weight, key_matrix, value_matrix, o_weight)
    at_own = lax.all_to_all(packed, ("z", "xh"), split_axis=0, concat_axis=0, tiled=True)

    parts = trade(prepare(y[None], gate_weight, up_weight, down_weight))
    half = HEAD // 2
    freq = jnp.exp(jnp.arange(half, dtype=F32) * (-2.0 * math.log(1000000.0) / HEAD))
    angle = positions.astype(F32)[:, None] * freq[None, :]
    cs = jnp.concatenate([jnp.cos(angle), jnp.sin(angle)], axis=1)
    group = join(parts)
    cs, at_own, group = hold((cs, at_own, group))
    mlp_own = lax.all_gather(group, ("z", "xh", "xl"), axis=0, tiled=False).reshape(8, 2, 4, 288, 256)
    lo = (jnp.arange(rows, dtype=jnp.int32) - positions)[:, None]

    at_oth = swap(at_own, "core")

    o_wide = jnp.broadcast_to(at_own[None, :, 512:], (4, 8, 256, 128))
    o_own = lax.all_to_all(o_wide, "y", split_axis=0, concat_axis=0, tiled=True)

    rows_in = pltpu.with_memory_space_constraint(tokens, pltpu.HBM)
    q, cache, tail = project(core[None], rows_in, at_own, at_oth, attn_gain, q_gain, key_norm_gain, cs)
    prior = lax.ppermute(tail, REQ, [(i - 1, i) for i in range(1, 16)])
    turn = lambda part: lax.all_to_all(part, "y", split_axis=0, concat_axis=0, tiled=True)
    theirs = attend(1 - xl[None], q, cache, prior, lo)
    _, q = hold((theirs, q))
    mine = attend(xl[None], q, cache, prior, lo)
    _, o_own = hold((mine, o_own))
    o_oth = swap(o_own, "core")
    send = out_project(core[None], turn(theirs), o_own, o_oth, BF)
    got = swap(send, "xl")
    _, mine = hold((send, mine))
    keep = out_project(core[None], turn(mine), o_own, o_oth, F32)

    own_rows = lax.dynamic_slice_in_dim(tokens, (xl * 4 + y) * 128, 128, 0).astype(F32)
    resid = (own_rows + (keep + got.astype(F32))).astype(BF)
    resid = hold(resid).astype(F32)
    scale = lax.rsqrt(jnp.mean(resid * resid, axis=-1, keepdims=True) + 1e-06)
    mlp_in = (resid * scale * mlp_gain).astype(BF)

    left = lax.ppermute(mlp_in, "y", ring(1))
    right = lax.ppermute(mlp_in, "y", ring(3))
    mlp_own, left, right = hold((mlp_own, left, right))
    mlp_oth = swap(mlp_own, "core")
    far_top = lax.ppermute(left[:64], "y", ring(1))
    far_bottom = lax.ppermute(right[64:], "y", ring(3))
    hidden = gate_up(y[None], (mlp_in, left, right, far_top, far_bottom), mlp_own, mlp_oth)
    top, bottom, weight = down_far(y[None], hidden, mlp_own, mlp_oth)
    via_left = lax.ppermute(top, "y", ring(1))
    via_right = lax.ppermute(bottom, "y", ring(3))
    keep, to_left, to_right = down(hidden, weight)
    via_left, via_right = hold((via_left, via_right))
    to_right = jnp.concatenate([(to_right[:64].astype(F32) + via_left.astype(F32)).astype(BF), to_right[64:]])
    to_left = jnp.concatenate([to_left[:64], (to_left[64:].astype(F32) + via_right.astype(F32)).astype(BF)])
    from_left = lax.ppermute(to_right, "y", ring(1))
    from_right = lax.ppermute(to_left, "y", ring(3))
    total = keep + from_left.astype(F32) + from_right.astype(F32)
    return ((resid + total).astype(BF), cache)


def solution(mesh):
    fine = Mesh(mesh.devices.reshape(4, 2, 2, 2, 4), REQ + MDL)
    rows = P(REQ)
    in_specs = (
        P(REQ, None),
        rows,
        rows,
        P(),
        P(),
        P(),
        P(),
        P(REQ, MDL),
        P(REQ, MDL),
        P(REQ, MDL),
        P(MDL, REQ),
        P(MDL, REQ),
        P(MDL, REQ),
        P(REQ, MDL),
    )
    out_specs = (P(REQ + MDL, None), P(None, REQ, MDL))
    return jax.shard_map(per_device, mesh=fine, in_specs=in_specs, out_specs=out_specs, check_vma=False)
```

```python
import math

import jax
import jax.numpy as jnp
from jax import lax
from jax.experimental import pallas as pl
from jax.experimental.pallas import tpu as pltpu
from jax.sharding import Mesh
from jax.sharding import PartitionSpec as P

HEAD = 128
BF = jnp.bfloat16
F32 = jnp.float32
REQ = ("z", "xh", "core")
MDL = ("xl", "y")


def ring(step):
    return [(i, (i + step) % 4) for i in range(4)]


def swap(block, axis):
    return lax.ppermute(block, axis, [(0, 1), (1, 0)])


def qkv_kernel(core_ref, x_ref, own_ref, oth_ref, gain_ref, qg_ref, kg_ref, cs_ref, q_ref, kv_ref, tail_ref, w_ref):
    core = core_ref[0]

    @pl.when(pl.program_id(0) == 0)
    def _():
        def place(i, carry):
            for src, side in ((own_ref, core), (oth_ref, 1 - core)):
                at = pl.ds(pl.multiple_of((2 * i + side) * 128, 128), 128)
                for k in range(4):
                    w_ref[at, k * 128 : k * 128 + 128] = src[i, k * 128 : k * 128 + 128]
            return carry

        lax.fori_loop(0, 8, place, 0)

    x = x_ref[...].astype(F32)
    scale = lax.rsqrt(jnp.mean(x * x, axis=-1, keepdims=True) + 1e-06)
    normed = (x * scale * gain_ref[...]).astype(BF)
    raw = jnp.dot(normed, w_ref[...], preferred_element_type=F32)
    cs = cs_ref[...]
    turned = pltpu.roll(cs, 64, 1)
    low = lax.broadcasted_iota(jnp.int32, cs.shape, 1) < 64
    cosine = jnp.where(low, cs, turned)
    sine = jnp.where(low, -turned, cs)

    def head(t, gain):
        t = t * lax.rsqrt(jnp.mean(t * t, axis=-1, keepdims=True) + 1e-06) * gain
        return (t * cosine + pltpu.roll(t, 64, 1) * sine).astype(BF)

    q_ref[:, :128] = head(raw[:, :128], qg_ref[...])
    q_ref[:, 128:] = head(raw[:, 128:256], qg_ref[...])
    keys = head(raw[:, 256:384], kg_ref[...])
    values = raw[:, 384:].astype(BF)
    kv_ref[0] = keys
    kv_ref[1] = values

    @pl.when(pl.program_id(0) >= 2)
    def _():
        tail_ref[0] = keys
        tail_ref[1] = values


def project(core, tokens, own, oth, attn_gain, q_gain, key_gain, cs):
    rows = tokens.shape[0]
    tile = 256
    fixed = lambda *shape: pl.BlockSpec(shape, lambda i, c: (0,) * len(shape))
    return pl.pallas_call(
        qkv_kernel,
        grid_spec=pltpu.PrefetchScalarGridSpec(
            num_scalar_prefetch=1,
            grid=(rows // tile,),
            in_specs=[
                pl.BlockSpec((tile, 2048), lambda i, c: (i, 0)),
                fixed(8, 512, 128),
                fixed(8, 512, 128),
                fixed(1, 2048),
                fixed(1, 128),
                fixed(1, 128),
                pl.BlockSpec((tile, 128), lambda i, c: (i, 0)),
            ],
            out_specs=[
                pl.BlockSpec((tile, 256), lambda i, c: (i, 0)),
                pl.BlockSpec((2, tile, 128), lambda i, c: (0, i, 0)),
                pl.BlockSpec((2, tile, 128), lambda i, c: (0, jnp.maximum(i - 2, 0), 0)),
            ],
            scratch_shapes=[pltpu.VMEM((2048, 512), BF)],
        ),
        out_shape=(
            jax.ShapeDtypeStruct((rows, 256), BF),
            jax.ShapeDtypeStruct((2, rows, 128), BF),
            jax.ShapeDtypeStruct((2, rows // 2, 128), BF),
        ),
        compiler_params=pltpu.CompilerParams(vmem_limit_bytes=24 << 20),
        name="qkv",
    )(core, tokens, own, oth, attn_gain[None], q_gain[None], key_gain[None], cs)


def widen_kernel(src_ref, out_ref, sems):
    copies = [pltpu.make_async_copy(src_ref.at[:, 512:], out_ref.at[k], sems.at[k]) for k in range(4)]
    for copy in copies:
        copy.start()
    for copy in copies:
        copy.wait()


def widen(gathered):
    return pl.pallas_call(
        widen_kernel,
        in_specs=[pl.BlockSpec(memory_space=pl.ANY)],
        out_specs=pl.BlockSpec(memory_space=pl.ANY),
        out_shape=jax.ShapeDtypeStruct((4, 8, 256, 128), BF),
        scratch_shapes=[pltpu.SemaphoreType.DMA((4,))],
        name="widen",
    )(gathered)


def attend_kernel(half_ref, q_ref, kv_ref, prior_ref, lo_ref, out_ref):
    factor = HEAD ** (-0.5) * math.log2(math.e)
    nt = (((1,), (1,)), ((), ()))

    def block(i):
        first = i * 256
        skip = 256 if i == 3 else 0
        count = first + 256
        lo = lo_ref[first : first + 256, :]
        row = lax.broadcasted_iota(jnp.int32, (256, count), 0) + first
        col = lax.broadcasted_iota(jnp.int32, (256, count), 1)
        near = (col >= lo) & (col <= row)
        prior_col = lax.broadcasted_iota(jnp.int32, (256, 512 - skip), 1) + (skip - 512)
        far = prior_col >= lo

        def head(h, carry):
            lanes = pl.ds(pl.multiple_of(h * 128, 128), 128)
            q = q_ref[first : first + 256, lanes]
            s1 = lax.dot_general(q, kv_ref[0, :count], nt, preferred_element_type=F32)
            s0 = lax.dot_general(q, prior_ref[0, skip:], nt, preferred_element_type=F32)
            s1 = jnp.where(near, s1, -1e30)
            s0 = jnp.where(far, s0, -1e30)
            top = jnp.maximum(jnp.max(s1, -1, keepdims=True), jnp.max(s0, -1, keepdims=True))
            e1 = jnp.exp2((s1 - top) * factor)
            e0 = jnp.exp2((s0 - top) * factor)
            inv = 1.0 / (jnp.sum(e1, -1, keepdims=True) + jnp.sum(e0, -1, keepdims=True))
            p1 = (e1 * inv).astype(BF)
            p0 = (e0 * inv).astype(BF)
            o = jnp.dot(p1, kv_ref[1, :count], preferred_element_type=F32)
            o = o + jnp.dot(p0, prior_ref[1, skip:], preferred_element_type=F32)
            o = o.astype(BF)
            for part in range(2):
                out_ref[(2 * i + part) % 4, :, lanes] = o[part * 128 : part * 128 + 128]
            return carry

        lax.fori_loop(0, 2, head, 0)

    @pl.when(half_ref[0] == 0)
    def _():
        block(0)
        block(1)

    @pl.when(half_ref[0] == 1)
    def _():
        block(2)
        block(3)


def attend(half, q, kv, prior, lo):
    vm = pl.BlockSpec(memory_space=pltpu.VMEM)
    return pl.pallas_call(
        attend_kernel,
        in_specs=[pl.BlockSpec(memory_space=pltpu.SMEM)] + [vm] * 4,
        out_shape=jax.ShapeDtypeStruct((4, 128, 256), BF),
        compiler_params=pltpu.CompilerParams(vmem_limit_bytes=20 << 20),
        name="attend",
    )(half, q, kv, prior, lo)


def out_kernel(core_ref, ctx_ref, own_ref, oth_ref, out_ref, w_ref, sems):
    core = core_ref[0]

    def each(act):
        def step(n, carry):
            s, i = n // 8, lax.rem(n, 8)
            for which, (src, side) in enumerate(((own_ref, core), (oth_ref, 1 - core))):
                at = pl.ds(pl.multiple_of((2 * i + side) * 128, 128), 128)
                act(pltpu.make_async_copy(
                    src.at[s, i], w_ref.at[pl.ds(pl.multiple_of(s * 256, 256), 256), at], sems.at[which, s, i]
                ))
            return carry

        lax.fori_loop(0, 32, step, 0)

    each(lambda c: c.start())
    x = jnp.concatenate([ctx_ref[s] for s in range(4)], axis=1)
    each(lambda c: c.wait())

    def column(n, carry):
        at = pl.ds(pl.multiple_of(n * 512, 512), 512)
        out_ref[:, at] = jnp.dot(x, w_ref[:, at], preferred_element_type=F32).astype(out_ref.dtype)
        return carry

    lax.fori_loop(0, 4, column, 0)


def out_project(core, ctx, own, oth, dtype):
    vm = pl.BlockSpec(memory_space=pltpu.VMEM)
    anywhere = pl.BlockSpec(memory_space=pl.ANY)
    return pl.pallas_call(
        out_kernel,
        in_specs=[pl.BlockSpec(memory_space=pltpu.SMEM), vm, anywhere, anywhere],
        out_shape=jax.ShapeDtypeStruct((128, 2048), dtype),
        scratch_shapes=[pltpu.VMEM((1024, 2048), BF), pltpu.SemaphoreType.DMA((2, 4, 8))],
        compiler_params=pltpu.CompilerParams(vmem_limit_bytes=14 << 20),
        name="oproj",
    )(core, ctx, own, oth)


def fetcher(own_ref, oth_ref, w_ref, sems, y, first):
    def copy(c, g, m):
        src = own_ref if c == 0 else oth_ref
        at = pl.multiple_of(((m // 4) * 4 + lax.rem(y + lax.rem(m, 4), 4)) * 256, 256)
        return pltpu.make_async_copy(
            src.at[:, m // 4, lax.rem(m, 4), first + g * 96 : first + g * 96 + 96, :],
            w_ref.at[g, c * 8 : c * 8 + 8, :, pl.ds(at, 256)],
            sems.at[g, c, m],
        )

    def each(c, groups, act):
        def step(m, carry):
            for g in range(groups):
                act(copy(c, g, m))
            return carry

        lax.fori_loop(0, 8, step, 0)

    return each


def gate_kernel(y_ref, x0_ref, x1_ref, x2_ref, x3_ref, x4_ref, src_ref, hid_ref, w_ref, x_ref, sems):
    nt = (((1,), (1,)), ((), ()))
    each = fetcher(src_ref, src_ref, w_ref, sems, y_ref[0], 0)
    each(0, 2, lambda c: c.start())
    x_ref[0:128] = x0_ref[...]
    x_ref[128:256] = x1_ref[...]
    x_ref[256:384] = x2_ref[...]
    x_ref[384:448] = x3_ref[...]
    x_ref[448:512] = x4_ref[...]
    x = x_ref[...]
    each(0, 2, lambda copy: copy.wait())
    gate_w = w_ref[0].reshape(768, 2048)
    up_w = w_ref[1].reshape(768, 2048)
    for t in range(3):
        gate = lax.dot_general(x, gate_w[t * 256 : t * 256 + 256], nt, preferred_element_type=F32)
        upper = lax.dot_general(x, up_w[t * 256 : t * 256 + 256], nt, preferred_element_type=F32)
        hidden = gate / (1.0 + jnp.exp(-gate)) * upper
        hid_ref[:, t * 256 : t * 256 + 256] = hidden.astype(BF)


def far_kernel(y_ref, hid0_ref, hid1_ref, own_ref, oth_ref, top_ref, bottom_ref, w_ref, sems):
    each = fetcher(own_ref, oth_ref, w_ref, sems, y_ref[0], 192)
    for c in range(2):
        each(c, 1, lambda copy: copy.start())
    for c in range(2):
        each(c, 1, lambda copy: copy.wait())
    hid = jnp.concatenate([hid0_ref[384:], hid1_ref[384:]], axis=1)

    def column(n, carry):
        at = pl.ds(pl.multiple_of(n * 512, 512), 512)
        out = jnp.dot(hid, w_ref[0, :, :, at].reshape(1536, 512), preferred_element_type=F32)
        top_ref[:, at] = out[:64].astype(BF)
        bottom_ref[:, at] = out[64:].astype(BF)
        return carry

    lax.fori_loop(0, 4, column, 0)


def down_kernel(hid0_ref, hid1_ref, w_ref, keep_ref, left_ref, right_ref):
    hid = jnp.concatenate([hid0_ref[:384], hid1_ref[:384]], axis=1)

    def column(n, carry):
        at = pl.ds(pl.multiple_of(n * 512, 512), 512)
        out = jnp.dot(hid, w_ref[0, :, :, at].reshape(1536, 512), preferred_element_type=F32)
        keep_ref[:, at] = out[:128]
        left_ref[:, at] = out[128:256].astype(BF)
        right_ref[:, at] = out[256:].astype(BF)
        return carry

    lax.fori_loop(0, 4, column, 0)


def gate_up(y, pieces, src):
    vm = pl.BlockSpec(memory_space=pltpu.VMEM)
    hbm = pl.BlockSpec(memory_space=pltpu.HBM)
    return pl.pallas_call(
        gate_kernel,
        in_specs=[pl.BlockSpec(memory_space=pltpu.SMEM)] + [vm] * 5 + [hbm],
        out_shape=jax.ShapeDtypeStruct((512, 768), BF),
        scratch_shapes=[
            pltpu.VMEM((2, 8, 96, 2048), BF),
            pltpu.VMEM((512, 2048), BF),
            pltpu.SemaphoreType.DMA((2, 1, 8)),
        ],
        compiler_params=pltpu.CompilerParams(vmem_limit_bytes=18 << 20),
        name="gate_up",
    )(y, *pieces, src)


def down_far(y, hidden, own, oth):
    vm = pl.BlockSpec(memory_space=pltpu.VMEM)
    hbm = pl.BlockSpec(memory_space=pltpu.HBM)
    half = jax.ShapeDtypeStruct((64, 2048), BF)
    return pl.pallas_call(
        far_kernel,
        in_specs=[pl.BlockSpec(memory_space=pltpu.SMEM), vm, vm] + [hbm] * 2,
        out_shape=(half, half, jax.ShapeDtypeStruct((1, 16, 96, 2048), BF)),
        scratch_shapes=[pltpu.SemaphoreType.DMA((1, 2, 8))],
        compiler_params=pltpu.CompilerParams(vmem_limit_bytes=14 << 20),
        name="down_far",
    )(y, *hidden, own, oth)


def down(hidden, weight):
    part = jax.ShapeDtypeStruct((128, 2048), BF)
    return pl.pallas_call(
        down_kernel,
        out_shape=(jax.ShapeDtypeStruct((128, 2048), F32), part, part),
        compiler_params=pltpu.CompilerParams(vmem_limit_bytes=14 << 20),
        name="down",
    )(*hidden, weight)


def pack_kernel(q_ref, k_ref, v_ref, o_ref, out_ref):
    parts = [q_ref[:, :128], q_ref[:, 128:], k_ref[...], v_ref[...], o_ref[...]]
    whole = jnp.concatenate(parts, axis=0).astype(BF)
    for i in range(8):
        out_ref[i] = whole


def pack(q, k, v, o):
    return pl.pallas_call(
        pack_kernel,
        out_shape=jax.ShapeDtypeStruct((8, 768, 128), BF),
        name="pack",
    )(q, k, v, o)


def prep_kernel(y_ref, gate_ref, up_ref, down_ref, p0_ref, p1_ref, p2_ref, p3_ref, g_ref, u_ref):
    g_ref[...] = gate_ref[...].T
    u_ref[...] = up_ref[...].T
    for k, out_ref in enumerate((p0_ref, p1_ref, p2_ref, p3_ref)):
        at = pl.ds(pl.multiple_of(lax.rem(y_ref[0] + k, 4) * 96, 96), 96)
        out_ref[:96] = g_ref[at, :].astype(BF)
        out_ref[96:192] = u_ref[at, :].astype(BF)
        out_ref[192:] = down_ref[at, :].astype(BF)


def prepare(y, gate, up, down):
    vm = pl.BlockSpec(memory_space=pltpu.VMEM)
    return pl.pallas_call(
        prep_kernel,
        in_specs=[pl.BlockSpec(memory_space=pltpu.SMEM)] + [vm] * 3,
        out_shape=[jax.ShapeDtypeStruct((288, 256), BF)] * 4,
        scratch_shapes=[pltpu.VMEM((384, 256), F32), pltpu.VMEM((384, 256), F32)],
        name="prep",
    )(y, gate, up, down)


def join_kernel(p0_ref, p1_ref, p2_ref, p3_ref, out_ref):
    for k, ref in enumerate((p0_ref, p1_ref, p2_ref, p3_ref)):
        out_ref[k] = ref[...]


def join(parts):
    return pl.pallas_call(join_kernel, out_shape=jax.ShapeDtypeStruct((4, 288, 256), BF), name="join")(*parts)


def trade(parts):
    return [parts[0]] + [lax.ppermute(parts[4 - k], "y", ring(4 - k)) for k in (1, 2, 3)]


def per_device(
    tokens,
    doc_ids,
    positions,
    attn_gain,
    mlp_gain,
    q_gain,
    key_norm_gain,
    q_weight,
    key_matrix,
    value_matrix,
    o_weight,
    gate_weight,
    up_weight,
    down_weight,
):
    rows = tokens.shape[0]
    core = lax.axis_index("core").astype(jnp.int32)
    xl = lax.axis_index("xl").astype(jnp.int32)
    y = lax.axis_index("y").astype(jnp.int32)
    hold = lax.optimization_barrier

    packed = pack(q_weight, key_matrix, value_matrix, o_weight)
    at_own = lax.all_to_all(packed, ("z", "xh"), split_axis=0, concat_axis=0, tiled=True)

    parts = trade(prepare(y[None], gate_weight, up_weight, down_weight))
    half = HEAD // 2
    freq = jnp.exp(jnp.arange(half, dtype=F32) * (-2.0 * math.log(1000000.0) / HEAD))
    angle = positions.astype(F32)[:, None] * freq[None, :]
    cs = jnp.concatenate([jnp.cos(angle), jnp.sin(angle)], axis=1)
    group = join(parts)
    cs, at_own, group = hold((cs, at_own, group))
    mlp_own = lax.all_gather(group, ("z", "xh", "xl"), axis=0, tiled=False).reshape(8, 2, 4, 288, 256)
    lo = (jnp.arange(rows, dtype=jnp.int32) - positions)[:, None]

    at_oth = swap(at_own, "core")

    o_own = lax.all_to_all(widen(at_own), "y", split_axis=0, concat_axis=0, tiled=True)

    rows_in = pltpu.with_memory_space_constraint(tokens, pltpu.HBM)
    q, cache, tail = project(core[None], rows_in, at_own, at_oth, attn_gain, q_gain, key_norm_gain, cs)
    prior = lax.ppermute(tail, REQ, [(i - 1, i) for i in range(1, 16)])
    turn = lambda part: lax.all_to_all(part, "y", split_axis=0, concat_axis=0, tiled=True)
    theirs = attend(1 - xl[None], q, cache, prior, lo)
    _, q = hold((theirs, q))
    mine = attend(xl[None], q, cache, prior, lo)
    _, o_own = hold((mine, o_own))
    o_oth = swap(o_own, "core")
    send = out_project(core[None], turn(theirs), o_own, o_oth, BF)
    got = swap(send, "xl")
    _, mine = hold((send, mine))
    keep = out_project(core[None], turn(mine), o_own, o_oth, F32)

    own_rows = lax.dynamic_slice_in_dim(tokens, (xl * 4 + y) * 128, 128, 0).astype(F32)
    resid = (own_rows + (keep + got.astype(F32))).astype(BF)
    resid = hold(resid).astype(F32)
    scale = lax.rsqrt(jnp.mean(resid * resid, axis=-1, keepdims=True) + 1e-06)
    mlp_in = (resid * scale * mlp_gain).astype(BF)

    left = lax.ppermute(mlp_in, "y", ring(1))
    right = lax.ppermute(mlp_in, "y", ring(3))
    mlp_own, left, right = hold((mlp_own, left, right))
    mlp_oth = swap(mlp_own, "core")
    far_top = lax.ppermute(left[:64], "y", ring(1))
    far_bottom = lax.ppermute(right[64:], "y", ring(3))
    pieces = (mlp_in, left, right, far_top, far_bottom)
    mlp_own = pltpu.with_memory_space_constraint(mlp_own, pltpu.HBM)
    first = gate_up(y[None], pieces, mlp_own)
    first, mlp_oth = hold((first, mlp_oth))
    hidden = (first, gate_up(y[None], pieces, mlp_oth))
    top, bottom, weight = down_far(y[None], hidden, mlp_own, mlp_oth)
    via_left = lax.ppermute(top, "y", ring(1))
    via_right = lax.ppermute(bottom, "y", ring(3))
    keep, to_left, to_right = down(hidden, weight)
    via_left, via_right = hold((via_left, via_right))
    to_right = jnp.concatenate([(to_right[:64].astype(F32) + via_left.astype(F32)).astype(BF), to_right[64:]])
    to_left = jnp.concatenate([to_left[:64], (to_left[64:].astype(F32) + via_right.astype(F32)).astype(BF)])
    from_left = lax.ppermute(to_right, "y", ring(1))
    from_right = lax.ppermute(to_left, "y", ring(3))
    total = keep + from_left.astype(F32) + from_right.astype(F32)
    return ((resid + total).astype(BF), cache)


def solution(mesh):
    fine = Mesh(mesh.devices.reshape(4, 2, 2, 2, 4), REQ + MDL)
    rows = P(REQ)
    in_specs = (
        P(REQ, None),
        rows,
        rows,
        P(),
        P(),
        P(),
        P(),
        P(REQ, MDL),
        P(REQ, MDL),
        P(REQ, MDL),
        P(MDL, REQ),
        P(MDL, REQ),
        P(MDL, REQ),
        P(REQ, MDL),
    )
    out_specs = (P(REQ + MDL, None), P(None, REQ, MDL))
    return jax.shard_map(per_device, mesh=fine, in_specs=in_specs, out_specs=out_specs, check_vma=False)
```

```python
import math

import jax
import jax.numpy as jnp
from jax import lax
from jax.experimental import pallas as pl
from jax.experimental.pallas import tpu as pltpu
from jax.sharding import Mesh
from jax.sharding import PartitionSpec as P

HEAD = 128
BF = jnp.bfloat16
F32 = jnp.float32
REQ = ("z", "xh", "core")
MDL = ("xl", "y")


def ring(step):
    return [(i, (i + step) % 4) for i in range(4)]


def swap(block, axis):
    return lax.ppermute(block, axis, [(0, 1), (1, 0)])


def qkv_kernel(core_ref, x_ref, own_ref, oth_ref, gain_ref, qg_ref, kg_ref, cs_ref, q_ref, kv_ref, tail_ref, w_ref):
    core = core_ref[0]

    @pl.when(pl.program_id(0) == 0)
    def _():
        def place(i, carry):
            for src, side in ((own_ref, core), (oth_ref, 1 - core)):
                at = pl.ds(pl.multiple_of((2 * i + side) * 128, 128), 128)
                for k in range(4):
                    w_ref[at, k * 128 : k * 128 + 128] = src[i, k * 128 : k * 128 + 128]
            return carry

        lax.fori_loop(0, 8, place, 0)

    x = x_ref[...].astype(F32)
    scale = lax.rsqrt(jnp.mean(x * x, axis=-1, keepdims=True) + 1e-06)
    normed = (x * scale * gain_ref[...]).astype(BF)
    raw = jnp.dot(normed, w_ref[...], preferred_element_type=F32)
    cs = cs_ref[...]
    turned = pltpu.roll(cs, 64, 1)
    low = lax.broadcasted_iota(jnp.int32, cs.shape, 1) < 64
    cosine = jnp.where(low, cs, turned)
    sine = jnp.where(low, -turned, cs)

    def head(t, gain):
        t = t * lax.rsqrt(jnp.mean(t * t, axis=-1, keepdims=True) + 1e-06) * gain
        return (t * cosine + pltpu.roll(t, 64, 1) * sine).astype(BF)

    q_ref[:, :128] = head(raw[:, :128], qg_ref[...])
    q_ref[:, 128:] = head(raw[:, 128:256], qg_ref[...])
    keys = head(raw[:, 256:384], kg_ref[...])
    values = raw[:, 384:].astype(BF)
    kv_ref[0] = keys
    kv_ref[1] = values

    @pl.when(pl.program_id(0) >= 2)
    def _():
        tail_ref[0] = keys
        tail_ref[1] = values


def project(core, tokens, own, oth, attn_gain, q_gain, key_gain, cs):
    rows = tokens.shape[0]
    tile = 256
    fixed = lambda *shape: pl.BlockSpec(shape, lambda i, c: (0,) * len(shape))
    return pl.pallas_call(
        qkv_kernel,
        grid_spec=pltpu.PrefetchScalarGridSpec(
            num_scalar_prefetch=1,
            grid=(rows // tile,),
            in_specs=[
                pl.BlockSpec((tile, 2048), lambda i, c: (i, 0)),
                fixed(8, 512, 128),
                fixed(8, 512, 128),
                fixed(1, 2048),
                fixed(1, 128),
                fixed(1, 128),
                pl.BlockSpec((tile, 128), lambda i, c: (i, 0)),
            ],
            out_specs=[
                pl.BlockSpec((tile, 256), lambda i, c: (i, 0)),
                pl.BlockSpec((2, tile, 128), lambda i, c: (0, i, 0)),
                pl.BlockSpec((2, tile, 128), lambda i, c: (0, jnp.maximum(i - 2, 0), 0)),
            ],
            scratch_shapes=[pltpu.VMEM((2048, 512), BF)],
        ),
        out_shape=(
            jax.ShapeDtypeStruct((rows, 256), BF),
            jax.ShapeDtypeStruct((2, rows, 128), BF),
            jax.ShapeDtypeStruct((2, rows // 2, 128), BF),
        ),
        compiler_params=pltpu.CompilerParams(vmem_limit_bytes=24 << 20),
        name="qkv",
    )(core, tokens, own, oth, attn_gain[None], q_gain[None], key_gain[None], cs)


def widen_kernel(src_ref, out_ref):
    for k in range(4):
        out_ref[k] = src_ref[...]


def widen(gathered):
    return pl.pallas_call(
        widen_kernel,
        grid=(1,),
        in_specs=[pl.BlockSpec((8, 256, 128), lambda i: (0, 2, 0))],
        out_specs=pl.BlockSpec((4, 8, 256, 128), lambda i: (0, 0, 0, 0)),
        out_shape=jax.ShapeDtypeStruct((4, 8, 256, 128), BF),
        name="widen",
    )(gathered)


def attend_kernel(half_ref, q_ref, kv_ref, prior_ref, lo_ref, out_ref):
    factor = HEAD ** (-0.5) * math.log2(math.e)
    nt = (((1,), (1,)), ((), ()))

    def block(i):
        first = i * 256
        skip = 256 if i == 3 else 0
        count = first + 256
        lo = lo_ref[first : first + 256, :]
        row = lax.broadcasted_iota(jnp.int32, (256, count), 0) + first
        col = lax.broadcasted_iota(jnp.int32, (256, count), 1)
        near = (col >= lo) & (col <= row)
        prior_col = lax.broadcasted_iota(jnp.int32, (256, 512 - skip), 1) + (skip - 512)
        far = prior_col >= lo

        def head(h, carry):
            lanes = pl.ds(pl.multiple_of(h * 128, 128), 128)
            q = q_ref[first : first + 256, lanes]
            s1 = lax.dot_general(q, kv_ref[0, :count], nt, preferred_element_type=F32)
            s0 = lax.dot_general(q, prior_ref[0, skip:], nt, preferred_element_type=F32)
            s1 = jnp.where(near, s1, -1e30)
            s0 = jnp.where(far, s0, -1e30)
            top = jnp.maximum(jnp.max(s1, -1, keepdims=True), jnp.max(s0, -1, keepdims=True))
            e1 = jnp.exp2((s1 - top) * factor)
            e0 = jnp.exp2((s0 - top) * factor)
            inv = 1.0 / (jnp.sum(e1, -1, keepdims=True) + jnp.sum(e0, -1, keepdims=True))
            p1 = (e1 * inv).astype(BF)
            p0 = (e0 * inv).astype(BF)
            o = jnp.dot(p1, kv_ref[1, :count], preferred_element_type=F32)
            o = o + jnp.dot(p0, prior_ref[1, skip:], preferred_element_type=F32)
            o = o.astype(BF)
            for part in range(2):
                out_ref[(2 * i + part) % 4, :, lanes] = o[part * 128 : part * 128 + 128]
            return carry

        lax.fori_loop(0, 2, head, 0)

    @pl.when(half_ref[0] == 0)
    def _():
        block(0)
        block(1)

    @pl.when(half_ref[0] == 1)
    def _():
        block(2)
        block(3)


def attend(half, q, kv, prior, lo):
    vm = pl.BlockSpec(memory_space=pltpu.VMEM)
    return pl.pallas_call(
        attend_kernel,
        in_specs=[pl.BlockSpec(memory_space=pltpu.SMEM)] + [vm] * 4,
        out_shape=jax.ShapeDtypeStruct((4, 128, 256), BF),
        compiler_params=pltpu.CompilerParams(vmem_limit_bytes=20 << 20),
        name="attend",
    )(half, q, kv, prior, lo)


def out_kernel(core_ref, ctx_ref, own_ref, oth_ref, out_ref, w_ref, sems):
    core = core_ref[0]

    def each(act):
        def step(n, carry):
            s, i = n // 8, lax.rem(n, 8)
            for which, (src, side) in enumerate(((own_ref, core), (oth_ref, 1 - core))):
                at = pl.ds(pl.multiple_of((2 * i + side) * 128, 128), 128)
                act(pltpu.make_async_copy(
                    src.at[s, i], w_ref.at[pl.ds(pl.multiple_of(s * 256, 256), 256), at], sems.at[which, s, i]
                ))
            return carry

        lax.fori_loop(0, 32, step, 0)

    each(lambda c: c.start())
    x = jnp.concatenate([ctx_ref[s] for s in range(4)], axis=1)
    each(lambda c: c.wait())

    def column(n, carry):
        at = pl.ds(pl.multiple_of(n * 512, 512), 512)
        out_ref[:, at] = jnp.dot(x, w_ref[:, at], preferred_element_type=F32).astype(out_ref.dtype)
        return carry

    lax.fori_loop(0, 4, column, 0)


def out_project(core, ctx, own, oth, dtype):
    vm = pl.BlockSpec(memory_space=pltpu.VMEM)
    anywhere = pl.BlockSpec(memory_space=pl.ANY)
    return pl.pallas_call(
        out_kernel,
        in_specs=[pl.BlockSpec(memory_space=pltpu.SMEM), vm, anywhere, anywhere],
        out_shape=jax.ShapeDtypeStruct((128, 2048), dtype),
        scratch_shapes=[pltpu.VMEM((1024, 2048), BF), pltpu.SemaphoreType.DMA((2, 4, 8))],
        compiler_params=pltpu.CompilerParams(vmem_limit_bytes=14 << 20),
        name="oproj",
    )(core, ctx, own, oth)


def fetcher(own_ref, oth_ref, w_ref, sems, y, first):
    def copy(c, g, m):
        src = own_ref if c == 0 else oth_ref
        at = pl.multiple_of(((m // 4) * 4 + lax.rem(y + lax.rem(m, 4), 4)) * 256, 256)
        return pltpu.make_async_copy(
            src.at[:, m // 4, lax.rem(m, 4), first + g * 96 : first + g * 96 + 96, :],
            w_ref.at[g, c * 8 : c * 8 + 8, :, pl.ds(at, 256)],
            sems.at[g, c, m],
        )

    def each(c, groups, act):
        def step(m, carry):
            for g in range(groups):
                act(copy(c, g, m))
            return carry

        lax.fori_loop(0, 8, step, 0)

    return each


def gate_kernel(y_ref, x0_ref, x1_ref, x2_ref, x3_ref, x4_ref, src_ref, hid_ref, w_ref, x_ref, sems):
    nt = (((1,), (1,)), ((), ()))
    each = fetcher(src_ref, src_ref, w_ref, sems, y_ref[0], 0)
    each(0, 2, lambda c: c.start())
    x_ref[0:128] = x0_ref[...]
    x_ref[128:256] = x1_ref[...]
    x_ref[256:384] = x2_ref[...]
    x_ref[384:448] = x3_ref[...]
    x_ref[448:512] = x4_ref[...]
    x = x_ref[...]
    each(0, 2, lambda copy: copy.wait())
    gate_w = w_ref[0].reshape(768, 2048)
    up_w = w_ref[1].reshape(768, 2048)
    for t in range(3):
        gate = lax.dot_general(x, gate_w[t * 256 : t * 256 + 256], nt, preferred_element_type=F32)
        upper = lax.dot_general(x, up_w[t * 256 : t * 256 + 256], nt, preferred_element_type=F32)
        hidden = gate / (1.0 + jnp.exp(-gate)) * upper
        hid_ref[:, t * 256 : t * 256 + 256] = hidden.astype(BF)


def far_kernel(y_ref, hid0_ref, hid1_ref, own_ref, oth_ref, top_ref, bottom_ref, w_ref, sems):
    each = fetcher(own_ref, oth_ref, w_ref, sems, y_ref[0], 192)
    for c in range(2):
        each(c, 1, lambda copy: copy.start())
    for c in range(2):
        each(c, 1, lambda copy: copy.wait())
    hid = jnp.concatenate([hid0_ref[384:], hid1_ref[384:]], axis=1)

    def column(n, carry):
        at = pl.ds(pl.multiple_of(n * 512, 512), 512)
        out = jnp.dot(hid, w_ref[0, :, :, at].reshape(1536, 512), preferred_element_type=F32)
        top_ref[:, at] = out[:64].astype(BF)
        bottom_ref[:, at] = out[64:].astype(BF)
        return carry

    lax.fori_loop(0, 4, column, 0)


def down_kernel(hid0_ref, hid1_ref, w_ref, keep_ref, left_ref, right_ref):
    hid = jnp.concatenate([hid0_ref[:384], hid1_ref[:384]], axis=1)

    def column(n, carry):
        at = pl.ds(pl.multiple_of(n * 512, 512), 512)
        out = jnp.dot(hid, w_ref[0, :, :, at].reshape(1536, 512), preferred_element_type=F32)
        keep_ref[:, at] = out[:128]
        left_ref[:, at] = out[128:256].astype(BF)
        right_ref[:, at] = out[256:].astype(BF)
        return carry

    lax.fori_loop(0, 4, column, 0)


def gate_up(y, pieces, src):
    vm = pl.BlockSpec(memory_space=pltpu.VMEM)
    hbm = pl.BlockSpec(memory_space=pltpu.HBM)
    return pl.pallas_call(
        gate_kernel,
        in_specs=[pl.BlockSpec(memory_space=pltpu.SMEM)] + [vm] * 5 + [hbm],
        out_shape=jax.ShapeDtypeStruct((512, 768), BF),
        scratch_shapes=[
            pltpu.VMEM((2, 8, 96, 2048), BF),
            pltpu.VMEM((512, 2048), BF),
            pltpu.SemaphoreType.DMA((2, 1, 8)),
        ],
        compiler_params=pltpu.CompilerParams(vmem_limit_bytes=18 << 20),
        name="gate_up",
    )(y, *pieces, src)


def down_far(y, hidden, own, oth):
    vm = pl.BlockSpec(memory_space=pltpu.VMEM)
    hbm = pl.BlockSpec(memory_space=pltpu.HBM)
    half = jax.ShapeDtypeStruct((64, 2048), BF)
    return pl.pallas_call(
        far_kernel,
        in_specs=[pl.BlockSpec(memory_space=pltpu.SMEM), vm, vm] + [hbm] * 2,
        out_shape=(half, half, jax.ShapeDtypeStruct((1, 16, 96, 2048), BF)),
        scratch_shapes=[pltpu.SemaphoreType.DMA((1, 2, 8))],
        compiler_params=pltpu.CompilerParams(vmem_limit_bytes=14 << 20),
        name="down_far",
    )(y, *hidden, own, oth)


def down(hidden, weight):
    part = jax.ShapeDtypeStruct((128, 2048), BF)
    return pl.pallas_call(
        down_kernel,
        out_shape=(jax.ShapeDtypeStruct((128, 2048), F32), part, part),
        compiler_params=pltpu.CompilerParams(vmem_limit_bytes=14 << 20),
        name="down",
    )(*hidden, weight)


def pack_kernel(q_ref, k_ref, v_ref, o_ref, out_ref):
    parts = [q_ref[:, :128], q_ref[:, 128:], k_ref[...], v_ref[...], o_ref[...]]
    whole = jnp.concatenate(parts, axis=0).astype(BF)
    for i in range(8):
        out_ref[i] = whole


def pack(q, k, v, o):
    return pl.pallas_call(
        pack_kernel,
        out_shape=jax.ShapeDtypeStruct((8, 768, 128), BF),
        name="pack",
    )(q, k, v, o)


def prep_kernel(y_ref, gate_ref, up_ref, down_ref, p0_ref, p1_ref, p2_ref, p3_ref, g_ref, u_ref):
    g_ref[...] = gate_ref[...].T
    u_ref[...] = up_ref[...].T
    for k, out_ref in enumerate((p0_ref, p1_ref, p2_ref, p3_ref)):
        at = pl.ds(pl.multiple_of(lax.rem(y_ref[0] + k, 4) * 96, 96), 96)
        out_ref[:96] = g_ref[at, :].astype(BF)
        out_ref[96:192] = u_ref[at, :].astype(BF)
        out_ref[192:] = down_ref[at, :].astype(BF)


def prepare(y, gate, up, down):
    vm = pl.BlockSpec(memory_space=pltpu.VMEM)
    return pl.pallas_call(
        prep_kernel,
        in_specs=[pl.BlockSpec(memory_space=pltpu.SMEM)] + [vm] * 3,
        out_shape=[jax.ShapeDtypeStruct((288, 256), BF)] * 4,
        scratch_shapes=[pltpu.VMEM((384, 256), F32), pltpu.VMEM((384, 256), F32)],
        name="prep",
    )(y, gate, up, down)


def join_kernel(p0_ref, p1_ref, p2_ref, p3_ref, out_ref):
    for k, ref in enumerate((p0_ref, p1_ref, p2_ref, p3_ref)):
        out_ref[k] = ref[...]


def join(parts):
    return pl.pallas_call(join_kernel, out_shape=jax.ShapeDtypeStruct((4, 288, 256), BF), name="join")(*parts)


def trade(parts):
    return [parts[0]] + [lax.ppermute(parts[4 - k], "y", ring(4 - k)) for k in (1, 2, 3)]


def per_device(
    tokens,
    doc_ids,
    positions,
    attn_gain,
    mlp_gain,
    q_gain,
    key_norm_gain,
    q_weight,
    key_matrix,
    value_matrix,
    o_weight,
    gate_weight,
    up_weight,
    down_weight,
):
    rows = tokens.shape[0]
    core = lax.axis_index("core").astype(jnp.int32)
    xl = lax.axis_index("xl").astype(jnp.int32)
    y = lax.axis_index("y").astype(jnp.int32)
    hold = lax.optimization_barrier

    packed = pack(q_weight, key_matrix, value_matrix, o_weight)
    at_own = lax.all_to_all(packed, ("z", "xh"), split_axis=0, concat_axis=0, tiled=True)

    parts = trade(prepare(y[None], gate_weight, up_weight, down_weight))
    half = HEAD // 2
    freq = jnp.exp(jnp.arange(half, dtype=F32) * (-2.0 * math.log(1000000.0) / HEAD))
    angle = positions.astype(F32)[:, None] * freq[None, :]
    cs = jnp.concatenate([jnp.cos(angle), jnp.sin(angle)], axis=1)
    group = join(parts)
    cs, at_own, group = hold((cs, at_own, group))
    mlp_own = lax.all_gather(group, ("z", "xh", "xl"), axis=0, tiled=False).reshape(8, 2, 4, 288, 256)
    lo = (jnp.arange(rows, dtype=jnp.int32) - positions)[:, None]

    at_oth = swap(at_own, "core")

    o_own = lax.all_to_all(widen(at_own), "y", split_axis=0, concat_axis=0, tiled=True)

    rows_in = pltpu.with_memory_space_constraint(tokens, pltpu.HBM)
    q, cache, tail = project(core[None], rows_in, at_own, at_oth, attn_gain, q_gain, key_norm_gain, cs)
    prior = lax.ppermute(tail, REQ, [(i - 1, i) for i in range(1, 16)])
    turn = lambda part: lax.all_to_all(part, "y", split_axis=0, concat_axis=0, tiled=True)
    theirs = attend(1 - xl[None], q, cache, prior, lo)
    _, q = hold((theirs, q))
    mine = attend(xl[None], q, cache, prior, lo)
    _, o_own = hold((mine, o_own))
    o_oth = swap(o_own, "core")
    send = out_project(core[None], turn(theirs), o_own, o_oth, BF)
    got = swap(send, "xl")
    _, mine = hold((send, mine))
    keep = out_project(core[None], turn(mine), o_own, o_oth, F32)

    own_rows = lax.dynamic_slice_in_dim(tokens, (xl * 4 + y) * 128, 128, 0).astype(F32)
    resid = (own_rows + (keep + got.astype(F32))).astype(BF)
    resid = hold(resid).astype(F32)
    scale = lax.rsqrt(jnp.mean(resid * resid, axis=-1, keepdims=True) + 1e-06)
    mlp_in = (resid * scale * mlp_gain).astype(BF)

    left = lax.ppermute(mlp_in, "y", ring(1))
    right = lax.ppermute(mlp_in, "y", ring(3))
    mlp_own, left, right = hold((mlp_own, left, right))
    mlp_oth = swap(mlp_own, "core")
    far_top = lax.ppermute(left[:64], "y", ring(1))
    far_bottom = lax.ppermute(right[64:], "y", ring(3))
    pieces = (mlp_in, left, right, far_top, far_bottom)
    mlp_own = pltpu.with_memory_space_constraint(mlp_own, pltpu.HBM)
    first = gate_up(y[None], pieces, mlp_own)
    first, mlp_oth = hold((first, mlp_oth))
    hidden = (first, gate_up(y[None], pieces, mlp_oth))
    top, bottom, weight = down_far(y[None], hidden, mlp_own, mlp_oth)
    via_left = lax.ppermute(top, "y", ring(1))
    via_right = lax.ppermute(bottom, "y", ring(3))
    keep, to_left, to_right = down(hidden, weight)
    via_left, via_right = hold((via_left, via_right))
    to_right = jnp.concatenate([(to_right[:64].astype(F32) + via_left.astype(F32)).astype(BF), to_right[64:]])
    to_left = jnp.concatenate([to_left[:64], (to_left[64:].astype(F32) + via_right.astype(F32)).astype(BF)])
    from_left = lax.ppermute(to_right, "y", ring(1))
    from_right = lax.ppermute(to_left, "y", ring(3))
    total = keep + from_left.astype(F32) + from_right.astype(F32)
    return ((resid + total).astype(BF), cache)


def solution(mesh):
    fine = Mesh(mesh.devices.reshape(4, 2, 2, 2, 4), REQ + MDL)
    rows = P(REQ)
    in_specs = (
        P(REQ, None),
        rows,
        rows,
        P(),
        P(),
        P(),
        P(),
        P(REQ, MDL),
        P(REQ, MDL),
        P(REQ, MDL),
        P(MDL, REQ),
        P(MDL, REQ),
        P(MDL, REQ),
        P(REQ, MDL),
    )
    out_specs = (P(REQ + MDL, None), P(None, REQ, MDL))
    return jax.shard_map(per_device, mesh=fine, in_specs=in_specs, out_specs=out_specs, check_vma=False)
```

```python
import math

import jax
import jax.numpy as jnp
from jax import lax
from jax.experimental import pallas as pl
from jax.experimental.pallas import tpu as pltpu
from jax.sharding import Mesh
from jax.sharding import PartitionSpec as P

HEAD = 128
BF = jnp.bfloat16
F32 = jnp.float32
REQ = ("z", "xh", "core")
MDL = ("xl", "y")


def ring(step):
    return [(i, (i + step) % 4) for i in range(4)]


def swap(block, axis):
    return lax.ppermute(block, axis, [(0, 1), (1, 0)])


def norm_kernel(x_ref, gain_ref, out_ref):
    x = x_ref[...].astype(F32)
    scale = lax.rsqrt(jnp.mean(x * x, axis=-1, keepdims=True) + 1e-06)
    out_ref[...] = (x * scale * gain_ref[...]).astype(BF)


def normalise(x, gain):
    block = pl.BlockSpec((256, 2048), lambda i: (i, 0))
    return pl.pallas_call(
        norm_kernel,
        grid=(x.shape[0] // 256,),
        in_specs=[block, pl.BlockSpec((1, 2048), lambda i: (0, 0))],
        out_specs=block,
        out_shape=jax.ShapeDtypeStruct(x.shape, BF),
        name="norm",
    )(x, gain[None])


def qkv_kernel(core_ref, x_ref, own_ref, oth_ref, qg_ref, kg_ref, cs_ref, q_ref, kv_ref, tail_ref, w_ref):
    core = core_ref[0]

    @pl.when(pl.program_id(0) == 0)
    def _():
        def place(i, carry):
            for src, side in ((own_ref, core), (oth_ref, 1 - core)):
                at = pl.ds(pl.multiple_of((2 * i + side) * 128, 128), 128)
                for k in range(4):
                    w_ref[at, k * 128 : k * 128 + 128] = src[i, k * 128 : k * 128 + 128]
            return carry

        lax.fori_loop(0, 8, place, 0)

    raw = jnp.dot(x_ref[...], w_ref[...], preferred_element_type=F32)
    cs = cs_ref[...]
    turned = pltpu.roll(cs, 64, 1)
    low = lax.broadcasted_iota(jnp.int32, cs.shape, 1) < 64
    cosine = jnp.where(low, cs, turned)
    sine = jnp.where(low, -turned, cs)

    def head(t, gain):
        t = t * lax.rsqrt(jnp.mean(t * t, axis=-1, keepdims=True) + 1e-06) * gain
        return (t * cosine + pltpu.roll(t, 64, 1) * sine).astype(BF)

    q_ref[:, :128] = head(raw[:, :128], qg_ref[...])
    q_ref[:, 128:] = head(raw[:, 128:256], qg_ref[...])
    keys = head(raw[:, 256:384], kg_ref[...])
    values = raw[:, 384:].astype(BF)
    kv_ref[0] = keys
    kv_ref[1] = values

    @pl.when(pl.program_id(0) >= 2)
    def _():
        tail_ref[0] = keys
        tail_ref[1] = values


def project(core, normed, own, oth, q_gain, key_gain, cs):
    rows = normed.shape[0]
    tile = 256
    fixed = lambda *shape: pl.BlockSpec(shape, lambda i, c: (0,) * len(shape))
    return pl.pallas_call(
        qkv_kernel,
        grid_spec=pltpu.PrefetchScalarGridSpec(
            num_scalar_prefetch=1,
            grid=(rows // tile,),
            in_specs=[
                pl.BlockSpec((tile, 2048), lambda i, c: (i, 0)),
                fixed(8, 512, 128),
                fixed(8, 512, 128),
                fixed(1, 128),
                fixed(1, 128),
                pl.BlockSpec((tile, 128), lambda i, c: (i, 0)),
            ],
            out_specs=[
                pl.BlockSpec((tile, 256), lambda i, c: (i, 0)),
                pl.BlockSpec((2, tile, 128), lambda i, c: (0, i, 0)),
                pl.BlockSpec((2, tile, 128), lambda i, c: (0, jnp.maximum(i - 2, 0), 0)),
            ],
            scratch_shapes=[pltpu.VMEM((2048, 512), BF)],
        ),
        out_shape=(
            jax.ShapeDtypeStruct((rows, 256), BF),
            jax.ShapeDtypeStruct((2, rows, 128), BF),
            jax.ShapeDtypeStruct((2, rows // 2, 128), BF),
        ),
        compiler_params=pltpu.CompilerParams(vmem_limit_bytes=24 << 20),
        name="qkv",
    )(core, normed, own, oth, q_gain[None], key_gain[None], cs)


def widen_kernel(src_ref, out_ref):
    for k in range(4):
        out_ref[k] = src_ref[...]


def widen(gathered):
    return pl.pallas_call(
        widen_kernel,
        grid=(1,),
        in_specs=[pl.BlockSpec((8, 256, 128), lambda i: (0, 2, 0))],
        out_specs=pl.BlockSpec((4, 8, 256, 128), lambda i: (0, 0, 0, 0)),
        out_shape=jax.ShapeDtypeStruct((4, 8, 256, 128), BF),
        name="widen",
    )(gathered)


def attend_kernel(half_ref, q_ref, kv_ref, prior_ref, lo_ref, out_ref):
    factor = HEAD ** (-0.5) * math.log2(math.e)
    nt = (((1,), (1,)), ((), ()))

    def block(i):
        first = i * 256
        skip = 256 if i == 3 else 0
        count = first + 256
        lo = lo_ref[first : first + 256, :]
        row = lax.broadcasted_iota(jnp.int32, (256, count), 0) + first
        col = lax.broadcasted_iota(jnp.int32, (256, count), 1)
        near = (col >= lo) & (col <= row)
        prior_col = lax.broadcasted_iota(jnp.int32, (256, 512 - skip), 1) + (skip - 512)
        far = prior_col >= lo

        def head(h, carry):
            lanes = pl.ds(pl.multiple_of(h * 128, 128), 128)
            q = q_ref[first : first + 256, lanes]
            s1 = lax.dot_general(q, kv_ref[0, :count], nt, preferred_element_type=F32)
            s0 = lax.dot_general(q, prior_ref[0, skip:], nt, preferred_element_type=F32)
            s1 = jnp.where(near, s1, -1e30)
            s0 = jnp.where(far, s0, -1e30)
            top = jnp.maximum(jnp.max(s1, -1, keepdims=True), jnp.max(s0, -1, keepdims=True))
            e1 = jnp.exp2((s1 - top) * factor)
            e0 = jnp.exp2((s0 - top) * factor)
            inv = 1.0 / (jnp.sum(e1, -1, keepdims=True) + jnp.sum(e0, -1, keepdims=True))
            p1 = (e1 * inv).astype(BF)
            p0 = (e0 * inv).astype(BF)
            o = jnp.dot(p1, kv_ref[1, :count], preferred_element_type=F32)
            o = o + jnp.dot(p0, prior_ref[1, skip:], preferred_element_type=F32)
            o = o.astype(BF)
            for part in range(2):
                out_ref[(2 * i + part) % 4, :, lanes] = o[part * 128 : part * 128 + 128]
            return carry

        lax.fori_loop(0, 2, head, 0)

    @pl.when(half_ref[0] == 0)
    def _():
        block(0)
        block(1)

    @pl.when(half_ref[0] == 1)
    def _():
        block(2)
        block(3)


def attend(half, q, kv, prior, lo):
    vm = pl.BlockSpec(memory_space=pltpu.VMEM)
    return pl.pallas_call(
        attend_kernel,
        in_specs=[pl.BlockSpec(memory_space=pltpu.SMEM)] + [vm] * 4,
        out_shape=jax.ShapeDtypeStruct((4, 128, 256), BF),
        compiler_params=pltpu.CompilerParams(vmem_limit_bytes=20 << 20),
        name="attend",
    )(half, q, kv, prior, lo)


def out_kernel(core_ref, ctx_ref, own_ref, oth_ref, out_ref, w_ref, sems):
    core = core_ref[0]

    def each(act):
        def step(n, carry):
            s, i = n // 8, lax.rem(n, 8)
            for which, (src, side) in enumerate(((own_ref, core), (oth_ref, 1 - core))):
                at = pl.ds(pl.multiple_of((2 * i + side) * 128, 128), 128)
                act(pltpu.make_async_copy(
                    src.at[s, i], w_ref.at[pl.ds(pl.multiple_of(s * 256, 256), 256), at], sems.at[which, s, i]
                ))
            return carry

        lax.fori_loop(0, 32, step, 0)

    each(lambda c: c.start())
    x = jnp.concatenate([ctx_ref[s] for s in range(4)], axis=1)
    each(lambda c: c.wait())

    def column(n, carry):
        at = pl.ds(pl.multiple_of(n * 512, 512), 512)
        out_ref[:, at] = jnp.dot(x, w_ref[:, at], preferred_element_type=F32).astype(out_ref.dtype)
        return carry

    lax.fori_loop(0, 4, column, 0)


def out_project(core, ctx, own, oth, dtype):
    vm = pl.BlockSpec(memory_space=pltpu.VMEM)
    anywhere = pl.BlockSpec(memory_space=pl.ANY)
    return pl.pallas_call(
        out_kernel,
        in_specs=[pl.BlockSpec(memory_space=pltpu.SMEM), vm, anywhere, anywhere],
        out_shape=jax.ShapeDtypeStruct((128, 2048), dtype),
        scratch_shapes=[pltpu.VMEM((1024, 2048), BF), pltpu.SemaphoreType.DMA((2, 4, 8))],
        compiler_params=pltpu.CompilerParams(vmem_limit_bytes=14 << 20),
        name="oproj",
    )(core, ctx, own, oth)


def fetcher(own_ref, oth_ref, w_ref, sems, y, first):
    def copy(c, g, m):
        src = own_ref if c == 0 else oth_ref
        at = pl.multiple_of(((m // 4) * 4 + lax.rem(y + lax.rem(m, 4), 4)) * 256, 256)
        return pltpu.make_async_copy(
            src.at[:, m // 4, lax.rem(m, 4), first + g * 96 : first + g * 96 + 96, :],
            w_ref.at[g, c * 8 : c * 8 + 8, :, pl.ds(at, 256)],
            sems.at[g, c, m],
        )

    def each(c, groups, act):
        def step(m, carry):
            for g in range(groups):
                act(copy(c, g, m))
            return carry

        lax.fori_loop(0, 8, step, 0)

    return each


def gate_kernel(y_ref, x0_ref, x1_ref, x2_ref, x3_ref, x4_ref, src_ref, hid_ref, w_ref, x_ref, sems):
    nt = (((1,), (1,)), ((), ()))
    each = fetcher(src_ref, src_ref, w_ref, sems, y_ref[0], 0)
    each(0, 2, lambda c: c.start())
    x_ref[0:128] = x0_ref[...]
    x_ref[128:256] = x1_ref[...]
    x_ref[256:384] = x2_ref[...]
    x_ref[384:448] = x3_ref[...]
    x_ref[448:512] = x4_ref[...]
    x = x_ref[...]
    each(0, 2, lambda copy: copy.wait())
    gate_w = w_ref[0].reshape(768, 2048)
    up_w = w_ref[1].reshape(768, 2048)
    for t in range(3):
        gate = lax.dot_general(x, gate_w[t * 256 : t * 256 + 256], nt, preferred_element_type=F32)
        upper = lax.dot_general(x, up_w[t * 256 : t * 256 + 256], nt, preferred_element_type=F32)
        hidden = gate / (1.0 + jnp.exp(-gate)) * upper
        hid_ref[:, t * 256 : t * 256 + 256] = hidden.astype(BF)


def far_kernel(y_ref, hid0_ref, hid1_ref, own_ref, oth_ref, top_ref, bottom_ref, w_ref, sems):
    each = fetcher(own_ref, oth_ref, w_ref, sems, y_ref[0], 192)
    for c in range(2):
        each(c, 1, lambda copy: copy.start())
    for c in range(2):
        each(c, 1, lambda copy: copy.wait())
    hid = jnp.concatenate([hid0_ref[384:], hid1_ref[384:]], axis=1)

    def column(n, carry):
        at = pl.ds(pl.multiple_of(n * 512, 512), 512)
        out = jnp.dot(hid, w_ref[0, :, :, at].reshape(1536, 512), preferred_element_type=F32)
        top_ref[:, at] = out[:64].astype(BF)
        bottom_ref[:, at] = out[64:].astype(BF)
        return carry

    lax.fori_loop(0, 4, column, 0)


def down_kernel(hid0_ref, hid1_ref, w_ref, keep_ref, left_ref, right_ref):
    hid = jnp.concatenate([hid0_ref[:384], hid1_ref[:384]], axis=1)

    def column(n, carry):
        at = pl.ds(pl.multiple_of(n * 512, 512), 512)
        out = jnp.dot(hid, w_ref[0, :, :, at].reshape(1536, 512), preferred_element_type=F32)
        keep_ref[:, at] = out[:128]
        left_ref[:, at] = out[128:256].astype(BF)
        right_ref[:, at] = out[256:].astype(BF)
        return carry

    lax.fori_loop(0, 4, column, 0)


def gate_up(y, pieces, src):
    vm = pl.BlockSpec(memory_space=pltpu.VMEM)
    hbm = pl.BlockSpec(memory_space=pltpu.HBM)
    return pl.pallas_call(
        gate_kernel,
        in_specs=[pl.BlockSpec(memory_space=pltpu.SMEM)] + [vm] * 5 + [hbm],
        out_shape=jax.ShapeDtypeStruct((512, 768), BF),
        scratch_shapes=[
            pltpu.VMEM((2, 8, 96, 2048), BF),
            pltpu.VMEM((512, 2048), BF),
            pltpu.SemaphoreType.DMA((2, 1, 8)),
        ],
        compiler_params=pltpu.CompilerParams(vmem_limit_bytes=18 << 20),
        name="gate_up",
    )(y, *pieces, src)


def down_far(y, hidden, own, oth):
    vm = pl.BlockSpec(memory_space=pltpu.VMEM)
    hbm = pl.BlockSpec(memory_space=pltpu.HBM)
    half = jax.ShapeDtypeStruct((64, 2048), BF)
    return pl.pallas_call(
        far_kernel,
        in_specs=[pl.BlockSpec(memory_space=pltpu.SMEM), vm, vm] + [hbm] * 2,
        out_shape=(half, half, jax.ShapeDtypeStruct((1, 16, 96, 2048), BF)),
        scratch_shapes=[pltpu.SemaphoreType.DMA((1, 2, 8))],
        compiler_params=pltpu.CompilerParams(vmem_limit_bytes=14 << 20),
        name="down_far",
    )(y, *hidden, own, oth)


def down(hidden, weight):
    part = jax.ShapeDtypeStruct((128, 2048), BF)
    return pl.pallas_call(
        down_kernel,
        out_shape=(jax.ShapeDtypeStruct((128, 2048), F32), part, part),
        compiler_params=pltpu.CompilerParams(vmem_limit_bytes=14 << 20),
        name="down",
    )(*hidden, weight)


def pack_kernel(q_ref, k_ref, v_ref, o_ref, out_ref):
    parts = [q_ref[:, :128], q_ref[:, 128:], k_ref[...], v_ref[...], o_ref[...]]
    whole = jnp.concatenate(parts, axis=0).astype(BF)
    for i in range(8):
        out_ref[i] = whole


def pack(q, k, v, o):
    return pl.pallas_call(
        pack_kernel,
        out_shape=jax.ShapeDtypeStruct((8, 768, 128), BF),
        name="pack",
    )(q, k, v, o)


def prep_kernel(y_ref, gate_ref, up_ref, down_ref, p0_ref, p1_ref, p2_ref, p3_ref, g_ref, u_ref):
    g_ref[...] = gate_ref[...].T
    u_ref[...] = up_ref[...].T
    for k, out_ref in enumerate((p0_ref, p1_ref, p2_ref, p3_ref)):
        at = pl.ds(pl.multiple_of(lax.rem(y_ref[0] + k, 4) * 96, 96), 96)
        out_ref[:96] = g_ref[at, :].astype(BF)
        out_ref[96:192] = u_ref[at, :].astype(BF)
        out_ref[192:] = down_ref[at, :].astype(BF)


def prepare(y, gate, up, down):
    vm = pl.BlockSpec(memory_space=pltpu.VMEM)
    return pl.pallas_call(
        prep_kernel,
        in_specs=[pl.BlockSpec(memory_space=pltpu.SMEM)] + [vm] * 3,
        out_shape=[jax.ShapeDtypeStruct((288, 256), BF)] * 4,
        scratch_shapes=[pltpu.VMEM((384, 256), F32), pltpu.VMEM((384, 256), F32)],
        name="prep",
    )(y, gate, up, down)


def join_kernel(p0_ref, p1_ref, p2_ref, p3_ref, out_ref):
    for k, ref in enumerate((p0_ref, p1_ref, p2_ref, p3_ref)):
        out_ref[k] = ref[...]


def join(parts):
    return pl.pallas_call(join_kernel, out_shape=jax.ShapeDtypeStruct((4, 288, 256), BF), name="join")(*parts)


def trade(parts):
    return [parts[0]] + [lax.ppermute(parts[4 - k], "y", ring(4 - k)) for k in (1, 2, 3)]


def per_device(
    tokens,
    doc_ids,
    positions,
    attn_gain,
    mlp_gain,
    q_gain,
    key_norm_gain,
    q_weight,
    key_matrix,
    value_matrix,
    o_weight,
    gate_weight,
    up_weight,
    down_weight,
):
    rows = tokens.shape[0]
    core = lax.axis_index("core").astype(jnp.int32)
    xl = lax.axis_index("xl").astype(jnp.int32)
    y = lax.axis_index("y").astype(jnp.int32)
    hold = lax.optimization_barrier

    packed = pack(q_weight, key_matrix, value_matrix, o_weight)
    at_own = lax.all_to_all(packed, ("z", "xh"), split_axis=0, concat_axis=0, tiled=True)

    parts = trade(prepare(y[None], gate_weight, up_weight, down_weight))
    half = HEAD // 2
    freq = jnp.exp(jnp.arange(half, dtype=F32) * (-2.0 * math.log(1000000.0) / HEAD))
    angle = positions.astype(F32)[:, None] * freq[None, :]
    cs = jnp.concatenate([jnp.cos(angle), jnp.sin(angle)], axis=1)
    group = join(parts)
    normed = normalise(tokens, attn_gain)
    cs, normed, at_own, group = hold((cs, normed, at_own, group))
    mlp_own = lax.all_gather(group, ("z", "xh", "xl"), axis=0, tiled=False).reshape(8, 2, 4, 288, 256)
    lo = (jnp.arange(rows, dtype=jnp.int32) - positions)[:, None]

    at_oth = swap(at_own, "core")

    o_own = lax.all_to_all(widen(at_own), "y", split_axis=0, concat_axis=0, tiled=True)

    normed = pltpu.with_memory_space_constraint(normed, pltpu.HBM)
    q, cache, tail = project(core[None], normed, at_own, at_oth, q_gain, key_norm_gain, cs)
    prior = lax.ppermute(tail, REQ, [(i - 1, i) for i in range(1, 16)])
    turn = lambda part: lax.all_to_all(part, "y", split_axis=0, concat_axis=0, tiled=True)
    theirs = attend(1 - xl[None], q, cache, prior, lo)
    _, q = hold((theirs, q))
    mine = attend(xl[None], q, cache, prior, lo)
    _, o_own = hold((mine, o_own))
    o_oth = swap(o_own, "core")
    send = out_project(core[None], turn(theirs), o_own, o_oth, BF)
    got = swap(send, "xl")
    _, mine = hold((send, mine))
    keep = out_project(core[None], turn(mine), o_own, o_oth, F32)

    own_rows = lax.dynamic_slice_in_dim(tokens, (xl * 4 + y) * 128, 128, 0).astype(F32)
    resid = (own_rows + (keep + got.astype(F32))).astype(BF)
    resid = hold(resid).astype(F32)
    scale = lax.rsqrt(jnp.mean(resid * resid, axis=-1, keepdims=True) + 1e-06)
    mlp_in = (resid * scale * mlp_gain).astype(BF)

    left = lax.ppermute(mlp_in, "y", ring(1))
    right = lax.ppermute(mlp_in, "y", ring(3))
    mlp_own, left, right = hold((mlp_own, left, right))
    mlp_oth = swap(mlp_own, "core")
    far_top = lax.ppermute(left[:64], "y", ring(1))
    far_bottom = lax.ppermute(right[64:], "y", ring(3))
    pieces = (mlp_in, left, right, far_top, far_bottom)
    mlp_own = pltpu.with_memory_space_constraint(mlp_own, pltpu.HBM)
    first = gate_up(y[None], pieces, mlp_own)
    first, mlp_oth = hold((first, mlp_oth))
    hidden = (first, gate_up(y[None], pieces, mlp_oth))
    top, bottom, weight = down_far(y[None], hidden, mlp_own, mlp_oth)
    via_left = lax.ppermute(top, "y", ring(1))
    via_right = lax.ppermute(bottom, "y", ring(3))
    keep, to_left, to_right = down(hidden, weight)
    via_left, via_right = hold((via_left, via_right))
    to_right = jnp.concatenate([(to_right[:64].astype(F32) + via_left.astype(F32)).astype(BF), to_right[64:]])
    to_left = jnp.concatenate([to_left[:64], (to_left[64:].astype(F32) + via_right.astype(F32)).astype(BF)])
    from_left = lax.ppermute(to_right, "y", ring(1))
    from_right = lax.ppermute(to_left, "y", ring(3))
    total = keep + from_left.astype(F32) + from_right.astype(F32)
    return ((resid + total).astype(BF), cache)


def solution(mesh):
    fine = Mesh(mesh.devices.reshape(4, 2, 2, 2, 4), REQ + MDL)
    rows = P(REQ)
    in_specs = (
        P(REQ, None),
        rows,
        rows,
        P(),
        P(),
        P(),
        P(),
        P(REQ, MDL),
        P(REQ, MDL),
        P(REQ, MDL),
        P(MDL, REQ),
        P(MDL, REQ),
        P(MDL, REQ),
        P(REQ, MDL),
    )
    out_specs = (P(REQ + MDL, None), P(None, REQ, MDL))
    return jax.shard_map(per_device, mesh=fine, in_specs=in_specs, out_specs=out_specs, check_vma=False)
```

```python
import math

import jax
import jax.numpy as jnp
from jax import lax
from jax.experimental import pallas as pl
from jax.experimental.pallas import tpu as pltpu
from jax.sharding import Mesh
from jax.sharding import PartitionSpec as P

HEAD = 128
BF = jnp.bfloat16
F32 = jnp.float32
REQ = ("z", "xh", "core")
MDL = ("xl", "y")


def ring(step):
    return [(i, (i + step) % 4) for i in range(4)]


def swap(block, axis):
    return lax.ppermute(block, axis, [(0, 1), (1, 0)])


def qkv_kernel(core_ref, x_ref, own_ref, oth_ref, gain_ref, qg_ref, kg_ref, cs_ref, q_ref, kv_ref, tail_ref, w_ref):
    core = core_ref[0]

    @pl.when(pl.program_id(0) == 0)
    def _():
        def place(i, carry):
            for src, side in ((own_ref, core), (oth_ref, 1 - core)):
                at = pl.ds(pl.multiple_of((2 * i + side) * 128, 128), 128)
                for k in range(4):
                    w_ref[at, k * 128 : k * 128 + 128] = src[i, k * 128 : k * 128 + 128]
            return carry

        lax.fori_loop(0, 8, place, 0)

    x = x_ref[...].astype(F32)
    scale = lax.rsqrt(jnp.mean(x * x, axis=-1, keepdims=True) + 1e-06)
    normed = (x * scale * gain_ref[...]).astype(BF)
    raw = jnp.dot(normed, w_ref[...], preferred_element_type=F32)
    cs = cs_ref[...]
    turned = pltpu.roll(cs, 64, 1)
    low = lax.broadcasted_iota(jnp.int32, cs.shape, 1) < 64
    cosine = jnp.where(low, cs, turned)
    sine = jnp.where(low, -turned, cs)

    def head(t, gain):
        t = t * lax.rsqrt(jnp.mean(t * t, axis=-1, keepdims=True) + 1e-06) * gain
        return (t * cosine + pltpu.roll(t, 64, 1) * sine).astype(BF)

    q_ref[:, :128] = head(raw[:, :128], qg_ref[...])
    q_ref[:, 128:] = head(raw[:, 128:256], qg_ref[...])
    keys = head(raw[:, 256:384], kg_ref[...])
    values = raw[:, 384:].astype(BF)
    kv_ref[0] = keys
    kv_ref[1] = values

    @pl.when(pl.program_id(0) >= 2)
    def _():
        tail_ref[0] = keys
        tail_ref[1] = values


def project(core, tokens, own, oth, attn_gain, q_gain, key_gain, cs):
    rows = tokens.shape[0]
    tile = 256
    fixed = lambda *shape: pl.BlockSpec(shape, lambda i, c: (0,) * len(shape))
    return pl.pallas_call(
        qkv_kernel,
        grid_spec=pltpu.PrefetchScalarGridSpec(
            num_scalar_prefetch=1,
            grid=(rows // tile,),
            in_specs=[
                pl.BlockSpec((tile, 2048), lambda i, c: (i, 0)),
                fixed(8, 512, 128),
                fixed(8, 512, 128),
                fixed(1, 2048),
                fixed(1, 128),
                fixed(1, 128),
                pl.BlockSpec((tile, 128), lambda i, c: (i, 0)),
            ],
            out_specs=[
                pl.BlockSpec((tile, 256), lambda i, c: (i, 0)),
                pl.BlockSpec((2, tile, 128), lambda i, c: (0, i, 0)),
                pl.BlockSpec((2, tile, 128), lambda i, c: (0, jnp.maximum(i - 2, 0), 0)),
            ],
            scratch_shapes=[pltpu.VMEM((2048, 512), BF)],
        ),
        out_shape=(
            jax.ShapeDtypeStruct((rows, 256), BF),
            jax.ShapeDtypeStruct((2, rows, 128), BF),
            jax.ShapeDtypeStruct((2, rows // 2, 128), BF),
        ),
        compiler_params=pltpu.CompilerParams(vmem_limit_bytes=24 << 20),
        name="qkv",
    )(core, tokens, own, oth, attn_gain[None], q_gain[None], key_gain[None], cs)


def widen_kernel(src_ref, out_ref):
    for k in range(4):
        out_ref[k] = src_ref[...]


def widen(gathered):
    return pl.pallas_call(
        widen_kernel,
        grid=(1,),
        in_specs=[pl.BlockSpec((8, 256, 128), lambda i: (0, 2, 0))],
        out_specs=pl.BlockSpec((4, 8, 256, 128), lambda i: (0, 0, 0, 0)),
        out_shape=jax.ShapeDtypeStruct((4, 8, 256, 128), BF),
        name="widen",
    )(gathered)


def attend_kernel(half_ref, q_ref, kv_ref, prior_ref, lo_ref, out_ref):
    factor = HEAD ** (-0.5) * math.log2(math.e)
    nt = (((1,), (1,)), ((), ()))

    def block(i):
        first = i * 256
        skip = 256 if i == 3 else 0
        count = first + 256
        lo = lo_ref[first : first + 256, :]
        row = lax.broadcasted_iota(jnp.int32, (256, count), 0) + first
        col = lax.broadcasted_iota(jnp.int32, (256, count), 1)
        near = (col >= lo) & (col <= row)
        prior_col = lax.broadcasted_iota(jnp.int32, (256, 512 - skip), 1) + (skip - 512)
        far = prior_col >= lo

        def head(h, carry):
            lanes = pl.ds(pl.multiple_of(h * 128, 128), 128)
            q = q_ref[first : first + 256, lanes]
            s1 = lax.dot_general(q, kv_ref[0, :count], nt, preferred_element_type=F32)
            s0 = lax.dot_general(q, prior_ref[0, skip:], nt, preferred_element_type=F32)
            s1 = jnp.where(near, s1, -1e30)
            s0 = jnp.where(far, s0, -1e30)
            top = jnp.maximum(jnp.max(s1, -1, keepdims=True), jnp.max(s0, -1, keepdims=True))
            e1 = jnp.exp2((s1 - top) * factor)
            e0 = jnp.exp2((s0 - top) * factor)
            inv = 1.0 / (jnp.sum(e1, -1, keepdims=True) + jnp.sum(e0, -1, keepdims=True))
            p1 = (e1 * inv).astype(BF)
            p0 = (e0 * inv).astype(BF)
            o = jnp.dot(p1, kv_ref[1, :count], preferred_element_type=F32)
            o = o + jnp.dot(p0, prior_ref[1, skip:], preferred_element_type=F32)
            o = o.astype(BF)
            for part in range(2):
                out_ref[(2 * i + part) % 4, :, lanes] = o[part * 128 : part * 128 + 128]
            return carry

        lax.fori_loop(0, 2, head, 0)

    @pl.when(half_ref[0] == 0)
    def _():
        block(0)
        block(1)

    @pl.when(half_ref[0] == 1)
    def _():
        block(2)
        block(3)


def attend(half, q, kv, prior, lo):
    vm = pl.BlockSpec(memory_space=pltpu.VMEM)
    return pl.pallas_call(
        attend_kernel,
        in_specs=[pl.BlockSpec(memory_space=pltpu.SMEM)] + [vm] * 4,
        out_shape=jax.ShapeDtypeStruct((4, 128, 256), BF),
        compiler_params=pltpu.CompilerParams(vmem_limit_bytes=20 << 20),
        name="attend",
    )(half, q, kv, prior, lo)


def lay_kernel(core_ref, own_ref, oth_ref, w_ref, sems):
    core = core_ref[0]

    def each(act):
        def step(n, carry):
            s, i = n // 8, lax.rem(n, 8)
            for which, (src, side) in enumerate(((own_ref, core), (oth_ref, 1 - core))):
                at = pl.ds(pl.multiple_of((2 * i + side) * 128, 128), 128)
                act(pltpu.make_async_copy(
                    src.at[s, i], w_ref.at[pl.ds(pl.multiple_of(s * 256, 256), 256), at], sems.at[which, s, i]
                ))
            return carry

        lax.fori_loop(0, 32, step, 0)

    each(lambda c: c.start())
    each(lambda c: c.wait())


def lay(core, own, oth):
    anywhere = pl.BlockSpec(memory_space=pl.ANY)
    return pl.pallas_call(
        lay_kernel,
        in_specs=[pl.BlockSpec(memory_space=pltpu.SMEM), anywhere, anywhere],
        out_shape=jax.ShapeDtypeStruct((1024, 2048), BF),
        scratch_shapes=[pltpu.SemaphoreType.DMA((2, 4, 8))],
        compiler_params=pltpu.CompilerParams(vmem_limit_bytes=6 << 20),
        name="lay",
    )(core, own, oth)


def out_kernel(ctx_ref, w_ref, out_ref):
    x = jnp.concatenate([ctx_ref[s] for s in range(4)], axis=1)

    def column(n, carry):
        at = pl.ds(pl.multiple_of(n * 512, 512), 512)
        out_ref[:, at] = jnp.dot(x, w_ref[:, at], preferred_element_type=F32).astype(out_ref.dtype)
        return carry

    lax.fori_loop(0, 4, column, 0)


def out_project(ctx, weight, dtype):
    return pl.pallas_call(
        out_kernel,
        out_shape=jax.ShapeDtypeStruct((128, 2048), dtype),
        compiler_params=pltpu.CompilerParams(vmem_limit_bytes=10 << 20),
        name="oproj",
    )(ctx, weight)


def fetcher(own_ref, oth_ref, w_ref, sems, y, first):
    def copy(c, g, m):
        src = own_ref if c == 0 else oth_ref
        at = pl.multiple_of(((m // 4) * 4 + lax.rem(y + lax.rem(m, 4), 4)) * 256, 256)
        return pltpu.make_async_copy(
            src.at[:, m // 4, lax.rem(m, 4), first + g * 96 : first + g * 96 + 96, :],
            w_ref.at[g, c * 8 : c * 8 + 8, :, pl.ds(at, 256)],
            sems.at[g, c, m],
        )

    def each(c, groups, act):
        def step(m, carry):
            for g in range(groups):
                act(copy(c, g, m))
            return carry

        lax.fori_loop(0, 8, step, 0)

    return each


def gate_kernel(y_ref, x0_ref, x1_ref, x2_ref, x3_ref, x4_ref, src_ref, hid_ref, w_ref, x_ref, sems):
    nt = (((1,), (1,)), ((), ()))
    each = fetcher(src_ref, src_ref, w_ref, sems, y_ref[0], 0)
    each(0, 2, lambda c: c.start())
    x_ref[0:128] = x0_ref[...]
    x_ref[128:256] = x1_ref[...]
    x_ref[256:384] = x2_ref[...]
    x_ref[384:448] = x3_ref[...]
    x_ref[448:512] = x4_ref[...]
    x = x_ref[...]
    each(0, 2, lambda copy: copy.wait())
    gate_w = w_ref[0].reshape(768, 2048)
    up_w = w_ref[1].reshape(768, 2048)
    for t in range(3):
        gate = lax.dot_general(x, gate_w[t * 256 : t * 256 + 256], nt, preferred_element_type=F32)
        upper = lax.dot_general(x, up_w[t * 256 : t * 256 + 256], nt, preferred_element_type=F32)
        hidden = gate / (1.0 + jnp.exp(-gate)) * upper
        hid_ref[:, t * 256 : t * 256 + 256] = hidden.astype(BF)


def far_kernel(y_ref, hid0_ref, hid1_ref, own_ref, oth_ref, top_ref, bottom_ref, w_ref, sems):
    each = fetcher(own_ref, oth_ref, w_ref, sems, y_ref[0], 192)
    for c in range(2):
        each(c, 1, lambda copy: copy.start())
    for c in range(2):
        each(c, 1, lambda copy: copy.wait())
    hid = jnp.concatenate([hid0_ref[384:], hid1_ref[384:]], axis=1)

    def column(n, carry):
        at = pl.ds(pl.multiple_of(n * 512, 512), 512)
        out = jnp.dot(hid, w_ref[0, :, :, at].reshape(1536, 512), preferred_element_type=F32)
        top_ref[:, at] = out[:64].astype(BF)
        bottom_ref[:, at] = out[64:].astype(BF)
        return carry

    lax.fori_loop(0, 4, column, 0)


def down_kernel(hid0_ref, hid1_ref, w_ref, keep_ref, left_ref, right_ref):
    hid = jnp.concatenate([hid0_ref[:384], hid1_ref[:384]], axis=1)

    def column(n, carry):
        at = pl.ds(pl.multiple_of(n * 512, 512), 512)
        out = jnp.dot(hid, w_ref[0, :, :, at].reshape(1536, 512), preferred_element_type=F32)
        keep_ref[:, at] = out[:128]
        left_ref[:, at] = out[128:256].astype(BF)
        right_ref[:, at] = out[256:].astype(BF)
        return carry

    lax.fori_loop(0, 4, column, 0)


def gate_up(y, pieces, src):
    vm = pl.BlockSpec(memory_space=pltpu.VMEM)
    hbm = pl.BlockSpec(memory_space=pltpu.HBM)
    return pl.pallas_call(
        gate_kernel,
        in_specs=[pl.BlockSpec(memory_space=pltpu.SMEM)] + [vm] * 5 + [hbm],
        out_shape=jax.ShapeDtypeStruct((512, 768), BF),
        scratch_shapes=[
            pltpu.VMEM((2, 8, 96, 2048), BF),
            pltpu.VMEM((512, 2048), BF),
            pltpu.SemaphoreType.DMA((2, 1, 8)),
        ],
        compiler_params=pltpu.CompilerParams(vmem_limit_bytes=18 << 20),
        name="gate_up",
    )(y, *pieces, src)


def down_far(y, hidden, own, oth):
    vm = pl.BlockSpec(memory_space=pltpu.VMEM)
    hbm = pl.BlockSpec(memory_space=pltpu.HBM)
    half = jax.ShapeDtypeStruct((64, 2048), BF)
    return pl.pallas_call(
        far_kernel,
        in_specs=[pl.BlockSpec(memory_space=pltpu.SMEM), vm, vm] + [hbm] * 2,
        out_shape=(half, half, jax.ShapeDtypeStruct((1, 16, 96, 2048), BF)),
        scratch_shapes=[pltpu.SemaphoreType.DMA((1, 2, 8))],
        compiler_params=pltpu.CompilerParams(vmem_limit_bytes=14 << 20),
        name="down_far",
    )(y, *hidden, own, oth)


def down(hidden, weight):
    part = jax.ShapeDtypeStruct((128, 2048), BF)
    return pl.pallas_call(
        down_kernel,
        out_shape=(jax.ShapeDtypeStruct((128, 2048), F32), part, part),
        compiler_params=pltpu.CompilerParams(vmem_limit_bytes=14 << 20),
        name="down",
    )(*hidden, weight)


def pack_kernel(q_ref, k_ref, v_ref, o_ref, out_ref):
    parts = [q_ref[:, :128], q_ref[:, 128:], k_ref[...], v_ref[...], o_ref[...]]
    whole = jnp.concatenate(parts, axis=0).astype(BF)
    for i in range(8):
        out_ref[i] = whole


def pack(q, k, v, o):
    return pl.pallas_call(
        pack_kernel,
        out_shape=jax.ShapeDtypeStruct((8, 768, 128), BF),
        name="pack",
    )(q, k, v, o)


def prep_kernel(y_ref, gate_ref, up_ref, down_ref, p0_ref, p1_ref, p2_ref, p3_ref, g_ref, u_ref):
    g_ref[...] = gate_ref[...].T
    u_ref[...] = up_ref[...].T
    for k, out_ref in enumerate((p0_ref, p1_ref, p2_ref, p3_ref)):
        at = pl.ds(pl.multiple_of(lax.rem(y_ref[0] + k, 4) * 96, 96), 96)
        out_ref[:96] = g_ref[at, :].astype(BF)
        out_ref[96:192] = u_ref[at, :].astype(BF)
        out_ref[192:] = down_ref[at, :].astype(BF)


def prepare(y, gate, up, down):
    vm = pl.BlockSpec(memory_space=pltpu.VMEM)
    return pl.pallas_call(
        prep_kernel,
        in_specs=[pl.BlockSpec(memory_space=pltpu.SMEM)] + [vm] * 3,
        out_shape=[jax.ShapeDtypeStruct((288, 256), BF)] * 4,
        scratch_shapes=[pltpu.VMEM((384, 256), F32), pltpu.VMEM((384, 256), F32)],
        name="prep",
    )(y, gate, up, down)


def join_kernel(p0_ref, p1_ref, p2_ref, p3_ref, out_ref):
    for k, ref in enumerate((p0_ref, p1_ref, p2_ref, p3_ref)):
        out_ref[k] = ref[...]


def join(parts):
    return pl.pallas_call(join_kernel, out_shape=jax.ShapeDtypeStruct((4, 288, 256), BF), name="join")(*parts)


def trade(parts):
    return [parts[0]] + [lax.ppermute(parts[4 - k], "y", ring(4 - k)) for k in (1, 2, 3)]


def per_device(
    tokens,
    doc_ids,
    positions,
    attn_gain,
    mlp_gain,
    q_gain,
    key_norm_gain,
    q_weight,
    key_matrix,
    value_matrix,
    o_weight,
    gate_weight,
    up_weight,
    down_weight,
):
    rows = tokens.shape[0]
    core = lax.axis_index("core").astype(jnp.int32)
    xl = lax.axis_index("xl").astype(jnp.int32)
    y = lax.axis_index("y").astype(jnp.int32)
    hold = lax.optimization_barrier

    packed = pack(q_weight, key_matrix, value_matrix, o_weight)
    at_own = lax.all_to_all(packed, ("z", "xh"), split_axis=0, concat_axis=0, tiled=True)

    parts = trade(prepare(y[None], gate_weight, up_weight, down_weight))
    half = HEAD // 2
    freq = jnp.exp(jnp.arange(half, dtype=F32) * (-2.0 * math.log(1000000.0) / HEAD))
    angle = positions.astype(F32)[:, None] * freq[None, :]
    cs = jnp.concatenate([jnp.cos(angle), jnp.sin(angle)], axis=1)
    group = join(parts)
    cs, at_own, group = hold((cs, at_own, group))
    mlp_own = lax.all_gather(group, ("z", "xh", "xl"), axis=0, tiled=False).reshape(8, 2, 4, 288, 256)
    lo = (jnp.arange(rows, dtype=jnp.int32) - positions)[:, None]

    at_oth = swap(at_own, "core")

    o_own = lax.all_to_all(widen(at_own), "y", split_axis=0, concat_axis=0, tiled=True)

    rows_in = pltpu.with_memory_space_constraint(tokens, pltpu.HBM)
    q, cache, tail = project(core[None], rows_in, at_own, at_oth, attn_gain, q_gain, key_norm_gain, cs)
    prior = lax.ppermute(tail, REQ, [(i - 1, i) for i in range(1, 16)])
    turn = lambda part: lax.all_to_all(part, "y", split_axis=0, concat_axis=0, tiled=True)
    theirs = attend(1 - xl[None], q, cache, prior, lo)
    _, q = hold((theirs, q))
    mine = attend(xl[None], q, cache, prior, lo)
    _, o_own = hold((mine, o_own))
    o_oth = swap(o_own, "core")
    o_whole = lay(core[None], o_own, o_oth)
    send = out_project(turn(theirs), o_whole, BF)
    got = swap(send, "xl")
    _, mine = hold((send, mine))
    keep = out_project(turn(mine), o_whole, F32)

    own_rows = lax.dynamic_slice_in_dim(tokens, (xl * 4 + y) * 128, 128, 0).astype(F32)
    resid = (own_rows + (keep + got.astype(F32))).astype(BF)
    resid = hold(resid).astype(F32)
    scale = lax.rsqrt(jnp.mean(resid * resid, axis=-1, keepdims=True) + 1e-06)
    mlp_in = (resid * scale * mlp_gain).astype(BF)

    left = lax.ppermute(mlp_in, "y", ring(1))
    right = lax.ppermute(mlp_in, "y", ring(3))
    mlp_own, left, right = hold((mlp_own, left, right))
    mlp_oth = swap(mlp_own, "core")
    far_top = lax.ppermute(left[:64], "y", ring(1))
    far_bottom = lax.ppermute(right[64:], "y", ring(3))
    pieces = (mlp_in, left, right, far_top, far_bottom)
    mlp_own = pltpu.with_memory_space_constraint(mlp_own, pltpu.HBM)
    first = gate_up(y[None], pieces, mlp_own)
    first, mlp_oth = hold((first, mlp_oth))
    hidden = (first, gate_up(y[None], pieces, mlp_oth))
    top, bottom, weight = down_far(y[None], hidden, mlp_own, mlp_oth)
    via_left = lax.ppermute(top, "y", ring(1))
    via_right = lax.ppermute(bottom, "y", ring(3))
    keep, to_left, to_right = down(hidden, weight)
    via_left, via_right = hold((via_left, via_right))
    to_right = jnp.concatenate([(to_right[:64].astype(F32) + via_left.astype(F32)).astype(BF), to_right[64:]])
    to_left = jnp.concatenate([to_left[:64], (to_left[64:].astype(F32) + via_right.astype(F32)).astype(BF)])
    from_left = lax.ppermute(to_right, "y", ring(1))
    from_right = lax.ppermute(to_left, "y", ring(3))
    total = keep + from_left.astype(F32) + from_right.astype(F32)
    return ((resid + total).astype(BF), cache)


def solution(mesh):
    fine = Mesh(mesh.devices.reshape(4, 2, 2, 2, 4), REQ + MDL)
    rows = P(REQ)
    in_specs = (
        P(REQ, None),
        rows,
        rows,
        P(),
        P(),
        P(),
        P(),
        P(REQ, MDL),
        P(REQ, MDL),
        P(REQ, MDL),
        P(MDL, REQ),
        P(MDL, REQ),
        P(MDL, REQ),
        P(REQ, MDL),
    )
    out_specs = (P(REQ + MDL, None), P(None, REQ, MDL))
    return jax.shard_map(per_device, mesh=fine, in_specs=in_specs, out_specs=out_specs, check_vma=False)
```

```python
import math

import jax
import jax.numpy as jnp
from jax import lax
from jax.experimental import pallas as pl
from jax.experimental.pallas import tpu as pltpu
from jax.sharding import Mesh
from jax.sharding import PartitionSpec as P

HEAD = 128
BF = jnp.bfloat16
F32 = jnp.float32
REQ = ("z", "xh", "core")
MDL = ("xl", "y")


def ring(step):
    return [(i, (i + step) % 4) for i in range(4)]


def swap(block, axis):
    return lax.ppermute(block, axis, [(0, 1), (1, 0)])


def qkv_kernel(core_ref, x_ref, own_ref, oth_ref, gain_ref, qg_ref, kg_ref, cs_ref, q_ref, kv_ref, tail_ref, w_ref):
    core = core_ref[0]

    @pl.when(pl.program_id(0) == 0)
    def _():
        def place(i, carry):
            for src, side in ((own_ref, core), (oth_ref, 1 - core)):
                at = pl.ds(pl.multiple_of((2 * i + side) * 128, 128), 128)
                for k in range(4):
                    w_ref[at, k * 128 : k * 128 + 128] = src[i, k * 128 : k * 128 + 128]
            return carry

        lax.fori_loop(0, 8, place, 0)

    x = x_ref[...].astype(F32)
    scale = lax.rsqrt(jnp.mean(x * x, axis=-1, keepdims=True) + 1e-06)
    normed = (x * scale * gain_ref[...]).astype(BF)
    raw = jnp.dot(normed, w_ref[...], preferred_element_type=F32)
    cs = cs_ref[...]
    turned = pltpu.roll(cs, 64, 1)
    low = lax.broadcasted_iota(jnp.int32, cs.shape, 1) < 64
    cosine = jnp.where(low, cs, turned)
    sine = jnp.where(low, -turned, cs)

    def head(t, gain):
        t = t * lax.rsqrt(jnp.mean(t * t, axis=-1, keepdims=True) + 1e-06) * gain
        return (t * cosine + pltpu.roll(t, 64, 1) * sine).astype(BF)

    q_ref[:, :128] = head(raw[:, :128], qg_ref[...])
    q_ref[:, 128:] = head(raw[:, 128:256], qg_ref[...])
    keys = head(raw[:, 256:384], kg_ref[...])
    values = raw[:, 384:].astype(BF)
    kv_ref[0] = keys
    kv_ref[1] = values

    @pl.when(pl.program_id(0) >= 2)
    def _():
        tail_ref[0] = keys
        tail_ref[1] = values


def project(core, tokens, own, oth, attn_gain, q_gain, key_gain, cs):
    rows = tokens.shape[0]
    tile = 256
    fixed = lambda *shape: pl.BlockSpec(shape, lambda i, c: (0,) * len(shape))
    return pl.pallas_call(
        qkv_kernel,
        grid_spec=pltpu.PrefetchScalarGridSpec(
            num_scalar_prefetch=1,
            grid=(rows // tile,),
            in_specs=[
                pl.BlockSpec((tile, 2048), lambda i, c: (i, 0)),
                fixed(8, 512, 128),
                fixed(8, 512, 128),
                fixed(1, 2048),
                fixed(1, 128),
                fixed(1, 128),
                pl.BlockSpec((tile, 128), lambda i, c: (i, 0)),
            ],
            out_specs=[
                pl.BlockSpec((tile, 256), lambda i, c: (i, 0)),
                pl.BlockSpec((2, tile, 128), lambda i, c: (0, i, 0)),
                pl.BlockSpec((2, tile, 128), lambda i, c: (0, jnp.maximum(i - 2, 0), 0)),
            ],
            scratch_shapes=[pltpu.VMEM((2048, 512), BF)],
        ),
        out_shape=(
            jax.ShapeDtypeStruct((rows, 256), BF),
            jax.ShapeDtypeStruct((2, rows, 128), BF),
            jax.ShapeDtypeStruct((2, rows // 2, 128), BF),
        ),
        compiler_params=pltpu.CompilerParams(vmem_limit_bytes=24 << 20),
        name="qkv",
    )(core, tokens, own, oth, attn_gain[None], q_gain[None], key_gain[None], cs)


def widen_kernel(src_ref, out_ref):
    for k in range(4):
        out_ref[k] = src_ref[...]


def widen(gathered):
    return pl.pallas_call(
        widen_kernel,
        grid=(1,),
        in_specs=[pl.BlockSpec((8, 256, 128), lambda i: (0, 2, 0))],
        out_specs=pl.BlockSpec((4, 8, 256, 128), lambda i: (0, 0, 0, 0)),
        out_shape=jax.ShapeDtypeStruct((4, 8, 256, 128), BF),
        name="widen",
    )(gathered)


def attend_kernel(half_ref, q_ref, kv_ref, prior_ref, lo_ref, out_ref):
    factor = HEAD ** (-0.5) * math.log2(math.e)
    nt = (((1,), (1,)), ((), ()))

    def block(i):
        first = i * 256
        skip = 256 if i == 3 else 0
        count = first + 256
        lo = lo_ref[first : first + 256, :]
        row = lax.broadcasted_iota(jnp.int32, (256, count), 0) + first
        col = lax.broadcasted_iota(jnp.int32, (256, count), 1)
        near = (col >= lo) & (col <= row)
        prior_col = lax.broadcasted_iota(jnp.int32, (256, 512 - skip), 1) + (skip - 512)
        far = prior_col >= lo

        def head(h, carry):
            lanes = pl.ds(pl.multiple_of(h * 128, 128), 128)
            q = q_ref[first : first + 256, lanes]
            s1 = lax.dot_general(q, kv_ref[0, :count], nt, preferred_element_type=F32)
            s0 = lax.dot_general(q, prior_ref[0, skip:], nt, preferred_element_type=F32)
            s1 = jnp.where(near, s1, -1e30)
            s0 = jnp.where(far, s0, -1e30)
            top = jnp.maximum(jnp.max(s1, -1, keepdims=True), jnp.max(s0, -1, keepdims=True))
            e1 = jnp.exp2((s1 - top) * factor)
            e0 = jnp.exp2((s0 - top) * factor)
            inv = 1.0 / (jnp.sum(e1, -1, keepdims=True) + jnp.sum(e0, -1, keepdims=True))
            p1 = (e1 * inv).astype(BF)
            p0 = (e0 * inv).astype(BF)
            o = jnp.dot(p1, kv_ref[1, :count], preferred_element_type=F32)
            o = o + jnp.dot(p0, prior_ref[1, skip:], preferred_element_type=F32)
            o = o.astype(BF)
            for part in range(2):
                out_ref[(2 * i + part) % 4, :, lanes] = o[part * 128 : part * 128 + 128]
            return carry

        lax.fori_loop(0, 2, head, 0)

    @pl.when(half_ref[0] == 0)
    def _():
        block(0)
        block(1)

    @pl.when(half_ref[0] == 1)
    def _():
        block(2)
        block(3)


def attend(half, q, kv, prior, lo):
    vm = pl.BlockSpec(memory_space=pltpu.VMEM)
    return pl.pallas_call(
        attend_kernel,
        in_specs=[pl.BlockSpec(memory_space=pltpu.SMEM)] + [vm] * 4,
        out_shape=jax.ShapeDtypeStruct((4, 128, 256), BF),
        compiler_params=pltpu.CompilerParams(vmem_limit_bytes=20 << 20),
        name="attend",
    )(half, q, kv, prior, lo)


def lay_kernel(core_ref, own_ref, oth_ref, w_ref, sems):
    core = core_ref[0]

    def each(act):
        def step(n, carry):
            s, i = n // 8, lax.rem(n, 8)
            for which, (src, side) in enumerate(((own_ref, core), (oth_ref, 1 - core))):
                at = pl.ds(pl.multiple_of((2 * i + side) * 128, 128), 128)
                act(pltpu.make_async_copy(
                    src.at[s, i], w_ref.at[pl.ds(pl.multiple_of(s * 256, 256), 256), at], sems.at[which, s, i]
                ))
            return carry

        lax.fori_loop(0, 32, step, 0)

    each(lambda c: c.start())
    each(lambda c: c.wait())


def lay(core, own, oth):
    anywhere = pl.BlockSpec(memory_space=pl.ANY)
    return pl.pallas_call(
        lay_kernel,
        in_specs=[pl.BlockSpec(memory_space=pltpu.SMEM), anywhere, anywhere],
        out_shape=jax.ShapeDtypeStruct((1024, 2048), BF),
        scratch_shapes=[pltpu.SemaphoreType.DMA((2, 4, 8))],
        compiler_params=pltpu.CompilerParams(vmem_limit_bytes=6 << 20),
        name="lay",
    )(core, own, oth)


def out_kernel(ctx_ref, w_ref, out_ref):
    x = jnp.concatenate([ctx_ref[s] for s in range(4)], axis=1)
    out_ref[...] = jnp.dot(x, w_ref[...], preferred_element_type=F32).astype(out_ref.dtype)


def out_project(ctx, weight, dtype):
    return pl.pallas_call(
        out_kernel,
        grid=(4,),
        in_specs=[pl.BlockSpec((4, 128, 256), lambda n: (0, 0, 0)), pl.BlockSpec((1024, 512), lambda n: (0, n))],
        out_specs=pl.BlockSpec((128, 512), lambda n: (0, n)),
        out_shape=jax.ShapeDtypeStruct((128, 2048), dtype),
        compiler_params=pltpu.CompilerParams(vmem_limit_bytes=14 << 20),
        name="oproj",
    )(ctx, weight)


def fetcher(own_ref, oth_ref, w_ref, sems, y, first):
    def copy(c, g, m):
        src = own_ref if c == 0 else oth_ref
        at = pl.multiple_of(((m // 4) * 4 + lax.rem(y + lax.rem(m, 4), 4)) * 256, 256)
        return pltpu.make_async_copy(
            src.at[:, m // 4, lax.rem(m, 4), first + g * 96 : first + g * 96 + 96, :],
            w_ref.at[g, c * 8 : c * 8 + 8, :, pl.ds(at, 256)],
            sems.at[g, c, m],
        )

    def each(c, groups, act):
        def step(m, carry):
            for g in range(groups):
                act(copy(c, g, m))
            return carry

        lax.fori_loop(0, 8, step, 0)

    return each


def gate_kernel(y_ref, x0_ref, x1_ref, x2_ref, x3_ref, x4_ref, src_ref, hid_ref, w_ref, x_ref, sems):
    nt = (((1,), (1,)), ((), ()))
    each = fetcher(src_ref, src_ref, w_ref, sems, y_ref[0], 0)
    each(0, 2, lambda c: c.start())
    x_ref[0:128] = x0_ref[...]
    x_ref[128:256] = x1_ref[...]
    x_ref[256:384] = x2_ref[...]
    x_ref[384:448] = x3_ref[...]
    x_ref[448:512] = x4_ref[...]
    x = x_ref[...]
    each(0, 2, lambda copy: copy.wait())
    gate_w = w_ref[0].reshape(768, 2048)
    up_w = w_ref[1].reshape(768, 2048)
    for t in range(3):
        gate = lax.dot_general(x, gate_w[t * 256 : t * 256 + 256], nt, preferred_element_type=F32)
        upper = lax.dot_general(x, up_w[t * 256 : t * 256 + 256], nt, preferred_element_type=F32)
        hidden = gate / (1.0 + jnp.exp(-gate)) * upper
        hid_ref[:, t * 256 : t * 256 + 256] = hidden.astype(BF)


def far_kernel(y_ref, hid0_ref, hid1_ref, own_ref, oth_ref, top_ref, bottom_ref, w_ref, sems):
    each = fetcher(own_ref, oth_ref, w_ref, sems, y_ref[0], 192)
    for c in range(2):
        each(c, 1, lambda copy: copy.start())
    for c in range(2):
        each(c, 1, lambda copy: copy.wait())
    hid = jnp.concatenate([hid0_ref[384:], hid1_ref[384:]], axis=1)

    def column(n, carry):
        at = pl.ds(pl.multiple_of(n * 512, 512), 512)
        out = jnp.dot(hid, w_ref[0, :, :, at].reshape(1536, 512), preferred_element_type=F32)
        top_ref[:, at] = out[:64].astype(BF)
        bottom_ref[:, at] = out[64:].astype(BF)
        return carry

    lax.fori_loop(0, 4, column, 0)


def down_kernel(hid0_ref, hid1_ref, w_ref, keep_ref, left_ref, right_ref):
    hid = jnp.concatenate([hid0_ref[:384], hid1_ref[:384]], axis=1)

    def column(n, carry):
        at = pl.ds(pl.multiple_of(n * 512, 512), 512)
        out = jnp.dot(hid, w_ref[0, :, :, at].reshape(1536, 512), preferred_element_type=F32)
        keep_ref[:, at] = out[:128]
        left_ref[:, at] = out[128:256].astype(BF)
        right_ref[:, at] = out[256:].astype(BF)
        return carry

    lax.fori_loop(0, 4, column, 0)


def gate_up(y, pieces, src):
    vm = pl.BlockSpec(memory_space=pltpu.VMEM)
    hbm = pl.BlockSpec(memory_space=pltpu.HBM)
    return pl.pallas_call(
        gate_kernel,
        in_specs=[pl.BlockSpec(memory_space=pltpu.SMEM)] + [vm] * 5 + [hbm],
        out_shape=jax.ShapeDtypeStruct((512, 768), BF),
        scratch_shapes=[
            pltpu.VMEM((2, 8, 96, 2048), BF),
            pltpu.VMEM((512, 2048), BF),
            pltpu.SemaphoreType.DMA((2, 1, 8)),
        ],
        compiler_params=pltpu.CompilerParams(vmem_limit_bytes=18 << 20),
        name="gate_up",
    )(y, *pieces, src)


def down_far(y, hidden, own, oth):
    vm = pl.BlockSpec(memory_space=pltpu.VMEM)
    hbm = pl.BlockSpec(memory_space=pltpu.HBM)
    half = jax.ShapeDtypeStruct((64, 2048), BF)
    return pl.pallas_call(
        far_kernel,
        in_specs=[pl.BlockSpec(memory_space=pltpu.SMEM), vm, vm] + [hbm] * 2,
        out_shape=(half, half, jax.ShapeDtypeStruct((1, 16, 96, 2048), BF)),
        scratch_shapes=[pltpu.SemaphoreType.DMA((1, 2, 8))],
        compiler_params=pltpu.CompilerParams(vmem_limit_bytes=14 << 20),
        name="down_far",
    )(y, *hidden, own, oth)


def down(hidden, weight):
    part = jax.ShapeDtypeStruct((128, 2048), BF)
    return pl.pallas_call(
        down_kernel,
        out_shape=(jax.ShapeDtypeStruct((128, 2048), F32), part, part),
        compiler_params=pltpu.CompilerParams(vmem_limit_bytes=14 << 20),
        name="down",
    )(*hidden, weight)


def pack_kernel(q_ref, k_ref, v_ref, o_ref, out_ref):
    parts = [q_ref[:, :128], q_ref[:, 128:], k_ref[...], v_ref[...], o_ref[...]]
    whole = jnp.concatenate(parts, axis=0).astype(BF)
    for i in range(8):
        out_ref[i] = whole


def pack(q, k, v, o):
    return pl.pallas_call(
        pack_kernel,
        out_shape=jax.ShapeDtypeStruct((8, 768, 128), BF),
        name="pack",
    )(q, k, v, o)


def prep_kernel(y_ref, gate_ref, up_ref, down_ref, p0_ref, p1_ref, p2_ref, p3_ref, g_ref, u_ref):
    g_ref[...] = gate_ref[...].T
    u_ref[...] = up_ref[...].T
    for k, out_ref in enumerate((p0_ref, p1_ref, p2_ref, p3_ref)):
        at = pl.ds(pl.multiple_of(lax.rem(y_ref[0] + k, 4) * 96, 96), 96)
        out_ref[:96] = g_ref[at, :].astype(BF)
        out_ref[96:192] = u_ref[at, :].astype(BF)
        out_ref[192:] = down_ref[at, :].astype(BF)


def prepare(y, gate, up, down):
    vm = pl.BlockSpec(memory_space=pltpu.VMEM)
    return pl.pallas_call(
        prep_kernel,
        in_specs=[pl.BlockSpec(memory_space=pltpu.SMEM)] + [vm] * 3,
        out_shape=[jax.ShapeDtypeStruct((288, 256), BF)] * 4,
        scratch_shapes=[pltpu.VMEM((384, 256), F32), pltpu.VMEM((384, 256), F32)],
        name="prep",
    )(y, gate, up, down)


def join_kernel(p0_ref, p1_ref, p2_ref, p3_ref, out_ref):
    for k, ref in enumerate((p0_ref, p1_ref, p2_ref, p3_ref)):
        out_ref[k] = ref[...]


def join(parts):
    return pl.pallas_call(join_kernel, out_shape=jax.ShapeDtypeStruct((4, 288, 256), BF), name="join")(*parts)


def trade(parts):
    return [parts[0]] + [lax.ppermute(parts[4 - k], "y", ring(4 - k)) for k in (1, 2, 3)]


def per_device(
    tokens,
    doc_ids,
    positions,
    attn_gain,
    mlp_gain,
    q_gain,
    key_norm_gain,
    q_weight,
    key_matrix,
    value_matrix,
    o_weight,
    gate_weight,
    up_weight,
    down_weight,
):
    rows = tokens.shape[0]
    core = lax.axis_index("core").astype(jnp.int32)
    xl = lax.axis_index("xl").astype(jnp.int32)
    y = lax.axis_index("y").astype(jnp.int32)
    hold = lax.optimization_barrier

    packed = pack(q_weight, key_matrix, value_matrix, o_weight)
    at_own = lax.all_to_all(packed, ("z", "xh"), split_axis=0, concat_axis=0, tiled=True)

    parts = trade(prepare(y[None], gate_weight, up_weight, down_weight))
    half = HEAD // 2
    freq = jnp.exp(jnp.arange(half, dtype=F32) * (-2.0 * math.log(1000000.0) / HEAD))
    angle = positions.astype(F32)[:, None] * freq[None, :]
    cs = jnp.concatenate([jnp.cos(angle), jnp.sin(angle)], axis=1)
    group = join(parts)
    cs, at_own, group = hold((cs, at_own, group))
    mlp_own = lax.all_gather(group, ("z", "xh", "xl"), axis=0, tiled=False).reshape(8, 2, 4, 288, 256)
    lo = (jnp.arange(rows, dtype=jnp.int32) - positions)[:, None]

    at_oth = swap(at_own, "core")

    o_own = lax.all_to_all(widen(at_own), "y", split_axis=0, concat_axis=0, tiled=True)

    rows_in = pltpu.with_memory_space_constraint(tokens, pltpu.HBM)
    q, cache, tail = project(core[None], rows_in, at_own, at_oth, attn_gain, q_gain, key_norm_gain, cs)
    prior = lax.ppermute(tail, REQ, [(i - 1, i) for i in range(1, 16)])
    turn = lambda part: lax.all_to_all(part, "y", split_axis=0, concat_axis=0, tiled=True)
    theirs = attend(1 - xl[None], q, cache, prior, lo)
    _, q = hold((theirs, q))
    mine = attend(xl[None], q, cache, prior, lo)
    _, o_own = hold((mine, o_own))
    o_oth = swap(o_own, "core")
    o_whole = pltpu.with_memory_space_constraint(lay(core[None], o_own, o_oth), pltpu.HBM)
    send = out_project(turn(theirs), o_whole, BF)
    got = swap(send, "xl")
    _, mine = hold((send, mine))
    keep = out_project(turn(mine), o_whole, F32)

    own_rows = lax.dynamic_slice_in_dim(tokens, (xl * 4 + y) * 128, 128, 0).astype(F32)
    resid = (own_rows + (keep + got.astype(F32))).astype(BF)
    resid = hold(resid).astype(F32)
    scale = lax.rsqrt(jnp.mean(resid * resid, axis=-1, keepdims=True) + 1e-06)
    mlp_in = (resid * scale * mlp_gain).astype(BF)

    left = lax.ppermute(mlp_in, "y", ring(1))
    right = lax.ppermute(mlp_in, "y", ring(3))
    mlp_own, left, right = hold((mlp_own, left, right))
    mlp_oth = swap(mlp_own, "core")
    far_top = lax.ppermute(left[:64], "y", ring(1))
    far_bottom = lax.ppermute(right[64:], "y", ring(3))
    pieces = (mlp_in, left, right, far_top, far_bottom)
    mlp_own = pltpu.with_memory_space_constraint(mlp_own, pltpu.HBM)
    first = gate_up(y[None], pieces, mlp_own)
    first, mlp_oth = hold((first, mlp_oth))
    hidden = (first, gate_up(y[None], pieces, mlp_oth))
    top, bottom, weight = down_far(y[None], hidden, mlp_own, mlp_oth)
    via_left = lax.ppermute(top, "y", ring(1))
    via_right = lax.ppermute(bottom, "y", ring(3))
    keep, to_left, to_right = down(hidden, weight)
    via_left, via_right = hold((via_left, via_right))
    to_right = jnp.concatenate([(to_right[:64].astype(F32) + via_left.astype(F32)).astype(BF), to_right[64:]])
    to_left = jnp.concatenate([to_left[:64], (to_left[64:].astype(F32) + via_right.astype(F32)).astype(BF)])
    from_left = lax.ppermute(to_right, "y", ring(1))
    from_right = lax.ppermute(to_left, "y", ring(3))
    total = keep + from_left.astype(F32) + from_right.astype(F32)
    return ((resid + total).astype(BF), cache)


def solution(mesh):
    fine = Mesh(mesh.devices.reshape(4, 2, 2, 2, 4), REQ + MDL)
    rows = P(REQ)
    in_specs = (
        P(REQ, None),
        rows,
        rows,
        P(),
        P(),
        P(),
        P(),
        P(REQ, MDL),
        P(REQ, MDL),
        P(REQ, MDL),
        P(MDL, REQ),
        P(MDL, REQ),
        P(MDL, REQ),
        P(REQ, MDL),
    )
    out_specs = (P(REQ + MDL, None), P(None, REQ, MDL))
    return jax.shard_map(per_device, mesh=fine, in_specs=in_specs, out_specs=out_specs, check_vma=False)
```
